32 devices in a mesh: gx: 8 (over y, x, core), gy: 4 (over z).
Axes of the slice: x: 2, y: 2, z: 4, core: 2. Of those that a mesh axis runs over, the one named last changes fastest.
Arguments:
- particle_count: int32 [8, 256, 1024], P(None, ('gx', 'gy')), may hold values from 0 to 12
- drag_coeff: float32 [8, 256, 1024], P(None, ('gx', 'gy')), may hold values from 0.05 to 2
- particle_velocity: float32 [3, 8, 256, 1024], P(None, None, ('gx', 'gy')), may hold values from -6 to 6
- fluid_velocity: float32 [3, 8, 256, 1024], P(None, None, 'gy', 'gx'), may hold values from -6 to 6
Outputs:
- pressure: float32 [8, 256, 1024], P(None, 'gy', 'gx')
- new_velocity: float32 [3, 8, 256, 1024], P(None, None, ('gx', 'gy'))
- pressure_gradient: float32 [3, 8, 256, 1024], P(None, None, ('gx', 'gy'))
The draws below stay inside these ranges and needn't reach their ends.
All inputs are finite; a program needn't handle non-finite values.
Results may differ from the reference program's by a relative error of at most 0.00002.
Values sent between devices are 32-bit elements; how exact they have to be, the bound alone decides.
A program may use at most 64 MiB of HBM per device.

```python
import math
import jax
import jax.numpy as jnp

NZ = 8
SWEEPS = 8
NX = 256
NY = 1024


def place_ends(result, rng, least, top_value):
    extent = result.shape
    spot = [jax.random.randint(jax.random.fold_in(rng, axis), (), 0, extent[axis]) for axis in range(len(extent))]
    result = result.at[tuple(spot)].set(least)
    longest = extent.index(max(extent))
    spot[longest] = (spot[longest] + 1) % extent[longest]
    return result.at[tuple(spot)].set(top_value)


def levels(own_key, dims, shards, low, high):
    def one(axis_at, blocks):
        steps = jax.random.uniform(jax.random.fold_in(jax.random.fold_in(own_key, 6), axis_at), (blocks,), jnp.float32, low / len(shards), high / len(shards))
        return jnp.repeat(jnp.exp(steps), dims[axis_at] // blocks).reshape((-1,) + (1,) * (len(dims) - axis_at - 1))

    gain = one(*shards[0])
    for cut in shards[1:]:
        gain = gain * one(*cut)
    return gain


def gaussian(key, dims, width, reach, split=(), held_as=jnp.bfloat16):
    level = levels(key, dims, split, -0.22, 0.18) if split else 1.0
    entries = jax.random.normal(key, dims, jnp.float32) * width * level
    return jnp.minimum(jnp.maximum(entries, -reach), reach).astype(held_as)


def setup_inputs(seed: int = 0) -> dict:
    arg_keys = jax.random.split(jax.random.key(seed), 5)
    particle_count = place_ends(jax.random.randint(arg_keys[0], (NZ, NX, NY), 0, 13), jax.random.fold_in(arg_keys[0], 1), 0, 12).astype(jnp.int32)
    drag_coeff = jnp.clip(jnp.exp(math.log(2.0) - 3.6888794 * jax.random.uniform(arg_keys[1], (NZ, NX, NY), jnp.float32) ** levels(arg_keys[1], (NZ, NX, NY), ((1, 32),), -0.2, 0.2)), 0.05, 2.0)
    particle_velocity = gaussian(arg_keys[2], (3, NZ, NX, NY), 1.0, 6.0, ((2, 32),), jnp.float32)
    fluid_velocity = gaussian(arg_keys[3], (3, NZ, NX, NY), 1.0, 6.0, ((2, 4), (3, 8)), jnp.float32)
    return {"particle_count": particle_count, "drag_coeff": drag_coeff, "particle_velocity": particle_velocity, "fluid_velocity": fluid_velocity}


particle_volume = 0.05
time_step = 0.5
viscosity = 0.1


def pad_depth(values):
    widths = [(0, 0)] * (values.ndim - 3) + [(1, 1), (0, 0), (0, 0)]
    return jnp.pad(values, widths)


def pad_plane(values):
    widths = [(0, 0)] * (values.ndim - 2) + [(1, 1), (1, 1)]
    return jnp.pad(values, widths)


def middle(values):
    return values[..., 1:-1, 1:-1, 1:-1]


def neighbour(values, which):
    if which == 0:
        return values[..., 2:, 1:-1, 1:-1]
    if which == 1:
        return values[..., :-2, 1:-1, 1:-1]
    if which == 2:
        return values[..., 1:-1, 2:, 1:-1]
    if which == 3:
        return values[..., 1:-1, :-2, 1:-1]
    if which == 4:
        return values[..., 1:-1, 1:-1, 2:]
    return values[..., 1:-1, 1:-1, :-2]


def face_weights(voids_wide):
    padded = pad_depth(voids_wide)
    centre = middle(padded)
    weights = jnp.stack([0.5 * (centre + neighbour(padded, which)) for which in range(6)])
    weight_sum = weights[0]
    for which in range(1, 6):
        weight_sum = weight_sum + weights[which]
    return weights, weight_sum


def momentum(velocity_wide, weights, voids, drag, drag_force):
    padded = pad_depth(velocity_wide)
    centre = middle(padded)
    diffusion = jnp.zeros_like(centre)
    for which in range(6):
        diffusion = diffusion + weights[which][None] * (neighbour(padded, which) - centre)
    return (voids[None] * centre + time_step * viscosity * diffusion + time_step * drag_force) / (voids[None] + time_step * drag[None])


def divergence(flux_wide):
    first = flux_wide[0][:, 2:, 1:-1] - flux_wide[0][:, :-2, 1:-1]
    second = flux_wide[1][:, 1:-1, 2:] - flux_wide[1][:, 1:-1, :-2]
    normal = pad_depth(flux_wide[2])[:, 1:-1, 1:-1]
    third = normal[2:] - normal[:-2]
    return 0.5 * (first + second + third) / time_step


def jacobi_sweep(pressure_wide, weights, weight_sum, source):
    padded = pad_depth(pressure_wide)
    total = weights[0] * neighbour(padded, 0)
    for which in range(1, 6):
        total = total + weights[which] * neighbour(padded, which)
    return (total - source) / weight_sum


def gradient_of(pressure_wide):
    padded = pad_depth(pressure_wide)
    first = 0.5 * (padded[1:-1, 2:, 1:-1] - padded[1:-1, :-2, 1:-1])
    second = 0.5 * (padded[1:-1, 1:-1, 2:] - padded[1:-1, 1:-1, :-2])
    third = 0.5 * (padded[2:, 1:-1, 1:-1] - padded[:-2, 1:-1, 1:-1])
    return jnp.stack([first, second, third])


def reference(particle_count, drag_coeff, particle_velocity, fluid_velocity):
    voids = 1.0 - particle_count.astype(jnp.float32) * particle_volume
    drag_force = drag_coeff[None] * particle_velocity
    weights, weight_sum = face_weights(pad_plane(voids))
    predicted = momentum(pad_plane(fluid_velocity), weights, voids, drag_coeff, drag_force)
    flux = voids[None] * predicted
    source = divergence(pad_plane(flux))
    pressure = (-source) / weight_sum
    for sweep_index in range(SWEEPS - 1):
        pressure = jacobi_sweep(pad_plane(pressure), weights, weight_sum, source)
    slopes = gradient_of(pad_plane(pressure))
    velocity = predicted - time_step * slopes
    return pressure, velocity, slopes
```

```python
import functools

import jax
import jax.numpy as jnp
from jax import lax
from jax.experimental import pallas as pl
from jax.experimental.pallas import tpu as pltpu
from jax.sharding import PartitionSpec as P

SWEEPS = 8
ROUNDS = (4, 4)

particle_volume = 0.05
time_step = 0.5
viscosity = 0.1


def kernel(
    K, G, R, NZ, NY, W,
    count_in, drag_in, pvel_in, fluid_in,
    press_out, vel_out, grad_out,
    fp, ub, cn, dr, pv, vo, total_w, wf, wr, wa, rh, pred, gr, fl, fr, t0, t1, pf, rl, po,
    loc_sem, fh_send, fh_recv, s2_send, s2_recv,
    hal_send, hal_recv, pr_send, pr_recv, out_send, out_recv, up_send, up_recv, *stages,
):
    H = max(ROUNDS)
    b = stages[0]
    C = G // K
    B = C * K
    x = lax.axis_index("gx")
    k = lax.axis_index("gy")
    place = x * K + k
    has_prev = place > 0
    has_next = place < G * K - 1
    prev_id = {"gx": jnp.where(k > 0, x, jnp.maximum(x - 1, 0)), "gy": lax.rem(k + K - 1, K)}
    next_id = {"gx": jnp.where(k < K - 1, x, jnp.minimum(x + 1, G - 1)), "gy": lax.rem(k + 1, K)}

    def remote(src, dst, ssem, rsem, to):
        return pltpu.make_async_remote_copy(
            src_ref=src, dst_ref=dst, send_sem=ssem, recv_sem=rsem, device_id=to, device_id_type=pl.DeviceIdType.MESH
        )

    rows = R * B

    local = [[] for _ in range(4)]
    for z in range(NZ):
        local[0].append(pltpu.make_async_copy(fluid_in.at[:, z], fp.at[:, 1:rows + 1, z], loc_sem.at[z]))
        local[1].append(pltpu.make_async_copy(count_in.at[z], cn.at[H:H + R, z], loc_sem.at[NZ + z]))
        local[2].append(pltpu.make_async_copy(drag_in.at[z], dr.at[:, z], loc_sem.at[2 * NZ + z]))
        local[3].append(pltpu.make_async_copy(pvel_in.at[:, z], pv.at[:, :, z], loc_sem.at[3 * NZ + z]))
    for copies in local:
        for copy in copies:
            copy.start()

    home = x // C
    barrier = pltpu.get_barrier_semaphore()

    def greet(to):
        pl.semaphore_signal(barrier, inc=1, device_id=to, device_id_type=pl.DeviceIdType.MESH)

    for d in range(1, K):
        greet({"gx": x, "gy": lax.rem(k + d, K)})
    @pl.when(has_prev)
    def _():
        greet(prev_id)

    @pl.when(has_next)
    def _():
        greet(next_id)

    for c in range(C):
        for j in range(K):
            @pl.when(jnp.logical_or(k * C + c != x, k != j))
            def _(c=c, j=j):
                greet({"gx": k * C + c, "gy": jnp.int32(j)})

    for t in range(G):
        @pl.when(jnp.logical_or(home != k, x != t))
        def _(t=t):
            greet({"gx": jnp.int32(t), "gy": home})

    for d in range(1, G):
        greet({"gx": lax.rem(x + d, G), "gy": k})

    one = jnp.int32(1)
    nothing = jnp.int32(0)
    heard = (
        K - 1 + G - 1 + G + C * K
        + jnp.where(has_prev, one, nothing)
        + jnp.where(has_next, one, nothing)
        - 2 * jnp.where(home == k, one, nothing)
    )

    @pl.when(k == 0)
    def _():
        fp[:, 0:1] = jnp.zeros((3, 1, NZ, W), jnp.float32)

    @pl.when(k == K - 1)
    def _():
        fp[:, rows + 1:rows + 2] = jnp.zeros((3, 1, NZ, W), jnp.float32)

    line = jnp.zeros((NZ, NY), jnp.float32)
    fl[0] = line
    fl[R + 1] = line
    edge = jnp.zeros((H, NZ, NY), jnp.float32)

    @pl.when(jnp.logical_not(has_prev))
    def _():
        fr[0] = line
        for buf in stages:
            buf[0:H] = edge

    @pl.when(jnp.logical_not(has_next))
    def _():
        fr[1] = line
        for buf in stages:
            buf[H + R:2 * H + R] = edge

    for copy in local[0]:
        copy.wait()
    pl.semaphore_wait(barrier, heard)

    up = {"gx": x, "gy": lax.rem(k + K - 1, K)}
    down = {"gx": x, "gy": lax.rem(k + 1, K)}
    to_up = remote(fp.at[:, 1:2], fp.at[:, rows + 1:rows + 2], fh_send.at[0], fh_recv.at[0], up)
    to_down = remote(fp.at[:, rows:rows + 1], fp.at[:, 0:1], fh_send.at[1], fh_recv.at[1], down)

    @pl.when(k > 0)
    def _():
        to_up.start()

    @pl.when(k < K - 1)
    def _():
        to_down.start()

    def part(at):
        return fp.at[:, pl.ds(at * R, R + 2)]

    def at_edge(c, j):
        low = (j == 0) if c == 0 else (j < 0)
        high = (j == K - 1) if c == C - 1 else (j < 0)
        return jnp.logical_or(low, high)

    columns = pl.ds(pl.multiple_of(x * W, W), W)

    sends = []
    for d in range(K):
        for c in range(C):
            j = lax.rem(k + d, K)
            target = k * C + c
            src = part(c * K + j)
            dst = ub.at[:, :, :, columns]
            far = remote(src, dst, s2_send.at[d * C + c], s2_recv.at[x], {"gx": target, "gy": j})
            near = pltpu.make_async_copy(src, dst, s2_recv.at[x])
            sends.append((c, j, far, near, jnp.logical_and(target == x, j == k)))

    def send_all(edges):
        for c, j, far, near, mine in sends:
            want = at_edge(c, j) if edges else jnp.logical_not(at_edge(c, j))

            @pl.when(jnp.logical_and(want, mine))
            def _(near=near):
                near.start()

            @pl.when(jnp.logical_and(want, jnp.logical_not(mine)))
            def _(far=far):
                far.start()

    send_all(False)

    @pl.when(k < K - 1)
    def _():
        to_up.wait_recv()

    @pl.when(k > 0)
    def _():
        to_down.wait_recv()

    send_all(True)

    halo_up = [remote(cn.at[H:2 * H], cn.at[H + R:2 * H + R], hal_send.at[0], hal_recv.at[0], prev_id)]
    halo_down = [remote(cn.at[R:R + H], cn.at[0:H], hal_send.at[1], hal_recv.at[1], next_id)]

    for copies in local[1:]:
        for copy in copies:
            copy.wait()

    @pl.when(has_prev)
    def _():
        for copy in halo_up:
            copy.start()

    @pl.when(has_next)
    def _():
        for copy in halo_down:
            copy.start()

    @pl.when(has_next)
    def _():
        for copy in halo_up:
            copy.wait_recv()

    @pl.when(has_prev)
    def _():
        for copy in halo_down:
            copy.wait_recv()

    lane = lax.broadcasted_iota(jnp.int32, (NZ, NY), 1)
    level = lax.broadcasted_iota(jnp.int32, (NZ, NY), 0)

    def above(v):
        return jnp.where(level < NZ - 1, pltpu.roll(v, NZ - 1, 0), 0.0)

    def below(v):
        return jnp.where(level > 0, pltpu.roll(v, 1, 0), 0.0)

    def right(v):
        return jnp.where(lane < NY - 1, pltpu.roll(v, NY - 1, 1), 0.0)

    def left(v):
        return jnp.where(lane > 0, pltpu.roll(v, 1, 1), 0.0)

    def plane_sum(v):
        return above(v) + below(v) + right(v) + left(v)

    def inside(i):
        at = place * R + i
        return jnp.logical_and(at >= 0, at < G * K * R)

    def voids_row(n, carry):
        v = 1.0 - cn[n].astype(jnp.float32) * particle_volume
        vo[n] = jnp.where(inside(n - H), v, 0.0)
        return carry

    lax.fori_loop(0, R + 2 * H, voids_row, 0)

    def weight_row(n, carry):
        v = vo[n]
        ws = 0.5 * (6.0 * v + vo[n - 1] + vo[n + 1] + plane_sum(v))
        total_w[n] = ws
        rh[n] = jnp.where(inside(n - H), 1.0 / ws, 0.0)
        wf[n] = 0.5 * (v + vo[n + 1])
        wr[n] = jnp.where(lane < NY - 1, 0.5 * (v + pltpu.roll(v, NY - 1, 1)), 0.0)
        wa[n] = jnp.where(level < NZ - 1, 0.5 * (v + pltpu.roll(v, NZ - 1, 0)), 0.0)
        return carry

    wf[0] = 0.5 * (vo[0] + vo[1])
    lax.fori_loop(1, R + 2 * H - 1, weight_row, 0)

    def weighted(n, p, pa, pb):
        r, a = wr[n], wa[n]
        across = r * pltpu.roll(p, NY - 1, 1) + pltpu.roll(r * p, 1, 1)
        upright = a * pltpu.roll(p, NZ - 1, 0) + pltpu.roll(a * p, 1, 0)
        return (wf[n - 1] * pa + wf[n] * pb) + (across + upright)

    for sender in range(G):
        spot = pl.ds(sender * W, W)
        here = {"gx": x, "gy": k}
        remote(part(0), ub.at[:, :, :, spot], s2_send.at[0], s2_recv.at[sender], here).wait_recv()

    def momentum_row(i, carry):
        v, ws = vo[H + i], total_w[H + i]
        drag = dr[i]
        below_line = 1.0 / (v + time_step * drag)
        for which in range(3):
            u = ub[which, i + 1]
            diffusion = weighted(H + i, u, ub[which, i], ub[which, i + 2]) - ws * u
            force = drag * pv[which, i]
            value = (v * u + (time_step * viscosity) * diffusion + time_step * force) * below_line
            pred[which, i] = value
            f = v * value
            if which == 0:
                fl[i + 1] = f
            elif which == 1:
                part_source = right(f) - left(f)
            else:
                b[H + i] = part_source + (above(f) - below(f))
        return carry

    lax.fori_loop(0, R, momentum_row, 0)

    def source_row(i, carry):
        b[H + i] = -(fl[i + 2] - fl[i] + b[H + i]) * rh[H + i]
        return carry

    lax.fori_loop(0, R, source_row, 0)

    def sweep(src, dst, reach):
        def row(n, carry):
            dst[n] = weighted(n, src[n], src[n - 1], src[n + 1]) * rh[n] + b[n]
            return carry

        lax.fori_loop(H - reach, H + R + reach, row, 0)

    def exchange(turn, depth):
        buf = stages[turn]
        upward = [
            remote(buf.at[H:H + depth], buf.at[H + R:H + R + depth], pr_send.at[2 * turn], pr_recv.at[2 * turn], prev_id)
        ]
        downward = [
            remote(
                buf.at[H + R - depth:H + R], buf.at[H - depth:H], pr_send.at[2 * turn + 1], pr_recv.at[2 * turn + 1], next_id
            )
        ]
        if turn == 0:
            upward.append(remote(fl.at[1], fr.at[1], hal_send.at[2], hal_recv.at[2], prev_id))
            downward.append(remote(fl.at[R], fr.at[0], hal_send.at[3], hal_recv.at[3], next_id))

        @pl.when(has_prev)
        def _():
            for copy in upward:
                copy.start()

        @pl.when(has_next)
        def _():
            for copy in downward:
                copy.start()

        @pl.when(has_prev)
        def _():
            for copy in upward:
                copy.wait_send()

        @pl.when(has_next)
        def _():
            for copy in downward:
                copy.wait_send()

        @pl.when(has_next)
        def _():
            for copy in upward:
                copy.wait_recv()

        @pl.when(has_prev)
        def _():
            for copy in downward:
                copy.wait_recv()

    done = 0
    for turn, depth in enumerate(ROUNDS):
        exchange(turn, depth)
        if turn == 0:
            b[H] = b[H] + fr[0] * rh[H]
            b[H + R - 1] = b[H + R - 1] - fr[1] * rh[H + R - 1]
            b[H - 1] = b[H - 1] - fl[1] * rh[H - 1]
            b[H + R] = b[H + R] + fl[R] * rh[H + R]
        src = stages[turn]
        for reach in range(depth - 1, -1, -1):
            done += 1
            if done == SWEEPS:
                break
            if done == SWEEPS - 1:
                dst = pf
            elif reach == 0:
                dst = stages[turn + 1]
            else:
                dst = t1 if src is t0 else t0
            sweep(src, dst, reach)
            src = dst

    outs = []
    for e in range(1, G):
        target = lax.rem(x + e, G)
        src = pf.at[H:H + R, :, pl.ds(pl.multiple_of(target * W, W), W)]
        outs.append(remote(src, rl.at[x], out_send.at[e], out_recv.at[x], {"gx": target, "gy": k}))
    kept = pltpu.make_async_copy(pf.at[H:H + R, :, columns], rl.at[x], out_recv.at[x])
    kept.start()
    for copy in outs:
        copy.start()

    def slope_row(i, carry):
        n = H + i
        p = pf[n]
        g0 = 0.5 * (pf[n + 1] - pf[n - 1])
        g1 = 0.5 * (right(p) - left(p))
        g2 = 0.5 * (above(p) - below(p))
        for which, g in enumerate((g0, g1, g2)):
            gr[which, i] = g
            pred[which, i] = pred[which, i] - time_step * g
        return carry

    lax.fori_loop(0, R, slope_row, 0)
    written = []
    for z in range(NZ):
        written.append(pltpu.make_async_copy(gr.at[:, :, z], grad_out.at[:, z], loc_sem.at[z]))
        written.append(pltpu.make_async_copy(pred.at[:, :, z], vel_out.at[:, z], loc_sem.at[NZ + z]))
    for copy in written:
        copy.start()

    @pl.when(k > 0)
    def _():
        to_up.wait_send()

    @pl.when(k < K - 1)
    def _():
        to_down.wait_send()

    for c, j, far, near, mine in sends:
        @pl.when(jnp.logical_not(mine))
        def _(far=far):
            far.wait_send()

    @pl.when(has_prev)
    def _():
        for copy in halo_up:
            copy.wait_send()

    @pl.when(has_next)
    def _():
        for copy in halo_down:
            copy.wait_send()

    here = {"gx": x, "gy": k}
    rises = []
    for d in range(K):
        to = lax.rem(home + d, K)
        for c in range(C):
            slot = to * C + c
            remote(pf.at[H:H + R, :, 0:W], rl.at[slot], out_send.at[0], out_recv.at[slot], here).wait_recv()
        src = rl.at[pl.ds(to * C, C)]
        far = remote(src, po.at[:, k], up_send.at[d], up_recv.at[k], {"gx": x, "gy": to})
        near = pltpu.make_async_copy(src, po.at[:, k], up_recv.at[k])

        @pl.when(to != k)
        def _(far=far):
            far.start()

        @pl.when(to == k)
        def _(near=near):
            near.start()

        rises.append((to, far))

    for copy in outs:
        copy.wait_send()

    for to, far in rises:
        @pl.when(to != k)
        def _(far=far):
            far.wait_send()

    for j in range(K):
        remote(rl.at[0:C], po.at[:, j], up_send.at[0], up_recv.at[j], here).wait_recv()
    last = [pltpu.make_async_copy(po.at[:, :, :, z], press_out.at[z], loc_sem.at[2 * NZ + z]) for z in range(NZ)]
    for copy in last:
        copy.start()
    for copy in written + last:
        copy.wait()


def shards(K, G, particle_count, drag_coeff, particle_velocity, fluid_velocity):
    NZ, R, NY = particle_count.shape
    rows, W = fluid_velocity.shape[2:]
    C = G // K
    H = max(ROUNDS)
    f32 = jnp.float32

    dma = pltpu.SemaphoreType.DMA
    pad = (R + 2 * H, NZ, NY)
    scratch = [
        pltpu.VMEM((3, rows + 2, NZ, W), f32),
        pltpu.VMEM((3, R + 2, NZ, NY), f32),
        pltpu.VMEM(pad, jnp.int32),
        pltpu.VMEM((R, NZ, NY), f32),
        pltpu.VMEM((3, R, NZ, NY), f32),
        *[pltpu.VMEM(pad, f32) for _ in range(6)],
        pltpu.VMEM((3, R, NZ, NY), f32),
        pltpu.VMEM((3, R, NZ, NY), f32),
        pltpu.VMEM((R + 2, NZ, NY), f32),
        pltpu.VMEM((2, NZ, NY), f32),
        pltpu.VMEM(pad, f32),
        pltpu.VMEM(pad, f32),
        pltpu.VMEM(pad, f32),
        pltpu.VMEM((G, R, NZ, W), f32),
        pltpu.VMEM((C, K, R, NZ, W), f32),
        dma((4 * NZ,)), dma((2,)), dma((2,)),
        dma((K * C,)), dma((G,)),
        dma((4,)), dma((4,)), dma((2 * len(ROUNDS),)), dma((2 * len(ROUNDS),)), dma((G,)), dma((G,)), dma((K,)), dma((K,)),
        *[pltpu.VMEM(pad, f32) for _ in ROUNDS],
    ]
    anywhere = pl.BlockSpec(memory_space=pl.ANY)
    pressure, velocity, slopes = pl.pallas_call(
        functools.partial(kernel, K, G, R, NZ, NY, W),
        out_shape=(
            jax.ShapeDtypeStruct((NZ, C, K, R, W), f32),
            jax.ShapeDtypeStruct((3, NZ, R, NY), f32),
            jax.ShapeDtypeStruct((3, NZ, R, NY), f32),
        ),
        in_specs=[anywhere] * 4,
        out_specs=(anywhere, anywhere, anywhere),
        scratch_shapes=scratch,
        compiler_params=pltpu.CompilerParams(collective_id=0, has_side_effects=True, vmem_limit_bytes=67043328),
    )(particle_count, drag_coeff, particle_velocity, fluid_velocity)
    return pressure.reshape(NZ, rows, W), velocity, slopes


def solution(mesh):
    placed = (
        P(None, ("gx", "gy"), None),
        P(None, ("gx", "gy"), None),
        P(None, None, ("gx", "gy"), None),
        P(None, None, "gy", "gx"),
    )
    return jax.shard_map(
        functools.partial(shards, mesh.shape["gy"], mesh.shape["gx"]),
        mesh=mesh,
        in_specs=placed,
        out_specs=(
            P(None, "gy", "gx"),
            P(None, None, ("gx", "gy"), None),
            P(None, None, ("gx", "gy"), None),
        ),
        check_vma=False,
    )
```

```python
import functools

import jax
import jax.numpy as jnp
from jax import lax
from jax.experimental import pallas as pl
from jax.experimental.pallas import tpu as pltpu
from jax.sharding import PartitionSpec as P

SWEEPS = 8
ROUNDS = (4, 4)

particle_volume = 0.05
time_step = 0.5
viscosity = 0.1


def kernel(
    K, G, R, NZ, NY, W,
    count_in, drag_in, pvel_in, fluid_in,
    press_out, vel_out, grad_out,
    fp, ub, cn, dr, pv, vo, total_w, wf, wr, wa, rh, pred, gr, fl, fr, eb, lv, rl, po,
    loc_sem, fh_send, fh_recv, s2_send, s2_recv,
    hal_send, hal_recv, b_send, b_recv, p_send, p_recv, out_send, out_recv, up_send, up_recv,
):
    H = max(ROUNDS)
    first, last_level = ROUNDS[0], SWEEPS - 1
    b, pf = lv.at[0], lv.at[last_level]
    C = G // K
    B = C * K
    x = lax.axis_index("gx")
    k = lax.axis_index("gy")
    place = x * K + k
    has_prev = place > 0
    has_next = place < G * K - 1
    prev_id = {"gx": jnp.where(k > 0, x, jnp.maximum(x - 1, 0)), "gy": lax.rem(k + K - 1, K)}
    next_id = {"gx": jnp.where(k < K - 1, x, jnp.minimum(x + 1, G - 1)), "gy": lax.rem(k + 1, K)}

    def remote(src, dst, ssem, rsem, to):
        return pltpu.make_async_remote_copy(
            src_ref=src, dst_ref=dst, send_sem=ssem, recv_sem=rsem, device_id=to, device_id_type=pl.DeviceIdType.MESH
        )

    rows = R * B

    local = [[] for _ in range(4)]
    for z in range(NZ):
        local[0].append(pltpu.make_async_copy(fluid_in.at[:, z], fp.at[:, 1:rows + 1, z], loc_sem.at[z]))
        local[1].append(pltpu.make_async_copy(count_in.at[z], cn.at[H:H + R, z], loc_sem.at[NZ + z]))
        local[2].append(pltpu.make_async_copy(drag_in.at[z], dr.at[:, z], loc_sem.at[2 * NZ + z]))
        local[3].append(pltpu.make_async_copy(pvel_in.at[:, z], pv.at[:, :, z], loc_sem.at[3 * NZ + z]))
    for copies in local:
        for copy in copies:
            copy.start()

    home = x // C
    barrier = pltpu.get_barrier_semaphore()

    def greet(to):
        pl.semaphore_signal(barrier, inc=1, device_id=to, device_id_type=pl.DeviceIdType.MESH)

    for d in range(1, K):
        greet({"gx": x, "gy": lax.rem(k + d, K)})
    @pl.when(has_prev)
    def _():
        greet(prev_id)

    @pl.when(has_next)
    def _():
        greet(next_id)

    for c in range(C):
        for j in range(K):
            @pl.when(jnp.logical_or(k * C + c != x, k != j))
            def _(c=c, j=j):
                greet({"gx": k * C + c, "gy": jnp.int32(j)})

    for t in range(G):
        @pl.when(jnp.logical_or(home != k, x != t))
        def _(t=t):
            greet({"gx": jnp.int32(t), "gy": home})

    for d in range(1, G):
        greet({"gx": lax.rem(x + d, G), "gy": k})

    one = jnp.int32(1)
    nothing = jnp.int32(0)
    heard = (
        K - 1 + G - 1 + G + C * K
        + jnp.where(has_prev, one, nothing)
        + jnp.where(has_next, one, nothing)
        - 2 * jnp.where(home == k, one, nothing)
    )

    @pl.when(k == 0)
    def _():
        fp[:, 0:1] = jnp.zeros((3, 1, NZ, W), jnp.float32)

    @pl.when(k == K - 1)
    def _():
        fp[:, rows + 1:rows + 2] = jnp.zeros((3, 1, NZ, W), jnp.float32)

    line = jnp.zeros((NZ, NY), jnp.float32)
    fl[0] = line
    fl[R + 1] = line
    edge = jnp.zeros((H, NZ, NY), jnp.float32)

    @pl.when(jnp.logical_not(has_prev))
    def _():
        fr[0] = line
        lv[0, 0:H] = edge
        lv[first, 0:H] = edge

    @pl.when(jnp.logical_not(has_next))
    def _():
        fr[1] = line
        lv[0, H + R:2 * H + R] = edge
        lv[first, H + R:2 * H + R] = edge

    for copy in local[0]:
        copy.wait()
    pl.semaphore_wait(barrier, heard)

    up = {"gx": x, "gy": lax.rem(k + K - 1, K)}
    down = {"gx": x, "gy": lax.rem(k + 1, K)}
    to_up = remote(fp.at[:, 1:2], fp.at[:, rows + 1:rows + 2], fh_send.at[0], fh_recv.at[0], up)
    to_down = remote(fp.at[:, rows:rows + 1], fp.at[:, 0:1], fh_send.at[1], fh_recv.at[1], down)

    @pl.when(k > 0)
    def _():
        to_up.start()

    @pl.when(k < K - 1)
    def _():
        to_down.start()

    def part(at):
        return fp.at[:, pl.ds(at * R, R + 2)]

    def at_edge(c, j):
        low = (j == 0) if c == 0 else (j < 0)
        high = (j == K - 1) if c == C - 1 else (j < 0)
        return jnp.logical_or(low, high)

    columns = pl.ds(pl.multiple_of(x * W, W), W)

    sends = []
    for d in range(K):
        for c in range(C):
            j = lax.rem(k + d, K)
            target = k * C + c
            src = part(c * K + j)
            dst = ub.at[:, :, :, columns]
            far = remote(src, dst, s2_send.at[d * C + c], s2_recv.at[x], {"gx": target, "gy": j})
            near = pltpu.make_async_copy(src, dst, s2_recv.at[x])
            sends.append((c, j, far, near, jnp.logical_and(target == x, j == k)))

    def send_all(edges):
        for c, j, far, near, mine in sends:
            want = at_edge(c, j) if edges else jnp.logical_not(at_edge(c, j))

            @pl.when(jnp.logical_and(want, mine))
            def _(near=near):
                near.start()

            @pl.when(jnp.logical_and(want, jnp.logical_not(mine)))
            def _(far=far):
                far.start()

    send_all(False)

    @pl.when(k < K - 1)
    def _():
        to_up.wait_recv()

    @pl.when(k > 0)
    def _():
        to_down.wait_recv()

    send_all(True)

    halo_up = [remote(cn.at[H:2 * H], cn.at[H + R:2 * H + R], hal_send.at[0], hal_recv.at[0], prev_id)]
    halo_down = [remote(cn.at[R:R + H], cn.at[0:H], hal_send.at[1], hal_recv.at[1], next_id)]

    for copies in local[1:]:
        for copy in copies:
            copy.wait()

    @pl.when(has_prev)
    def _():
        for copy in halo_up:
            copy.start()

    @pl.when(has_next)
    def _():
        for copy in halo_down:
            copy.start()

    @pl.when(has_next)
    def _():
        for copy in halo_up:
            copy.wait_recv()

    @pl.when(has_prev)
    def _():
        for copy in halo_down:
            copy.wait_recv()

    lane = lax.broadcasted_iota(jnp.int32, (NZ, NY), 1)
    level = lax.broadcasted_iota(jnp.int32, (NZ, NY), 0)

    def above(v):
        return jnp.where(level < NZ - 1, pltpu.roll(v, NZ - 1, 0), 0.0)

    def below(v):
        return jnp.where(level > 0, pltpu.roll(v, 1, 0), 0.0)

    def right(v):
        return jnp.where(lane < NY - 1, pltpu.roll(v, NY - 1, 1), 0.0)

    def left(v):
        return jnp.where(lane > 0, pltpu.roll(v, 1, 1), 0.0)

    def plane_sum(v):
        return above(v) + below(v) + right(v) + left(v)

    def inside(i):
        at = place * R + i
        return jnp.logical_and(at >= 0, at < G * K * R)

    def voids_row(n, carry):
        v = 1.0 - cn[n].astype(jnp.float32) * particle_volume
        vo[n] = jnp.where(inside(n - H), v, 0.0)
        return carry

    lax.fori_loop(0, R + 2 * H, voids_row, 0)

    def weight_row(n, carry):
        v = vo[n]
        ws = 0.5 * (6.0 * v + vo[n - 1] + vo[n + 1] + plane_sum(v))
        total_w[n] = ws
        rh[n] = jnp.where(inside(n - H), 1.0 / ws, 0.0)
        wf[n] = 0.5 * (v + vo[n + 1])
        wr[n] = jnp.where(lane < NY - 1, 0.5 * (v + pltpu.roll(v, NY - 1, 1)), 0.0)
        wa[n] = jnp.where(level < NZ - 1, 0.5 * (v + pltpu.roll(v, NZ - 1, 0)), 0.0)
        return carry

    wf[0] = 0.5 * (vo[0] + vo[1])
    lax.fori_loop(1, R + 2 * H - 1, weight_row, 0)

    def weighted(n, p, pa, pb):
        r, a = wr[n], wa[n]
        across = r * pltpu.roll(p, NY - 1, 1) + pltpu.roll(r * p, 1, 1)
        upright = a * pltpu.roll(p, NZ - 1, 0) + pltpu.roll(a * p, 1, 0)
        return (wf[n - 1] * pa + wf[n] * pb) + (across + upright)

    for sender in range(G):
        spot = pl.ds(sender * W, W)
        here = {"gx": x, "gy": k}
        remote(part(0), ub.at[:, :, :, spot], s2_send.at[0], s2_recv.at[sender], here).wait_recv()

    def pass_on(src_up, dst_up, src_down, dst_down, ssem, rsem, at):
        return (
            remote(src_up, dst_up, ssem.at[0, at], rsem.at[0, at], prev_id),
            remote(src_down, dst_down, ssem.at[1, at], rsem.at[1, at], next_id),
        )

    def flux_rows():
        return pass_on(fl.at[1], fr.at[1], fl.at[R], fr.at[0], b_send, b_recv, 0)

    def level_rows(buf, s, ssem, rsem, at):
        return pass_on(buf.at[H + s], buf.at[H + R + s], buf.at[H + R - 1 - s], buf.at[H - 1 - s], ssem, rsem, at)

    def base_rows(s):
        return level_rows(b, s, b_send, b_recv, s + 1)

    def edge_rows():
        return pass_on(eb.at[0], b.at[H + R], eb.at[1], b.at[H - 1], b_send, b_recv, 1)

    def mid_rows(s):
        return level_rows(lv.at[first], s, p_send, p_recv, s)

    def launch(copies):
        @pl.when(has_prev)
        def _():
            copies[0].start()

        @pl.when(has_next)
        def _():
            copies[1].start()

    def arrived(copies):
        @pl.when(has_next)
        def _():
            copies[0].wait_recv()

        @pl.when(has_prev)
        def _():
            copies[1].wait_recv()

    def sent(copies):
        @pl.when(has_prev)
        def _():
            copies[0].wait_send()

        @pl.when(has_next)
        def _():
            copies[1].wait_send()

    def momentum(i, which):
        v, ws, drag, u = vo[H + i], total_w[H + i], dr[i], ub[which, i + 1]
        diffusion = weighted(H + i, u, ub[which, i], ub[which, i + 2]) - ws * u
        force = drag * pv[which, i]
        return (v * u + (time_step * viscosity) * diffusion + time_step * force) / (v + time_step * drag)

    def finish(i):
        b[H + i] = -(fl[i + 2] - fl[i] + b[H + i]) * rh[H + i]

    def momentum_step(s, carry):
        pair = (s, R - 1 - s)
        for which in range(3):
            values = [momentum(i, which) for i in pair]
            for i, value in zip(pair, values):
                pred[which, i] = value
            flux = [vo[H + i] * value for i, value in zip(pair, values)]
            if which == 0:
                for i, f in zip(pair, flux):
                    fl[i + 1] = f

                @pl.when(s == 0)
                def _():
                    launch(flux_rows())

            elif which == 1:
                part_source = [right(f) - left(f) for f in flux]
            else:
                for i, f, part in zip(pair, flux, part_source):
                    b[H + i] = part + (above(f) - below(f))

        @pl.when(s > 0)
        def _():
            finish(s - 1)
            finish(R - s)

            @pl.when(s == 1)
            def _():
                eb[0] = b[H]
                eb[1] = b[H + R - 1]
                launch(edge_rows())

            @pl.when(jnp.logical_and(s > 1, s <= H))
            def _():
                launch(base_rows(s - 1))

        return carry

    half = R // 2
    lax.fori_loop(0, half, momentum_step, 0)
    finish(half - 1)
    finish(R - half)
    if half <= H:
        launch(base_rows(half - 1))

    def sweep_pair(l, lo):
        hi = 2 * H + R - 1 - lo
        values = [
            weighted(n, lv[l - 1, n], lv[l - 1, n - 1], lv[l - 1, n + 1]) * rh[n] + b[n] for n in (lo, hi)
        ]
        lv[l, lo] = values[0]
        lv[l, hi] = values[1]

    def diagonal(j, start, stop):
        def level(l, carry):
            sweep_pair(l, l + (H - j))
            return carry

        lax.fori_loop(start, stop, level, 0)

    def rows_of(l, start, stop):
        def row(lo, carry):
            sweep_pair(l, lo)
            return carry

        lax.fori_loop(H + start, H + stop, row, 0)

    for j in range(2 - half, H + 1):
        if j == 0:
            arrived(flux_rows())
            b[H] = b[H] + fr[0] * rh[H]
            b[H + R - 1] = b[H + R - 1] - fr[1] * rh[H + R - 1]
        elif j > 0:
            arrived(base_rows(j - 1))
            if j == 1:
                b[H - 1] = b[H - 1] - fl[1] * rh[H - 1]
                b[H + R] = b[H + R] + fl[R] * rh[H + R]
        stop = min(last_level, j + half - 1) + 1
        diagonal(j, 1, min(stop, first + 1))
        if j > 0:
            launch(mid_rows(first - j))
        if stop > first + 1:
            diagonal(j, first + 1, stop)

    depth = last_level - first
    for s in range(first - 1, 0, -1):
        arrived(mid_rows(s))
    rows_of(first + 1, -depth, 1 - depth)
    arrived(mid_rows(0))
    for l in range(first + 1, last_level + 1):
        low = l - last_level - 1 + (1 if l in (first + 1, last_level) else 0)
        rows_of(l, low, l - H)

    outs = []
    for e in range(1, G):
        target = lax.rem(x + e, G)
        src = pf.at[H:H + R, :, pl.ds(pl.multiple_of(target * W, W), W)]
        outs.append(remote(src, rl.at[x], out_send.at[e], out_recv.at[x], {"gx": target, "gy": k}))
    kept = pltpu.make_async_copy(pf.at[H:H + R, :, columns], rl.at[x], out_recv.at[x])
    kept.start()
    for copy in outs:
        copy.start()

    rows_of(last_level, -1, 0)

    def slope_row(i, carry):
        n = H + i
        p = pf[n]
        g0 = 0.5 * (pf[n + 1] - pf[n - 1])
        g1 = 0.5 * (right(p) - left(p))
        g2 = 0.5 * (above(p) - below(p))
        for which, g in enumerate((g0, g1, g2)):
            gr[which, i] = g
            pred[which, i] = pred[which, i] - time_step * g
        return carry

    lax.fori_loop(0, R, slope_row, 0)
    written = []
    for z in range(NZ):
        written.append(pltpu.make_async_copy(gr.at[:, :, z], grad_out.at[:, z], loc_sem.at[z]))
        written.append(pltpu.make_async_copy(pred.at[:, :, z], vel_out.at[:, z], loc_sem.at[NZ + z]))
    for copy in written:
        copy.start()

    @pl.when(k > 0)
    def _():
        to_up.wait_send()

    @pl.when(k < K - 1)
    def _():
        to_down.wait_send()

    for c, j, far, near, mine in sends:
        @pl.when(jnp.logical_not(mine))
        def _(far=far):
            far.wait_send()

    @pl.when(has_prev)
    def _():
        for copy in halo_up:
            copy.wait_send()

    @pl.when(has_next)
    def _():
        for copy in halo_down:
            copy.wait_send()

    here = {"gx": x, "gy": k}
    rises = []
    for d in range(K):
        to = lax.rem(home + d, K)
        for c in range(C):
            slot = to * C + c
            remote(pf.at[H:H + R, :, 0:W], rl.at[slot], out_send.at[0], out_recv.at[slot], here).wait_recv()
        src = rl.at[pl.ds(to * C, C)]
        far = remote(src, po.at[:, k], up_send.at[d], up_recv.at[k], {"gx": x, "gy": to})
        near = pltpu.make_async_copy(src, po.at[:, k], up_recv.at[k])

        @pl.when(to != k)
        def _(far=far):
            far.start()

        @pl.when(to == k)
        def _(near=near):
            near.start()

        rises.append((to, far))

    for copies in [flux_rows(), edge_rows()] + [base_rows(i) for i in range(1, H)] + [mid_rows(i) for i in range(first)]:
        sent(copies)

    for copy in outs:
        copy.wait_send()

    for to, far in rises:
        @pl.when(to != k)
        def _(far=far):
            far.wait_send()

    for j in range(K):
        remote(rl.at[0:C], po.at[:, j], up_send.at[0], up_recv.at[j], here).wait_recv()
    last = [pltpu.make_async_copy(po.at[:, :, :, z], press_out.at[z], loc_sem.at[2 * NZ + z]) for z in range(NZ)]
    for copy in last:
        copy.start()
    for copy in written + last:
        copy.wait()


def settle(*refs):
    n = len(refs) // 2
    copies = [pltpu.make_async_copy(refs[i], refs[n + i], refs[-1].at[i]) for i in range(n)]
    for copy in copies:
        copy.start()
    for copy in copies:
        copy.wait()


def shards(K, G, particle_count, drag_coeff, particle_velocity, fluid_velocity):
    NZ, R, NY = particle_count.shape
    rows, W = fluid_velocity.shape[2:]
    C = G // K
    H = max(ROUNDS)
    f32 = jnp.float32

    dma = pltpu.SemaphoreType.DMA
    pad = (R + 2 * H, NZ, NY)
    scratch = [
        pltpu.VMEM((3, rows + 2, NZ, W), f32),
        pltpu.VMEM((3, R + 2, NZ, NY), f32),
        pltpu.VMEM(pad, jnp.int32),
        pltpu.VMEM((R, NZ, NY), f32),
        pltpu.VMEM((3, R, NZ, NY), f32),
        *[pltpu.VMEM(pad, f32) for _ in range(6)],
        pltpu.VMEM((3, R, NZ, NY), f32),
        pltpu.VMEM((3, R, NZ, NY), f32),
        pltpu.VMEM((R + 2, NZ, NY), f32),
        pltpu.VMEM((2, NZ, NY), f32),
        pltpu.VMEM((2, NZ, NY), f32),
        pltpu.VMEM((SWEEPS,) + pad, f32),
        pltpu.VMEM((G, R, NZ, W), f32),
        pltpu.VMEM((C, K, R, NZ, W), f32),
        dma((4 * NZ,)), dma((2,)), dma((2,)),
        dma((K * C,)), dma((G,)),
        dma((2,)), dma((2,)), dma((2, H + 1)), dma((2, H + 1)), dma((2, H)), dma((2, H)), dma((G,)), dma((G,)), dma((K,)), dma((K,)),
    ]
    anywhere = pl.BlockSpec(memory_space=pl.ANY)
    pressure, velocity, slopes = pl.pallas_call(
        functools.partial(kernel, K, G, R, NZ, NY, W),
        out_shape=(
            jax.ShapeDtypeStruct((NZ, C, K, R, W), f32),
            jax.ShapeDtypeStruct((3, NZ, R, NY), f32),
            jax.ShapeDtypeStruct((3, NZ, R, NY), f32),
        ),
        in_specs=[anywhere] * 4,
        out_specs=(anywhere, anywhere, anywhere),
        scratch_shapes=scratch,
        compiler_params=pltpu.CompilerParams(collective_id=0, has_side_effects=True, vmem_limit_bytes=67043328),
    )(particle_count, drag_coeff, particle_velocity, fluid_velocity)
    found = (pressure.reshape(NZ, rows, W), velocity, slopes)
    return pl.pallas_call(
        settle,
        out_shape=[jax.ShapeDtypeStruct(v.shape, f32) for v in found],
        in_specs=[pl.BlockSpec(memory_space=pltpu.VMEM)] * 3,
        out_specs=[anywhere] * 3,
        scratch_shapes=[dma((3,))],
    )(*found)


def solution(mesh):
    placed = (
        P(None, ("gx", "gy"), None),
        P(None, ("gx", "gy"), None),
        P(None, None, ("gx", "gy"), None),
        P(None, None, "gy", "gx"),
    )
    return jax.shard_map(
        functools.partial(shards, mesh.shape["gy"], mesh.shape["gx"]),
        mesh=mesh,
        in_specs=placed,
        out_specs=(
            P(None, "gy", "gx"),
            P(None, None, ("gx", "gy"), None),
            P(None, None, ("gx", "gy"), None),
        ),
        check_vma=False,
    )
```

```python
import functools

import jax
import jax.numpy as jnp
from jax import lax
from jax.experimental import pallas as pl
from jax.experimental.pallas import tpu as pltpu
from jax.sharding import PartitionSpec as P

SWEEPS = 8
ROUNDS = (4, 4)

particle_volume = 0.05
time_step = 0.5
viscosity = 0.1


def kernel(
    K, G, R, NZ, NY, W,
    count_in, drag_in, pvel_in, fluid_in,
    press_out, vel_out, grad_out,
    fp, ub, cn, dr, pv, vo, total_w, wf, wr, wa, rh, pred, gr, fl, fr, eb, lv, rl, po,
    loc_sem, row_send, row_recv, s2_send, s2_recv,
    hal_send, hal_recv, b_send, b_recv, p_send, p_recv, out_send, out_recv, up_send, up_recv,
):
    H = max(ROUNDS)
    first, last_level = ROUNDS[0], SWEEPS - 1
    b, pf = lv.at[0], lv.at[last_level]
    C = G // K
    B = C * K
    x = lax.axis_index("gx")
    k = lax.axis_index("gy")
    place = x * K + k
    has_prev = place > 0
    has_next = place < G * K - 1
    prev_id = {"gx": jnp.where(k > 0, x, jnp.maximum(x - 1, 0)), "gy": lax.rem(k + K - 1, K)}
    next_id = {"gx": jnp.where(k < K - 1, x, jnp.minimum(x + 1, G - 1)), "gy": lax.rem(k + 1, K)}

    def remote(src, dst, ssem, rsem, to):
        return pltpu.make_async_remote_copy(
            src_ref=src, dst_ref=dst, send_sem=ssem, recv_sem=rsem, device_id=to, device_id_type=pl.DeviceIdType.MESH
        )

    rows = R * B

    local = [[] for _ in range(4)]
    for z in range(NZ):
        local[0].append(pltpu.make_async_copy(fluid_in.at[:, z], fp.at[:, :, z], loc_sem.at[z]))
        local[1].append(pltpu.make_async_copy(count_in.at[z], cn.at[H:H + R, z], loc_sem.at[NZ + z]))
        local[2].append(pltpu.make_async_copy(drag_in.at[z], dr.at[:, z], loc_sem.at[2 * NZ + z]))
        local[3].append(pltpu.make_async_copy(pvel_in.at[:, z], pv.at[:, :, z], loc_sem.at[3 * NZ + z]))
    for copy in local[0]:
        copy.start()

    home = x // C
    barrier = pltpu.get_barrier_semaphore()
    for d in range(1, G * K):
        to = {"gx": lax.rem(x + d // K, G), "gy": lax.rem(k + d % K, K)}
        pl.semaphore_signal(barrier, inc=1, device_id=to, device_id_type=pl.DeviceIdType.MESH)

    for copies in local[1:]:
        for copy in copies:
            copy.start()

    line = jnp.zeros((NZ, NY), jnp.float32)

    @pl.when(jnp.logical_not(has_prev))
    def _():
        for which in range(3):
            ub[which, 0] = line

    @pl.when(jnp.logical_not(has_next))
    def _():
        for which in range(3):
            ub[which, R + 1] = line

    fl[0] = line
    fl[R + 1] = line
    edge = jnp.zeros((H, NZ, NY), jnp.float32)

    @pl.when(jnp.logical_not(has_prev))
    def _():
        fr[0] = line
        lv[0, 0:H] = edge
        lv[first, 0:H] = edge

    @pl.when(jnp.logical_not(has_next))
    def _():
        fr[1] = line
        lv[0, H + R:2 * H + R] = edge
        lv[first, H + R:2 * H + R] = edge

    for copy in local[0]:
        copy.wait()
    pl.semaphore_wait(barrier, G * K - 1)

    columns = pl.ds(pl.multiple_of(x * W, W), W)
    chip = x // C
    sends = []
    for c in range(C):
        for d in range(K):
            j = lax.rem(k + d + K - chip, K)
            at = (c * K + j) * R
            mine = jnp.logical_and(k * C + c == x, j == k)
            low = (j == 0) if c == 0 else None
            high = (j == K - 1) if c == C - 1 else None
            inner = jnp.bool_(True)
            forms = []
            if low is not None:
                inner = jnp.logical_and(inner, jnp.logical_not(low))
                forms.append((low, 0, 1))
            if high is not None:
                inner = jnp.logical_and(inner, jnp.logical_not(high))
                forms.append((high, 1, 0))
            forms.append((inner, 1, 1))
            for want, before, after in forms:
                n = before + R + after
                src = fp.at[:, pl.ds(at - before, n)]
                dst = ub.at[:, pl.ds(1 - before, n), :, columns]
                far = remote(src, dst, s2_send.at[c * K + d], s2_recv.at[x], {"gx": k * C + c, "gy": j})
                near = pltpu.make_async_copy(src, dst, s2_recv.at[x])
                near_when = jnp.logical_and(want, mine)
                far_when = jnp.logical_and(want, jnp.logical_not(mine))

                @pl.when(near_when)
                def _(near=near):
                    near.start()

                @pl.when(far_when)
                def _(far=far):
                    far.start()

                sends.append((far_when, far))

    for n, (want, row, at, gx, gy) in enumerate((
        (k > 0, 0, R + 1, jnp.maximum(k * C - 1, 0), K - 1),
        (k < K - 1, rows - 1, 0, jnp.minimum((k + 1) * C, G - 1), 0),
    )):
        src = fp.at[:, row:row + 1]
        dst = ub.at[:, at:at + 1, :, columns]
        far = remote(src, dst, row_send.at[n], row_recv.at[x], {"gx": gx, "gy": jnp.int32(gy)})
        near = pltpu.make_async_copy(src, dst, row_recv.at[x])
        mine = jnp.logical_and(gx == x, k == gy)
        far_when = jnp.logical_and(want, jnp.logical_not(mine))

        @pl.when(jnp.logical_and(want, mine))
        def _(near=near):
            near.start()

        @pl.when(far_when)
        def _(far=far):
            far.start()

        sends.append((far_when, far))

    halo_up = [remote(cn.at[H:2 * H], cn.at[H + R:2 * H + R], hal_send.at[0], hal_recv.at[0], prev_id)]
    halo_down = [remote(cn.at[R:R + H], cn.at[0:H], hal_send.at[1], hal_recv.at[1], next_id)]

    for copies in local[1:]:
        for copy in copies:
            copy.wait()

    @pl.when(has_prev)
    def _():
        for copy in halo_up:
            copy.start()

    @pl.when(has_next)
    def _():
        for copy in halo_down:
            copy.start()

    @pl.when(has_next)
    def _():
        for copy in halo_up:
            copy.wait_recv()

    @pl.when(has_prev)
    def _():
        for copy in halo_down:
            copy.wait_recv()

    lane = lax.broadcasted_iota(jnp.int32, (NZ, NY), 1)
    level = lax.broadcasted_iota(jnp.int32, (NZ, NY), 0)

    def above(v):
        return jnp.where(level < NZ - 1, pltpu.roll(v, NZ - 1, 0), 0.0)

    def below(v):
        return jnp.where(level > 0, pltpu.roll(v, 1, 0), 0.0)

    def right(v):
        return jnp.where(lane < NY - 1, pltpu.roll(v, NY - 1, 1), 0.0)

    def left(v):
        return jnp.where(lane > 0, pltpu.roll(v, 1, 1), 0.0)

    def plane_sum(v):
        return above(v) + below(v) + right(v) + left(v)

    def inside(i):
        at = place * R + i
        return jnp.logical_and(at >= 0, at < G * K * R)

    def voids_row(n, carry):
        v = 1.0 - cn[n].astype(jnp.float32) * particle_volume
        vo[n] = jnp.where(inside(n - H), v, 0.0)
        return carry

    lax.fori_loop(0, R + 2 * H, voids_row, 0)

    def weight_row(n, carry):
        v = vo[n]
        ws = 0.5 * (6.0 * v + vo[n - 1] + vo[n + 1] + plane_sum(v))
        total_w[n] = ws
        rh[n] = jnp.where(inside(n - H), 1.0 / ws, 0.0)
        wf[n] = 0.5 * (v + vo[n + 1])
        wr[n] = jnp.where(lane < NY - 1, 0.5 * (v + pltpu.roll(v, NY - 1, 1)), 0.0)
        wa[n] = jnp.where(level < NZ - 1, 0.5 * (v + pltpu.roll(v, NZ - 1, 0)), 0.0)
        return carry

    wf[0] = 0.5 * (vo[0] + vo[1])
    lax.fori_loop(1, R + 2 * H - 1, weight_row, 0)

    def weighted(n, p, pa, pb):
        r, a = wr[n], wa[n]
        across = r * pltpu.roll(p, NY - 1, 1) + pltpu.roll(r * p, 1, 1)
        upright = a * pltpu.roll(p, NZ - 1, 0) + pltpu.roll(a * p, 1, 0)
        return (wf[n - 1] * pa + wf[n] * pb) + (across + upright)

    here = {"gx": x, "gy": k}
    slab_low = jnp.logical_and(lax.rem(x, C) == 0, k == 0)
    slab_high = jnp.logical_and(lax.rem(x, C) == C - 1, k == K - 1)
    at_side = jnp.logical_or(slab_low, slab_high)
    extra = jnp.logical_or(jnp.logical_and(slab_low, has_prev), jnp.logical_and(slab_high, has_next))

    def landed(n, sem):
        for sender in range(G):
            spot = pl.ds(sender * W, W)
            remote(fp.at[:, 0:n], ub.at[:, 0:n, :, spot], row_send.at[0], sem.at[sender], here).wait_recv()

    @pl.when(at_side)
    def _():
        landed(R + 1, s2_recv)

    @pl.when(jnp.logical_not(at_side))
    def _():
        landed(R + 2, s2_recv)

    @pl.when(extra)
    def _():
        landed(1, row_recv)

    def pass_on(src_up, dst_up, src_down, dst_down, ssem, rsem, at):
        return (
            remote(src_up, dst_up, ssem.at[0, at], rsem.at[0, at], prev_id),
            remote(src_down, dst_down, ssem.at[1, at], rsem.at[1, at], next_id),
        )

    def flux_rows():
        return pass_on(fl.at[1], fr.at[1], fl.at[R], fr.at[0], b_send, b_recv, 0)

    def level_rows(buf, s, ssem, rsem, at):
        return pass_on(buf.at[H + s], buf.at[H + R + s], buf.at[H + R - 1 - s], buf.at[H - 1 - s], ssem, rsem, at)

    def base_rows(s):
        return level_rows(b, s, b_send, b_recv, s + 1)

    def edge_rows():
        return pass_on(eb.at[0], b.at[H + R], eb.at[1], b.at[H - 1], b_send, b_recv, 1)

    def mid_rows(s):
        return level_rows(lv.at[first], s, p_send, p_recv, s)

    def launch(copies):
        @pl.when(has_prev)
        def _():
            copies[0].start()

        @pl.when(has_next)
        def _():
            copies[1].start()

    def arrived(copies):
        @pl.when(has_next)
        def _():
            copies[0].wait_recv()

        @pl.when(has_prev)
        def _():
            copies[1].wait_recv()

    def sent(copies):
        @pl.when(has_prev)
        def _():
            copies[0].wait_send()

        @pl.when(has_next)
        def _():
            copies[1].wait_send()

    def momentum(i, which):
        v, ws, drag, u = vo[H + i], total_w[H + i], dr[i], ub[which, i + 1]
        diffusion = weighted(H + i, u, ub[which, i], ub[which, i + 2]) - ws * u
        force = drag * pv[which, i]
        return (v * u + (time_step * viscosity) * diffusion + time_step * force) / (v + time_step * drag)

    def finish(i):
        b[H + i] = -(fl[i + 2] - fl[i] + b[H + i]) * rh[H + i]

    def momentum_step(s, carry):
        pair = (s, R - 1 - s)
        for which in range(3):
            values = [momentum(i, which) for i in pair]
            for i, value in zip(pair, values):
                pred[which, i] = value
            flux = [vo[H + i] * value for i, value in zip(pair, values)]
            if which == 0:
                for i, f in zip(pair, flux):
                    fl[i + 1] = f

                @pl.when(s == 0)
                def _():
                    launch(flux_rows())

            elif which == 1:
                part_source = [right(f) - left(f) for f in flux]
            else:
                for i, f, part in zip(pair, flux, part_source):
                    b[H + i] = part + (above(f) - below(f))

        @pl.when(s > 0)
        def _():
            finish(s - 1)
            finish(R - s)

            @pl.when(s == 1)
            def _():
                eb[0] = b[H]
                eb[1] = b[H + R - 1]
                launch(edge_rows())

            @pl.when(jnp.logical_and(s > 1, s <= H))
            def _():
                launch(base_rows(s - 1))

        return carry

    half = R // 2
    lax.fori_loop(0, half, momentum_step, 0)
    finish(half - 1)
    finish(R - half)
    if half <= H:
        launch(base_rows(half - 1))

    def sweep_pair(l, lo):
        hi = 2 * H + R - 1 - lo
        values = [
            weighted(n, lv[l - 1, n], lv[l - 1, n - 1], lv[l - 1, n + 1]) * rh[n] + b[n] for n in (lo, hi)
        ]
        lv[l, lo] = values[0]
        lv[l, hi] = values[1]

    def diagonal(j, start, stop):
        def level(l, carry):
            sweep_pair(l, l + (H - j))
            return carry

        lax.fori_loop(start, stop, level, 0)

    def rows_of(l, start, stop):
        def row(lo, carry):
            sweep_pair(l, lo)
            return carry

        lax.fori_loop(H + start, H + stop, row, 0)

    for j in range(2 - half, H + 1):
        if j == 0:
            arrived(flux_rows())
            b[H] = b[H] + fr[0] * rh[H]
            b[H + R - 1] = b[H + R - 1] - fr[1] * rh[H + R - 1]
        elif j > 0:
            arrived(base_rows(j - 1))
            if j == 1:
                b[H - 1] = b[H - 1] - fl[1] * rh[H - 1]
                b[H + R] = b[H + R] + fl[R] * rh[H + R]
        stop = min(last_level, j + half - 1) + 1
        diagonal(j, 1, min(stop, first + 1))
        if j > 0:
            launch(mid_rows(first - j))
        if stop > first + 1:
            diagonal(j, first + 1, stop)

    depth = last_level - first
    for s in range(first - 1, 0, -1):
        arrived(mid_rows(s))
    rows_of(first + 1, -depth, 1 - depth)
    arrived(mid_rows(0))
    for l in range(first + 1, last_level + 1):
        low = l - last_level - 1 + (1 if l in (first + 1, last_level) else 0)
        rows_of(l, low, l - H)

    outs = []
    for e in range(1, G):
        target = lax.rem(x + e, G)
        src = pf.at[H:H + R, :, pl.ds(pl.multiple_of(target * W, W), W)]
        outs.append(remote(src, rl.at[x], out_send.at[e], out_recv.at[x], {"gx": target, "gy": k}))
    kept = pltpu.make_async_copy(pf.at[H:H + R, :, columns], rl.at[x], out_recv.at[x])
    kept.start()
    for copy in outs:
        copy.start()

    rows_of(last_level, -1, 0)

    def slope_row(i, carry):
        n = H + i
        p = pf[n]
        g0 = 0.5 * (pf[n + 1] - pf[n - 1])
        g1 = 0.5 * (right(p) - left(p))
        g2 = 0.5 * (above(p) - below(p))
        for which, g in enumerate((g0, g1, g2)):
            gr[which, i] = g
            pred[which, i] = pred[which, i] - time_step * g
        return carry

    lax.fori_loop(0, R, slope_row, 0)
    written = []
    for z in range(NZ):
        written.append(pltpu.make_async_copy(gr.at[:, :, z], grad_out.at[:, z], loc_sem.at[z]))
        written.append(pltpu.make_async_copy(pred.at[:, :, z], vel_out.at[:, z], loc_sem.at[NZ + z]))
    for copy in written:
        copy.start()

    for want, copy in sends:
        @pl.when(want)
        def _(copy=copy):
            copy.wait_send()

    @pl.when(has_prev)
    def _():
        for copy in halo_up:
            copy.wait_send()

    @pl.when(has_next)
    def _():
        for copy in halo_down:
            copy.wait_send()

    rises = []
    for d in range(K):
        to = lax.rem(home + d, K)
        for c in range(C):
            slot = to * C + c
            remote(pf.at[H:H + R, :, 0:W], rl.at[slot], out_send.at[0], out_recv.at[slot], here).wait_recv()
        src = rl.at[pl.ds(to * C, C)]
        far = remote(src, po.at[:, k], up_send.at[d], up_recv.at[k], {"gx": x, "gy": to})
        near = pltpu.make_async_copy(src, po.at[:, k], up_recv.at[k])

        @pl.when(to != k)
        def _(far=far):
            far.start()

        @pl.when(to == k)
        def _(near=near):
            near.start()

        rises.append((to, far))

    for copies in [flux_rows(), edge_rows()] + [base_rows(i) for i in range(1, H)] + [mid_rows(i) for i in range(first)]:
        sent(copies)

    for copy in outs:
        copy.wait_send()

    for to, far in rises:
        @pl.when(to != k)
        def _(far=far):
            far.wait_send()

    for j in range(K):
        remote(rl.at[0:C], po.at[:, j], up_send.at[0], up_recv.at[j], here).wait_recv()
    last = [pltpu.make_async_copy(po.at[:, :, :, z], press_out.at[z], loc_sem.at[2 * NZ + z]) for z in range(NZ)]
    for copy in last:
        copy.start()
    for copy in written + last:
        copy.wait()


def settle(*refs):
    n = len(refs) // 2
    copies = [pltpu.make_async_copy(refs[i], refs[n + i], refs[-1].at[i]) for i in range(n)]
    for copy in copies:
        copy.start()
    for copy in copies:
        copy.wait()


def shards(K, G, particle_count, drag_coeff, particle_velocity, fluid_velocity):
    NZ, R, NY = particle_count.shape
    rows, W = fluid_velocity.shape[2:]
    C = G // K
    H = max(ROUNDS)
    f32 = jnp.float32

    dma = pltpu.SemaphoreType.DMA
    pad = (R + 2 * H, NZ, NY)
    scratch = [
        pltpu.VMEM((3, rows, NZ, W), f32),
        pltpu.VMEM((3, R + 2, NZ, NY), f32),
        pltpu.VMEM(pad, jnp.int32),
        pltpu.VMEM((R, NZ, NY), f32),
        pltpu.VMEM((3, R, NZ, NY), f32),
        *[pltpu.VMEM(pad, f32) for _ in range(6)],
        pltpu.VMEM((3, R, NZ, NY), f32),
        pltpu.VMEM((3, R, NZ, NY), f32),
        pltpu.VMEM((R + 2, NZ, NY), f32),
        pltpu.VMEM((2, NZ, NY), f32),
        pltpu.VMEM((2, NZ, NY), f32),
        pltpu.VMEM((SWEEPS,) + pad, f32),
        pltpu.VMEM((G, R, NZ, W), f32),
        pltpu.VMEM((C, K, R, NZ, W), f32),
        dma((4 * NZ,)), dma((2,)), dma((G,)),
        dma((K * C,)), dma((G,)),
        dma((2,)), dma((2,)), dma((2, H + 1)), dma((2, H + 1)), dma((2, H)), dma((2, H)), dma((G,)), dma((G,)), dma((K,)), dma((K,)),
    ]
    anywhere = pl.BlockSpec(memory_space=pl.ANY)
    pressure, velocity, slopes = pl.pallas_call(
        functools.partial(kernel, K, G, R, NZ, NY, W),
        out_shape=(
            jax.ShapeDtypeStruct((NZ, C, K, R, W), f32),
            jax.ShapeDtypeStruct((3, NZ, R, NY), f32),
            jax.ShapeDtypeStruct((3, NZ, R, NY), f32),
        ),
        in_specs=[anywhere] * 4,
        out_specs=(anywhere, anywhere, anywhere),
        scratch_shapes=scratch,
        compiler_params=pltpu.CompilerParams(collective_id=0, has_side_effects=True, vmem_limit_bytes=67043328),
    )(particle_count, drag_coeff, particle_velocity, fluid_velocity)
    found = (pressure.reshape(NZ, rows, W), velocity, slopes)
    return pl.pallas_call(
        settle,
        out_shape=[jax.ShapeDtypeStruct(v.shape, f32) for v in found],
        in_specs=[pl.BlockSpec(memory_space=pltpu.VMEM)] * 3,
        out_specs=[anywhere] * 3,
        scratch_shapes=[dma((3,))],
    )(*found)


def solution(mesh):
    placed = (
        P(None, ("gx", "gy"), None),
        P(None, ("gx", "gy"), None),
        P(None, None, ("gx", "gy"), None),
        P(None, None, "gy", "gx"),
    )
    return jax.shard_map(
        functools.partial(shards, mesh.shape["gy"], mesh.shape["gx"]),
        mesh=mesh,
        in_specs=placed,
        out_specs=(
            P(None, "gy", "gx"),
            P(None, None, ("gx", "gy"), None),
            P(None, None, ("gx", "gy"), None),
        ),
        check_vma=False,
    )
```

```python
import functools

import jax
import jax.numpy as jnp
from jax import lax
from jax.experimental import pallas as pl
from jax.experimental.pallas import tpu as pltpu
from jax.sharding import PartitionSpec as P

SWEEPS = 8
ROUNDS = (4, 4)

particle_volume = 0.05
time_step = 0.5
viscosity = 0.1


def kernel(
    K, G, R, NZ, NY, W,
    count_in, drag_in, pvel_in, fluid_in,
    press_out, vel_out, grad_out,
    fp, ub, cn, dr, pv, vo, total_w, wf, wr, wa, rh, pred, gr, fl, fr, eb, lv, rl,
    loc_sem, row_send, row_recv, s2_send, s2_recv,
    hal_send, hal_recv, b_send, b_recv, p_send, p_recv, out_send, out_recv, up_send, up_recv,
):
    H = max(ROUNDS)
    first, last_level = ROUNDS[0], SWEEPS - 1
    b, pf = lv.at[0], lv.at[last_level]
    C = G // K
    B = C * K
    x = lax.axis_index("gx")
    k = lax.axis_index("gy")
    place = x * K + k
    has_prev = place > 0
    has_next = place < G * K - 1
    prev_id = {"gx": jnp.where(k > 0, x, jnp.maximum(x - 1, 0)), "gy": lax.rem(k + K - 1, K)}
    next_id = {"gx": jnp.where(k < K - 1, x, jnp.minimum(x + 1, G - 1)), "gy": lax.rem(k + 1, K)}

    def remote(src, dst, ssem, rsem, to):
        return pltpu.make_async_remote_copy(
            src_ref=src, dst_ref=dst, send_sem=ssem, recv_sem=rsem, device_id=to, device_id_type=pl.DeviceIdType.MESH
        )

    rows = R * B

    local = [[] for _ in range(4)]
    for z in range(NZ):
        local[0].append(pltpu.make_async_copy(fluid_in.at[:, z], fp.at[:, :, z], loc_sem.at[z]))
        local[1].append(pltpu.make_async_copy(count_in.at[z], cn.at[H:H + R, z], loc_sem.at[NZ + z]))
        local[2].append(pltpu.make_async_copy(drag_in.at[z], dr.at[:, z], loc_sem.at[2 * NZ + z]))
        local[3].append(pltpu.make_async_copy(pvel_in.at[:, z], pv.at[:, :, z], loc_sem.at[3 * NZ + z]))
    home = x // C
    barrier = pltpu.get_barrier_semaphore()
    for d in range(1, G * K):
        to = {"gx": lax.rem(x + d // K, G), "gy": lax.rem(k + d % K, K)}
        pl.semaphore_signal(barrier, inc=1, device_id=to, device_id_type=pl.DeviceIdType.MESH)

    for copies in local:
        for copy in copies:
            copy.start()

    line = jnp.zeros((NZ, NY), jnp.float32)

    @pl.when(jnp.logical_not(has_prev))
    def _():
        for which in range(3):
            ub[which, 0] = line

    @pl.when(jnp.logical_not(has_next))
    def _():
        for which in range(3):
            ub[which, R + 1] = line

    fl[0] = line
    fl[R + 1] = line
    edge = jnp.zeros((H, NZ, NY), jnp.float32)

    @pl.when(jnp.logical_not(has_prev))
    def _():
        fr[0] = line
        lv[0, 0:H] = edge
        lv[first, 0:H] = edge

    @pl.when(jnp.logical_not(has_next))
    def _():
        fr[1] = line
        lv[0, H + R:2 * H + R] = edge
        lv[first, H + R:2 * H + R] = edge

    for copy in local[0]:
        copy.wait()
    pl.semaphore_wait(barrier, G * K - 1)

    def count_rows(begin, stop, at):
        return (
            remote(cn.at[H + begin:H + stop], cn.at[H + R + begin:H + R + stop], hal_send.at[at, 0], hal_recv.at[at, 0], prev_id),
            remote(cn.at[H + R - stop:H + R - begin], cn.at[H - stop:H - begin], hal_send.at[at, 1], hal_recv.at[at, 1], next_id),
        )

    near_counts, far_counts = count_rows(0, 1, 0), count_rows(1, H, 1)

    turned = k == K - 1

    def launch(copies):
        @pl.when(jnp.logical_and(turned, has_next))
        def _():
            copies[1].start()

        @pl.when(has_prev)
        def _():
            copies[0].start()

        @pl.when(jnp.logical_and(jnp.logical_not(turned), has_next))
        def _():
            copies[1].start()

    def arrived(copies):
        @pl.when(has_next)
        def _():
            copies[0].wait_recv()

        @pl.when(has_prev)
        def _():
            copies[1].wait_recv()

    def sent(copies):
        @pl.when(has_prev)
        def _():
            copies[0].wait_send()

        @pl.when(has_next)
        def _():
            copies[1].wait_send()

    for copy in local[1]:
        copy.wait()

    launch(near_counts)

    columns = pl.ds(pl.multiple_of(x * W, W), W)
    chip = x // C
    sends = []
    for c in range(C):
        for d in range(K):
            j = lax.rem(k + d + K - chip, K)
            at = (c * K + j) * R
            mine = jnp.logical_and(k * C + c == x, j == k)
            low = (j == 0) if c == 0 else None
            high = (j == K - 1) if c == C - 1 else None
            inner = jnp.bool_(True)
            forms = []
            if low is not None:
                inner = jnp.logical_and(inner, jnp.logical_not(low))
                forms.append((low, 0, 1))
            if high is not None:
                inner = jnp.logical_and(inner, jnp.logical_not(high))
                forms.append((high, 1, 0))
            forms.append((inner, 1, 1))
            for want, before, after in forms:
                n = before + R + after
                src = fp.at[:, pl.ds(at - before, n)]
                dst = ub.at[:, pl.ds(1 - before, n), :, columns]
                far = remote(src, dst, s2_send.at[c * K + d], s2_recv.at[x], {"gx": k * C + c, "gy": j})
                near = pltpu.make_async_copy(src, dst, s2_recv.at[x])
                near_when = jnp.logical_and(want, mine)
                far_when = jnp.logical_and(want, jnp.logical_not(mine))

                @pl.when(near_when)
                def _(near=near):
                    near.start()

                @pl.when(far_when)
                def _(far=far):
                    far.start()

                sends.append((far_when, far))

    for n, (want, row, at, gx, gy) in enumerate((
        (k > 0, 0, R + 1, jnp.maximum(k * C - 1, 0), K - 1),
        (k < K - 1, rows - 1, 0, jnp.minimum((k + 1) * C, G - 1), 0),
    )):
        src = fp.at[:, row:row + 1]
        dst = ub.at[:, at:at + 1, :, columns]
        far = remote(src, dst, row_send.at[n], row_recv.at[x], {"gx": gx, "gy": jnp.int32(gy)})
        near = pltpu.make_async_copy(src, dst, row_recv.at[x])
        mine = jnp.logical_and(gx == x, k == gy)
        far_when = jnp.logical_and(want, jnp.logical_not(mine))

        @pl.when(jnp.logical_and(want, mine))
        def _(near=near):
            near.start()

        @pl.when(far_when)
        def _(far=far):
            far.start()

        sends.append((far_when, far))

    launch(far_counts)
    arrived(near_counts)
    for copies in local[2:]:
        for copy in copies:
            copy.wait()

    lane = lax.broadcasted_iota(jnp.int32, (NZ, NY), 1)
    level = lax.broadcasted_iota(jnp.int32, (NZ, NY), 0)

    def above(v):
        return jnp.where(level < NZ - 1, pltpu.roll(v, NZ - 1, 0), 0.0)

    def below(v):
        return jnp.where(level > 0, pltpu.roll(v, 1, 0), 0.0)

    def right(v):
        return jnp.where(lane < NY - 1, pltpu.roll(v, NY - 1, 1), 0.0)

    def left(v):
        return jnp.where(lane > 0, pltpu.roll(v, 1, 1), 0.0)

    def plane_sum(v):
        return above(v) + below(v) + right(v) + left(v)

    def inside(i):
        at = place * R + i
        return jnp.logical_and(at >= 0, at < G * K * R)

    def voids_row(n, carry):
        v = 1.0 - cn[n].astype(jnp.float32) * particle_volume
        vo[n] = jnp.where(inside(n - H), v, 0.0)
        return carry

    lax.fori_loop(H - 1, R + H + 1, voids_row, 0)

    def weight_row(n, carry):
        v = vo[n]
        ws = 0.5 * (6.0 * v + vo[n - 1] + vo[n + 1] + plane_sum(v))
        total_w[n] = ws
        rh[n] = jnp.where(inside(n - H), 1.0 / ws, 0.0)
        wf[n] = 0.5 * (v + vo[n + 1])
        wr[n] = jnp.where(lane < NY - 1, 0.5 * (v + pltpu.roll(v, NY - 1, 1)), 0.0)
        wa[n] = jnp.where(level < NZ - 1, 0.5 * (v + pltpu.roll(v, NZ - 1, 0)), 0.0)
        return carry

    wf[H - 1] = 0.5 * (vo[H - 1] + vo[H])
    lax.fori_loop(H, R + H, weight_row, 0)

    def weighted(n, p, pa, pb):
        r, a = wr[n], wa[n]
        across = r * pltpu.roll(p, NY - 1, 1) + pltpu.roll(r * p, 1, 1)
        upright = a * pltpu.roll(p, NZ - 1, 0) + pltpu.roll(a * p, 1, 0)
        return (wf[n - 1] * pa + wf[n] * pb) + (across + upright)

    for want, copy in sends:
        @pl.when(want)
        def _(copy=copy):
            copy.wait_send()


    here = {"gx": x, "gy": k}
    slab_low = jnp.logical_and(lax.rem(x, C) == 0, k == 0)
    slab_high = jnp.logical_and(lax.rem(x, C) == C - 1, k == K - 1)
    at_side = jnp.logical_or(slab_low, slab_high)
    extra = jnp.logical_or(jnp.logical_and(slab_low, has_prev), jnp.logical_and(slab_high, has_next))

    def landed(n, sem):
        for sender in range(G):
            spot = pl.ds(sender * W, W)
            remote(fp.at[:, 0:n], ub.at[:, 0:n, :, spot], row_send.at[0], sem.at[sender], here).wait_recv()

    @pl.when(at_side)
    def _():
        landed(R + 1, s2_recv)

    @pl.when(jnp.logical_not(at_side))
    def _():
        landed(R + 2, s2_recv)

    @pl.when(extra)
    def _():
        landed(1, row_recv)

    def pass_on(src_up, dst_up, src_down, dst_down, ssem, rsem, at):
        return (
            remote(src_up, dst_up, ssem.at[0, at], rsem.at[0, at], prev_id),
            remote(src_down, dst_down, ssem.at[1, at], rsem.at[1, at], next_id),
        )

    def flux_rows():
        return pass_on(fl.at[1], fr.at[1], fl.at[R], fr.at[0], b_send, b_recv, 0)

    def level_rows(buf, s, ssem, rsem, at):
        return pass_on(buf.at[H + s], buf.at[H + R + s], buf.at[H + R - 1 - s], buf.at[H - 1 - s], ssem, rsem, at)

    def base_rows(s):
        return level_rows(b, s, b_send, b_recv, s + 1)

    def edge_rows():
        return pass_on(eb.at[0], b.at[H + R], eb.at[1], b.at[H - 1], b_send, b_recv, 1)

    def mid_rows(s):
        return level_rows(lv.at[first], s, p_send, p_recv, s)

    def momentum(i, which):
        v, ws, drag, u = vo[H + i], total_w[H + i], dr[i], ub[which, i + 1]
        diffusion = weighted(H + i, u, ub[which, i], ub[which, i + 2]) - ws * u
        force = drag * pv[which, i]
        return (v * u + (time_step * viscosity) * diffusion + time_step * force) / (v + time_step * drag)

    def finish(i):
        b[H + i] = -(fl[i + 2] - fl[i] + b[H + i]) * rh[H + i]

    def momentum_step(s, carry):
        pair = (s, R - 1 - s)
        for which in range(3):
            values = [momentum(i, which) for i in pair]
            for i, value in zip(pair, values):
                pred[which, i] = value
            flux = [vo[H + i] * value for i, value in zip(pair, values)]
            if which == 0:
                for i, f in zip(pair, flux):
                    fl[i + 1] = f

                @pl.when(s == 0)
                def _():
                    launch(flux_rows())

            elif which == 1:
                part_source = [right(f) - left(f) for f in flux]
            else:
                for i, f, part in zip(pair, flux, part_source):
                    b[H + i] = part + (above(f) - below(f))

        @pl.when(s > 0)
        def _():
            finish(s - 1)
            finish(R - s)

            @pl.when(s == 1)
            def _():
                eb[0] = b[H]
                eb[1] = b[H + R - 1]
                launch(edge_rows())

            @pl.when(jnp.logical_and(s > 1, s <= H))
            def _():
                launch(base_rows(s - 1))

        return carry

    half = R // 2
    lax.fori_loop(0, half, momentum_step, 0)
    finish(half - 1)
    finish(R - half)
    if half <= H:
        launch(base_rows(half - 1))

    arrived(far_counts)
    lax.fori_loop(0, H - 1, voids_row, 0)
    lax.fori_loop(R + H + 1, R + 2 * H, voids_row, 0)
    wf[0] = 0.5 * (vo[0] + vo[1])
    lax.fori_loop(1, H, weight_row, 0)
    lax.fori_loop(R + H, R + 2 * H - 1, weight_row, 0)

    def sweep_pair(l, lo):
        hi = 2 * H + R - 1 - lo
        values = [
            weighted(n, lv[l - 1, n], lv[l - 1, n - 1], lv[l - 1, n + 1]) * rh[n] + b[n] for n in (lo, hi)
        ]
        lv[l, lo] = values[0]
        lv[l, hi] = values[1]

    def diagonal(j, start, stop):
        def level(l, carry):
            sweep_pair(l, l + (H - j))
            return carry

        lax.fori_loop(start, stop, level, 0)

    def rows_of(l, start, stop):
        def row(lo, carry):
            sweep_pair(l, lo)
            return carry

        lax.fori_loop(H + start, H + stop, row, 0)

    for j in range(2 - half, H + 1):
        if j == 0:
            arrived(flux_rows())
            b[H] = b[H] + fr[0] * rh[H]
            b[H + R - 1] = b[H + R - 1] - fr[1] * rh[H + R - 1]
        elif j > 0:
            arrived(base_rows(j - 1))
            if j == 1:
                b[H - 1] = b[H - 1] - fl[1] * rh[H - 1]
                b[H + R] = b[H + R] + fl[R] * rh[H + R]
        stop = min(last_level, j + half - 1) + 1
        diagonal(j, 1, min(stop, first + 1))
        if j > 0:
            launch(mid_rows(first - j))
        if stop > first + 1:
            diagonal(j, first + 1, stop)

    depth = last_level - first
    for s in range(first - 1, 0, -1):
        arrived(mid_rows(s))
    rows_of(first + 1, -depth, 1 - depth)
    arrived(mid_rows(0))
    for l in range(first + 1, last_level + 1):
        low = l - last_level - 1 + (1 if l in (first + 1, last_level) else 0)
        rows_of(l, low, l - H)

    def partner(d, back=False):
        if K & (K - 1) == 0:
            return chip ^ d
        return lax.rem(chip + (K - d if back else d), K)

    outs = []
    for d in range(K):
        for c in range(C):
            target = partner(d) * C + lax.rem(x + c, C)
            src = pf.at[H:H + R, :, pl.ds(pl.multiple_of(target * W, W), W)]
            if d == c == 0:
                pltpu.make_async_copy(src, rl.at[x], out_recv.at[x]).start()
            else:
                outs.append(remote(src, rl.at[x], out_send.at[d * C + c], out_recv.at[x], {"gx": target, "gy": k}))
                outs[-1].start()

    rises = []

    def rise(d):
        to = partner(d, back=True)
        for c in range(C):
            slot = to * C + c
            remote(pf.at[H:H + R, :, 0:W], rl.at[slot], out_send.at[0], out_recv.at[slot], here).wait_recv()
        src = rl.at[pl.ds(to * C, C)]
        far = remote(src, press_out.at[:, k], up_send.at[d], up_recv.at[k], {"gx": x, "gy": to})
        near = pltpu.make_async_copy(src, press_out.at[:, k], up_recv.at[k])

        @pl.when(to != k)
        def _():
            far.start()

        @pl.when(to == k)
        def _():
            near.start()

        rises.append((to, far))

    for d in range(K):
        rise(d)

    rows_of(last_level, -1, 0)

    def slope_row(i, carry):
        n = H + i
        p = pf[n]
        g0 = 0.5 * (pf[n + 1] - pf[n - 1])
        g1 = 0.5 * (right(p) - left(p))
        g2 = 0.5 * (above(p) - below(p))
        for which, g in enumerate((g0, g1, g2)):
            gr[which, i] = g
            pred[which, i] = pred[which, i] - time_step * g
        return carry

    lax.fori_loop(0, R, slope_row, 0)
    written = []
    for z in range(NZ):
        written.append(pltpu.make_async_copy(gr.at[:, :, z], grad_out.at[:, z], loc_sem.at[z]))
        written.append(pltpu.make_async_copy(pred.at[:, :, z], vel_out.at[:, z], loc_sem.at[NZ + z]))
    for copy in written:
        copy.start()

    for copies in [near_counts, far_counts, flux_rows(), edge_rows()] + [base_rows(i) for i in range(1, H)] + [mid_rows(i) for i in range(first)]:
        sent(copies)

    for copy in outs:
        copy.wait_send()

    for to, far in rises:
        @pl.when(to != k)
        def _(far=far):
            far.wait_send()

    for j in range(K):
        remote(rl.at[0:C], press_out.at[:, j], up_send.at[0], up_recv.at[j], here).wait_recv()
    for copy in written:
        copy.wait()


def settle(press_in, vel_in, grad_in, press_out, vel_out, grad_out, press, vel, grad, in_sem, out_sem):
    C, K, R, NZ, W = press.shape
    steps = []

    def step(src, held, stores):
        at = len(steps)
        steps.append((pltpu.make_async_copy(src, held, in_sem.at[at]), stores))

    step(press_in, press, [pltpu.make_async_copy(press.at[:, :, :, z], press_out.at[z], out_sem.at[2 * vel.shape[0] + z]) for z in range(NZ)])

    for n, (src, held, dst) in enumerate(((vel_in, vel, vel_out), (grad_in, grad, grad_out))):
        for i in range(held.shape[0]):
            stores = [pltpu.make_async_copy(held.at[i], dst.at[i], out_sem.at[n * held.shape[0] + i])]
            step(src.at[i], held.at[i], stores)

    for load, _ in steps:
        load.start()
    for load, stores in steps:
        load.wait()
        for store in stores:
            store.start()
    for _, stores in steps:
        for store in stores:
            store.wait()


def shards(K, G, particle_count, drag_coeff, particle_velocity, fluid_velocity):
    NZ, R, NY = particle_count.shape
    rows, W = fluid_velocity.shape[2:]
    C = G // K
    H = max(ROUNDS)
    f32 = jnp.float32

    dma = pltpu.SemaphoreType.DMA
    pad = (R + 2 * H, NZ, NY)
    scratch = [
        pltpu.VMEM((3, rows, NZ, W), f32),
        pltpu.VMEM((3, R + 2, NZ, NY), f32),
        pltpu.VMEM(pad, jnp.int32),
        pltpu.VMEM((R, NZ, NY), f32),
        pltpu.VMEM((3, R, NZ, NY), f32),
        *[pltpu.VMEM(pad, f32) for _ in range(6)],
        pltpu.VMEM((3, R, NZ, NY), f32),
        pltpu.VMEM((3, R, NZ, NY), f32),
        pltpu.VMEM((R + 2, NZ, NY), f32),
        pltpu.VMEM((2, NZ, NY), f32),
        pltpu.VMEM((2, NZ, NY), f32),
        pltpu.VMEM((SWEEPS,) + pad, f32),
        pltpu.VMEM((G, R, NZ, W), f32),
        dma((4 * NZ,)), dma((2,)), dma((G,)),
        dma((K * C,)), dma((G,)),
        dma((2, 2)), dma((2, 2)), dma((2, H + 1)), dma((2, H + 1)), dma((2, H)), dma((2, H)), dma((G,)), dma((G,)), dma((K,)), dma((K,)),
    ]
    anywhere = pl.BlockSpec(memory_space=pl.ANY)
    pressure, velocity, slopes = pl.pallas_call(
        functools.partial(kernel, K, G, R, NZ, NY, W),
        out_shape=(
            jax.ShapeDtypeStruct((C, K, R, NZ, W), f32),
            jax.ShapeDtypeStruct((3, NZ, R, NY), f32),
            jax.ShapeDtypeStruct((3, NZ, R, NY), f32),
        ),
        in_specs=[anywhere] * 4,
        out_specs=(anywhere, anywhere, anywhere),
        scratch_shapes=scratch,
        compiler_params=pltpu.CompilerParams(collective_id=0, has_side_effects=True, vmem_limit_bytes=67043328),
    )(particle_count, drag_coeff, particle_velocity, fluid_velocity)
    first = [pressure, velocity, slopes]
    pressure, velocity, slopes = pl.pallas_call(
        settle,
        out_shape=[
            jax.ShapeDtypeStruct((NZ, C, K, R, W), f32),
            jax.ShapeDtypeStruct(velocity.shape, f32),
            jax.ShapeDtypeStruct(slopes.shape, f32),
        ],
        in_specs=[anywhere] * 3,
        out_specs=[anywhere] * 3,
        scratch_shapes=[*[pltpu.VMEM(v.shape, f32) for v in first], dma((1 + 2 * 3,)), dma((NZ + 2 * 3,))],
        compiler_params=pltpu.CompilerParams(vmem_limit_bytes=67043328),
    )(*first)
    return pressure.reshape(NZ, rows, W), velocity, slopes


def solution(mesh):
    placed = (
        P(None, ("gx", "gy"), None),
        P(None, ("gx", "gy"), None),
        P(None, None, ("gx", "gy"), None),
        P(None, None, "gy", "gx"),
    )
    return jax.shard_map(
        functools.partial(shards, mesh.shape["gy"], mesh.shape["gx"]),
        mesh=mesh,
        in_specs=placed,
        out_specs=(
            P(None, "gy", "gx"),
            P(None, None, ("gx", "gy"), None),
            P(None, None, ("gx", "gy"), None),
        ),
        check_vma=False,
    )
```

```python
import functools

import jax
import jax.numpy as jnp
from jax import lax
from jax.experimental import pallas as pl
from jax.experimental.pallas import tpu as pltpu
from jax.sharding import PartitionSpec as P

SWEEPS = 8
ROUNDS = (4, 4)

particle_volume = 0.05
time_step = 0.5
viscosity = 0.1


def kernel(
    K, G, R, NZ, NY, W,
    count_in, drag_in, pvel_in, fluid_in,
    press_out, vel_out, grad_out,
    fp, ub, cn, dr, pv, vo, total_w, wf, wr, wa, rh, pred, gr, fl, fr, eb, lv, rl,
    loc_sem, row_send, row_recv, s2_send, s2_recv,
    hal_send, hal_recv, b_send, b_recv, p_send, p_recv, out_send, out_recv, up_send, up_recv,
):
    H = max(ROUNDS)
    first, last_level = ROUNDS[0], SWEEPS - 1
    b, pf = lv.at[0], lv.at[last_level]
    C = G // K
    B = C * K
    x = lax.axis_index("gx")
    k = lax.axis_index("gy")
    place = x * K + k
    has_prev = place > 0
    has_next = place < G * K - 1
    prev_id = {"gx": jnp.where(k > 0, x, jnp.maximum(x - 1, 0)), "gy": lax.rem(k + K - 1, K)}
    next_id = {"gx": jnp.where(k < K - 1, x, jnp.minimum(x + 1, G - 1)), "gy": lax.rem(k + 1, K)}

    def remote(src, dst, ssem, rsem, to):
        return pltpu.make_async_remote_copy(
            src_ref=src, dst_ref=dst, send_sem=ssem, recv_sem=rsem, device_id=to, device_id_type=pl.DeviceIdType.MESH
        )

    rows = R * B

    local = [[] for _ in range(4)]
    for z in range(NZ):
        local[0].append(pltpu.make_async_copy(fluid_in.at[:, z], fp.at[:, :, z], loc_sem.at[z]))
        local[1].append(pltpu.make_async_copy(count_in.at[z], cn.at[H:H + R, z], loc_sem.at[NZ + z]))
        local[2].append(pltpu.make_async_copy(drag_in.at[z], dr.at[:, z], loc_sem.at[2 * NZ + z]))
        local[3].append(pltpu.make_async_copy(pvel_in.at[:, z], pv.at[:, :, z], loc_sem.at[3 * NZ + z]))
    home = x // C
    barrier = pltpu.get_barrier_semaphore()
    for d in range(1, G * K):
        to = {"gx": lax.rem(x + d // K, G), "gy": lax.rem(k + d % K, K)}
        pl.semaphore_signal(barrier, inc=1, device_id=to, device_id_type=pl.DeviceIdType.MESH)

    for copies in local:
        for copy in copies:
            copy.start()

    line = jnp.zeros((NZ, NY), jnp.float32)

    @pl.when(jnp.logical_not(has_prev))
    def _():
        for which in range(3):
            ub[which, 0] = line

    @pl.when(jnp.logical_not(has_next))
    def _():
        for which in range(3):
            ub[which, R + 1] = line

    fl[0] = line
    fl[R + 1] = line
    edge = jnp.zeros((H, NZ, NY), jnp.float32)

    @pl.when(jnp.logical_not(has_prev))
    def _():
        fr[0] = line
        for l in (0, first):
            lv[l, 0:H] = edge
            lv[l + 1, 1] = line

    @pl.when(jnp.logical_not(has_next))
    def _():
        fr[1] = line
        for l in (0, first):
            lv[l, H + R:2 * H + R] = edge
            lv[l + 1, 2 * H + R - 2] = line

    for copy in local[0]:
        copy.wait()
    pl.semaphore_wait(barrier, G * K - 1)

    def count_rows(begin, stop, at):
        return (
            remote(cn.at[H + begin:H + stop], cn.at[H + R + begin:H + R + stop], hal_send.at[at, 0], hal_recv.at[at, 0], prev_id),
            remote(cn.at[H + R - stop:H + R - begin], cn.at[H - stop:H - begin], hal_send.at[at, 1], hal_recv.at[at, 1], next_id),
        )

    near_counts, far_counts = count_rows(0, 1, 0), count_rows(1, H - 1, 1)

    turned = k == K - 1
    wraps = (jnp.logical_and(k == 0, has_prev), jnp.logical_and(turned, has_next))
    plain = (jnp.logical_and(k > 0, has_prev), jnp.logical_and(jnp.logical_not(turned), has_next))

    def launch(copies, only=None):
        for group in ((wraps, plain) if only is None else (only,)):
            for when, copy in zip(group, copies):
                @pl.when(when)
                def _(copy=copy):
                    copy.start()

    def arrived(copies):
        @pl.when(has_next)
        def _():
            copies[0].wait_recv()

        @pl.when(has_prev)
        def _():
            copies[1].wait_recv()

    def sent(copies):
        @pl.when(has_prev)
        def _():
            copies[0].wait_send()

        @pl.when(has_next)
        def _():
            copies[1].wait_send()

    for copy in local[1]:
        copy.wait()

    launch(near_counts)

    columns = pl.ds(pl.multiple_of(x * W, W), W)
    chip = x // C
    sends = []
    for c in range(C):
        for d in range(K):
            j = lax.rem(k + d + K - chip, K)
            at = (c * K + j) * R
            mine = jnp.logical_and(k * C + c == x, j == k)
            low = (j == 0) if c == 0 else None
            high = (j == K - 1) if c == C - 1 else None
            inner = jnp.bool_(True)
            forms = []
            if low is not None:
                inner = jnp.logical_and(inner, jnp.logical_not(low))
                forms.append((low, 0, 1))
            if high is not None:
                inner = jnp.logical_and(inner, jnp.logical_not(high))
                forms.append((high, 1, 0))
            forms.append((inner, 1, 1))
            for want, before, after in forms:
                n = before + R + after
                src = fp.at[:, pl.ds(at - before, n)]
                dst = ub.at[:, pl.ds(1 - before, n), :, columns]
                far = remote(src, dst, s2_send.at[c * K + d], s2_recv.at[x], {"gx": k * C + c, "gy": j})
                near = pltpu.make_async_copy(src, dst, s2_recv.at[x])
                near_when = jnp.logical_and(want, mine)
                far_when = jnp.logical_and(want, jnp.logical_not(mine))

                @pl.when(near_when)
                def _(near=near):
                    near.start()

                @pl.when(far_when)
                def _(far=far):
                    far.start()

                sends.append((far_when, far))

    for n, (want, row, at, gx, gy) in enumerate((
        (k > 0, 0, R + 1, jnp.maximum(k * C - 1, 0), K - 1),
        (k < K - 1, rows - 1, 0, jnp.minimum((k + 1) * C, G - 1), 0),
    )):
        src = fp.at[:, row:row + 1]
        dst = ub.at[:, at:at + 1, :, columns]
        far = remote(src, dst, row_send.at[n], row_recv.at[x], {"gx": gx, "gy": jnp.int32(gy)})
        near = pltpu.make_async_copy(src, dst, row_recv.at[x])
        mine = jnp.logical_and(gx == x, k == gy)
        far_when = jnp.logical_and(want, jnp.logical_not(mine))

        @pl.when(jnp.logical_and(want, mine))
        def _(near=near):
            near.start()

        @pl.when(far_when)
        def _(far=far):
            far.start()

        sends.append((far_when, far))

    launch(far_counts)
    arrived(near_counts)
    for copies in local[2:]:
        for copy in copies:
            copy.wait()

    lane = lax.broadcasted_iota(jnp.int32, (NZ, NY), 1)
    level = lax.broadcasted_iota(jnp.int32, (NZ, NY), 0)

    def above(v):
        return jnp.where(level < NZ - 1, pltpu.roll(v, NZ - 1, 0), 0.0)

    def below(v):
        return jnp.where(level > 0, pltpu.roll(v, 1, 0), 0.0)

    def right(v):
        return jnp.where(lane < NY - 1, pltpu.roll(v, NY - 1, 1), 0.0)

    def left(v):
        return jnp.where(lane > 0, pltpu.roll(v, 1, 1), 0.0)

    def plane_sum(v):
        return above(v) + below(v) + right(v) + left(v)

    def inside(i):
        at = place * R + i
        return jnp.logical_and(at >= 0, at < G * K * R)

    def voids_row(n, carry):
        v = 1.0 - cn[n].astype(jnp.float32) * particle_volume
        vo[n] = jnp.where(inside(n - H), v, 0.0)
        return carry

    lax.fori_loop(H - 1, R + H + 1, voids_row, 0)

    def weight_row(n, carry):
        v = vo[n]
        ws = 0.5 * (6.0 * v + vo[n - 1] + vo[n + 1] + plane_sum(v))
        total_w[n] = ws
        rh[n] = jnp.where(inside(n - H), 1.0 / ws, 0.0)
        wf[n] = 0.5 * (v + vo[n + 1])
        wr[n] = jnp.where(lane < NY - 1, 0.5 * (v + pltpu.roll(v, NY - 1, 1)), 0.0)
        wa[n] = jnp.where(level < NZ - 1, 0.5 * (v + pltpu.roll(v, NZ - 1, 0)), 0.0)
        return carry

    wf[H - 1] = 0.5 * (vo[H - 1] + vo[H])
    lax.fori_loop(H, R + H, weight_row, 0)

    def weighted(n, p, pa, pb):
        r, a = wr[n], wa[n]
        across = r * pltpu.roll(p, NY - 1, 1) + pltpu.roll(r * p, 1, 1)
        upright = a * pltpu.roll(p, NZ - 1, 0) + pltpu.roll(a * p, 1, 0)
        return (wf[n - 1] * pa + wf[n] * pb) + (across + upright)

    for want, copy in sends:
        @pl.when(want)
        def _(copy=copy):
            copy.wait_send()


    here = {"gx": x, "gy": k}
    slab_low = jnp.logical_and(lax.rem(x, C) == 0, k == 0)
    slab_high = jnp.logical_and(lax.rem(x, C) == C - 1, k == K - 1)
    at_side = jnp.logical_or(slab_low, slab_high)
    extra = jnp.logical_or(jnp.logical_and(slab_low, has_prev), jnp.logical_and(slab_high, has_next))

    def landed(n, sem):
        for sender in range(G):
            spot = pl.ds(sender * W, W)
            remote(fp.at[:, 0:n], ub.at[:, 0:n, :, spot], row_send.at[0], sem.at[sender], here).wait_recv()

    @pl.when(at_side)
    def _():
        landed(R + 1, s2_recv)

    @pl.when(jnp.logical_not(at_side))
    def _():
        landed(R + 2, s2_recv)

    @pl.when(extra)
    def _():
        landed(1, row_recv)

    def pass_on(src_up, dst_up, src_down, dst_down, ssem, rsem, at):
        return (
            remote(src_up, dst_up, ssem.at[0, at], rsem.at[0, at], prev_id),
            remote(src_down, dst_down, ssem.at[1, at], rsem.at[1, at], next_id),
        )

    def flux_rows():
        return pass_on(fl.at[1], fr.at[1], fl.at[R], fr.at[0], b_send, b_recv, 0)

    def level_rows(buf, s, ssem, rsem, at):
        return pass_on(buf.at[H + s], buf.at[H + R + s], buf.at[H + R - 1 - s], buf.at[H - 1 - s], ssem, rsem, at)

    def base_rows(s):
        return level_rows(b, s, b_send, b_recv, s + 1)

    def base_last():
        return level_rows(lv.at[1], H - 2, b_send, b_recv, H)

    def edge_rows():
        return pass_on(eb.at[0], b.at[H + R], eb.at[1], b.at[H - 1], b_send, b_recv, 1)

    def mid_rows(s):
        return level_rows(lv.at[first], s, p_send, p_recv, s)

    def mid_last():
        return level_rows(lv.at[first + 1], H - 2, p_send, p_recv, H - 1)

    def momentum(i, which):
        v, ws, drag, u = vo[H + i], total_w[H + i], dr[i], ub[which, i + 1]
        diffusion = weighted(H + i, u, ub[which, i], ub[which, i + 2]) - ws * u
        force = drag * pv[which, i]
        return (v * u + (time_step * viscosity) * diffusion + time_step * force) / (v + time_step * drag)

    def finish(i):
        b[H + i] = -(fl[i + 2] - fl[i] + b[H + i]) * rh[H + i]

    def momentum_step(s, carry):
        pair = (s, R - 1 - s)
        for which in range(3):
            values = [momentum(i, which) for i in pair]
            for i, value in zip(pair, values):
                pred[which, i] = value
            flux = [vo[H + i] * value for i, value in zip(pair, values)]
            if which == 0:
                for i, f in zip(pair, flux):
                    fl[i + 1] = f

                @pl.when(s == 0)
                def _():
                    launch(flux_rows())

            elif which == 1:
                part_source = [right(f) - left(f) for f in flux]
            else:
                for i, f, part in zip(pair, flux, part_source):
                    b[H + i] = part + (above(f) - below(f))

        @pl.when(s > 0)
        def _():
            finish(s - 1)
            finish(R - s)

            @pl.when(s == 1)
            def _():
                eb[0] = b[H]
                eb[1] = b[H + R - 1]
                launch(edge_rows())

            @pl.when(jnp.logical_and(s > 1, s < H))
            def _():
                launch(base_rows(s - 1))

        return carry

    half = R // 2
    lax.fori_loop(0, half, momentum_step, 0)
    finish(half - 1)
    finish(R - half)

    def sweep_pair(l, lo):
        hi = 2 * H + R - 1 - lo
        values = [
            weighted(n, lv[l - 1, n], lv[l - 1, n - 1], lv[l - 1, n + 1]) * rh[n] + b[n] for n in (lo, hi)
        ]
        lv[l, lo] = values[0]
        lv[l, hi] = values[1]

    def diagonal(j, start, stop):
        def level(l, carry):
            sweep_pair(l, l + (H - j))
            return carry

        lax.fori_loop(start, stop, level, 0)

    def rows_of(l, start, stop):
        def row(lo, carry):
            sweep_pair(l, lo)
            return carry

        lax.fori_loop(H + start, H + stop, row, 0)

    for j in range(2 - half, H + 1):
        if j == 0:
            arrived(far_counts)
            lax.fori_loop(1, H - 1, voids_row, 0)
            lax.fori_loop(R + H + 1, R + 2 * H - 1, voids_row, 0)
            wf[1] = 0.5 * (vo[1] + vo[2])
            lax.fori_loop(2, H, weight_row, 0)
            lax.fori_loop(R + H, R + 2 * H - 2, weight_row, 0)
            arrived(flux_rows())
            b[H] = b[H] + fr[0] * rh[H]
            b[H + R - 1] = b[H + R - 1] - fr[1] * rh[H + R - 1]
        elif j == H:
            arrived(base_last())
        elif j > 0:
            arrived(base_rows(j - 1))
            if j == 1:
                b[H - 1] = b[H - 1] - fl[1] * rh[H - 1]
                b[H + R] = b[H + R] + fl[R] * rh[H + R]
        stop = min(last_level, j + half - 1) + 1
        diagonal(j, 2 if j == H else 1, min(stop, first + 1))
        if j == 3 - H:
            launch(base_last())
        if j > 1:
            launch(mid_rows(first - j))
        if stop > first + 1:
            diagonal(j, first + 1, stop)
        if j == first + 3 - H:
            launch(mid_last())

    for s in range(first - 2, 0, -1):
        arrived(mid_rows(s))
    arrived(mid_last())
    arrived(mid_rows(0))
    for l in range(first + 1, last_level + 1):
        low = l - last_level - 1 + (1 if l in (first + 1, last_level) else 0)
        rows_of(l, low, l - H)

    def partner(d, back=False):
        if K & (K - 1) == 0:
            return chip ^ d
        return lax.rem(chip + (K - d if back else d), K)

    outs = []
    for d in range(K):
        for c in range(C):
            target = partner(d) * C + lax.rem(x + c, C)
            src = pf.at[H:H + R, :, pl.ds(pl.multiple_of(target * W, W), W)]
            if d == c == 0:
                pltpu.make_async_copy(src, rl.at[x], out_recv.at[x]).start()
            else:
                outs.append(remote(src, rl.at[x], out_send.at[d * C + c], out_recv.at[x], {"gx": target, "gy": k}))
                outs[-1].start()

    rises = []

    def rise(d):
        to = partner(d, back=True)
        for c in range(C):
            slot = to * C + c
            remote(pf.at[H:H + R, :, 0:W], rl.at[slot], out_send.at[0], out_recv.at[slot], here).wait_recv()
        src = rl.at[pl.ds(to * C, C)]
        far = remote(src, press_out.at[:, k], up_send.at[d], up_recv.at[k], {"gx": x, "gy": to})
        near = pltpu.make_async_copy(src, press_out.at[:, k], up_recv.at[k])

        @pl.when(to != k)
        def _():
            far.start()

        @pl.when(to == k)
        def _():
            near.start()

        rises.append((to, far))

    for d in range(K):
        rise(d)

    rows_of(last_level, -1, 0)

    def slope_row(i, carry):
        n = H + i
        p = pf[n]
        g0 = 0.5 * (pf[n + 1] - pf[n - 1])
        g1 = 0.5 * (right(p) - left(p))
        g2 = 0.5 * (above(p) - below(p))
        for which, g in enumerate((g0, g1, g2)):
            gr[which, i] = g
            pred[which, i] = pred[which, i] - time_step * g
        return carry

    lax.fori_loop(0, R, slope_row, 0)
    written = []
    for z in range(NZ):
        written.append(pltpu.make_async_copy(gr.at[:, :, z], grad_out.at[:, z], loc_sem.at[z]))
        written.append(pltpu.make_async_copy(pred.at[:, :, z], vel_out.at[:, z], loc_sem.at[NZ + z]))
    for copy in written:
        copy.start()

    for copies in [near_counts, far_counts, flux_rows(), edge_rows()] + [base_rows(i) for i in range(1, H - 1)] + [base_last(), mid_last()] + [mid_rows(i) for i in range(first - 1)]:
        sent(copies)

    for copy in outs:
        copy.wait_send()

    for to, far in rises:
        @pl.when(to != k)
        def _(far=far):
            far.wait_send()

    for j in range(K):
        remote(rl.at[0:C], press_out.at[:, j], up_send.at[0], up_recv.at[j], here).wait_recv()
    for copy in written:
        copy.wait()


def settle(press_in, vel_in, grad_in, press_out, vel_out, grad_out, press, vel, grad, in_sem, out_sem):
    C, K, R, NZ, W = press.shape
    steps = []

    def step(src, held, stores):
        at = len(steps)
        steps.append((pltpu.make_async_copy(src, held, in_sem.at[at]), stores))

    step(press_in, press, [pltpu.make_async_copy(press.at[:, :, :, z], press_out.at[z], out_sem.at[2 * vel.shape[0] + z]) for z in range(NZ)])

    for n, (src, held, dst) in enumerate(((vel_in, vel, vel_out), (grad_in, grad, grad_out))):
        for i in range(held.shape[0]):
            stores = [pltpu.make_async_copy(held.at[i], dst.at[i], out_sem.at[n * held.shape[0] + i])]
            step(src.at[i], held.at[i], stores)

    for load, _ in steps:
        load.start()
    for load, stores in steps:
        load.wait()
        for store in stores:
            store.start()
    for _, stores in steps:
        for store in stores:
            store.wait()


def shards(K, G, particle_count, drag_coeff, particle_velocity, fluid_velocity):
    NZ, R, NY = particle_count.shape
    rows, W = fluid_velocity.shape[2:]
    C = G // K
    H = max(ROUNDS)
    f32 = jnp.float32

    dma = pltpu.SemaphoreType.DMA
    pad = (R + 2 * H, NZ, NY)
    scratch = [
        pltpu.VMEM((3, rows, NZ, W), f32),
        pltpu.VMEM((3, R + 2, NZ, NY), f32),
        pltpu.VMEM(pad, jnp.int32),
        pltpu.VMEM((R, NZ, NY), f32),
        pltpu.VMEM((3, R, NZ, NY), f32),
        *[pltpu.VMEM(pad, f32) for _ in range(6)],
        pltpu.VMEM((3, R, NZ, NY), f32),
        pltpu.VMEM((3, R, NZ, NY), f32),
        pltpu.VMEM((R + 2, NZ, NY), f32),
        pltpu.VMEM((2, NZ, NY), f32),
        pltpu.VMEM((2, NZ, NY), f32),
        pltpu.VMEM((SWEEPS,) + pad, f32),
        pltpu.VMEM((G, R, NZ, W), f32),
        dma((4 * NZ,)), dma((2,)), dma((G,)),
        dma((K * C,)), dma((G,)),
        dma((2, 2)), dma((2, 2)), dma((2, H + 1)), dma((2, H + 1)), dma((2, H)), dma((2, H)), dma((G,)), dma((G,)), dma((K,)), dma((K,)),
    ]
    anywhere = pl.BlockSpec(memory_space=pl.ANY)
    pressure, velocity, slopes = pl.pallas_call(
        functools.partial(kernel, K, G, R, NZ, NY, W),
        out_shape=(
            jax.ShapeDtypeStruct((C, K, R, NZ, W), f32),
            jax.ShapeDtypeStruct((3, NZ, R, NY), f32),
            jax.ShapeDtypeStruct((3, NZ, R, NY), f32),
        ),
        in_specs=[anywhere] * 4,
        out_specs=(anywhere, anywhere, anywhere),
        scratch_shapes=scratch,
        compiler_params=pltpu.CompilerParams(collective_id=0, has_side_effects=True, vmem_limit_bytes=67043328),
    )(particle_count, drag_coeff, particle_velocity, fluid_velocity)
    first = [pressure, velocity, slopes]
    pressure, velocity, slopes = pl.pallas_call(
        settle,
        out_shape=[
            jax.ShapeDtypeStruct((NZ, C, K, R, W), f32),
            jax.ShapeDtypeStruct(velocity.shape, f32),
            jax.ShapeDtypeStruct(slopes.shape, f32),
        ],
        in_specs=[anywhere] * 3,
        out_specs=[anywhere] * 3,
        scratch_shapes=[*[pltpu.VMEM(v.shape, f32) for v in first], dma((1 + 2 * 3,)), dma((NZ + 2 * 3,))],
        compiler_params=pltpu.CompilerParams(vmem_limit_bytes=67043328),
    )(*first)
    return pressure.reshape(NZ, rows, W), velocity, slopes


def solution(mesh):
    placed = (
        P(None, ("gx", "gy"), None),
        P(None, ("gx", "gy"), None),
        P(None, None, ("gx", "gy"), None),
        P(None, None, "gy", "gx"),
    )
    return jax.shard_map(
        functools.partial(shards, mesh.shape["gy"], mesh.shape["gx"]),
        mesh=mesh,
        in_specs=placed,
        out_specs=(
            P(None, "gy", "gx"),
            P(None, None, ("gx", "gy"), None),
            P(None, None, ("gx", "gy"), None),
        ),
        check_vma=False,
    )
```

```python
import functools

import jax
import jax.numpy as jnp
from jax import lax
from jax.experimental import pallas as pl
from jax.experimental.pallas import tpu as pltpu
from jax.sharding import PartitionSpec as P

SWEEPS = 8
ROUNDS = (4, 4)

particle_volume = 0.05
time_step = 0.5
viscosity = 0.1


def kernel(
    K, G, R, NZ, NY, W,
    count_in, drag_in, pvel_in, fluid_in,
    press_out, vel_out, grad_out,
    fp, ub, cn, dr, pv, vo, total_w, wf, wr, wa, rh, pred, gr, fl, fr, eb, lv, rl,
    loc_sem, row_send, row_recv, s2_send, s2_recv,
    hal_send, hal_recv, b_send, b_recv, p_send, p_recv, out_send, out_recv, up_send, up_recv,
):
    H = max(ROUNDS)
    first, last_level = ROUNDS[0], SWEEPS - 1
    b, pf = lv.at[0], lv.at[last_level]
    C = G // K
    B = C * K
    x = lax.axis_index("gx")
    k = lax.axis_index("gy")
    place = x * K + k
    has_prev = place > 0
    has_next = place < G * K - 1
    prev_id = {"gx": jnp.where(k > 0, x, jnp.maximum(x - 1, 0)), "gy": lax.rem(k + K - 1, K)}
    next_id = {"gx": jnp.where(k < K - 1, x, jnp.minimum(x + 1, G - 1)), "gy": lax.rem(k + 1, K)}

    def remote(src, dst, ssem, rsem, to):
        return pltpu.make_async_remote_copy(
            src_ref=src, dst_ref=dst, send_sem=ssem, recv_sem=rsem, device_id=to, device_id_type=pl.DeviceIdType.MESH
        )

    rows = R * B

    local = [[] for _ in range(4)]
    for z in range(NZ):
        local[0].append(pltpu.make_async_copy(fluid_in.at[:, z], fp.at[:, :, z], loc_sem.at[z]))
        local[1].append(pltpu.make_async_copy(count_in.at[z], cn.at[H:H + R, z], loc_sem.at[NZ + z]))
        local[2].append(pltpu.make_async_copy(drag_in.at[z], dr.at[:, z], loc_sem.at[2 * NZ + z]))
        local[3].append(pltpu.make_async_copy(pvel_in.at[:, z], pv.at[:, :, z], loc_sem.at[3 * NZ + z]))
    home = x // C
    barrier = pltpu.get_barrier_semaphore()
    for d in range(1, G * K):
        to = {"gx": lax.rem(x + d // K, G), "gy": lax.rem(k + d % K, K)}
        pl.semaphore_signal(barrier, inc=1, device_id=to, device_id_type=pl.DeviceIdType.MESH)

    for copies in local:
        for copy in copies:
            copy.start()

    line = jnp.zeros((NZ, NY), jnp.float32)

    @pl.when(jnp.logical_not(has_prev))
    def _():
        for which in range(3):
            ub[which, 0] = line

    @pl.when(jnp.logical_not(has_next))
    def _():
        for which in range(3):
            ub[which, R + 1] = line

    fl[0] = line
    fl[R + 1] = line
    edge = jnp.zeros((H, NZ, NY), jnp.float32)

    @pl.when(jnp.logical_not(has_prev))
    def _():
        fr[0] = line
        for l in (0, first):
            lv[l, 0:H] = edge
            lv[l + 1, 1] = line

    @pl.when(jnp.logical_not(has_next))
    def _():
        fr[1] = line
        for l in (0, first):
            lv[l, H + R:2 * H + R] = edge
            lv[l + 1, 2 * H + R - 2] = line

    for copy in local[0]:
        copy.wait()
    pl.semaphore_wait(barrier, G * K - 1)

    def count_rows(begin, stop, at):
        return (
            remote(cn.at[H + begin:H + stop], cn.at[H + R + begin:H + R + stop], hal_send.at[at, 0], hal_recv.at[at, 0], prev_id),
            remote(cn.at[H + R - stop:H + R - begin], cn.at[H - stop:H - begin], hal_send.at[at, 1], hal_recv.at[at, 1], next_id),
        )

    near_counts, far_counts = count_rows(0, 1, 0), count_rows(1, H - 1, 1)

    turned = k == K - 1
    wraps = (jnp.logical_and(k == 0, has_prev), jnp.logical_and(turned, has_next))
    plain = (jnp.logical_and(k > 0, has_prev), jnp.logical_and(jnp.logical_not(turned), has_next))

    def launch(copies, only=None):
        for group in ((wraps, plain) if only is None else (only,)):
            for when, copy in zip(group, copies):
                @pl.when(when)
                def _(copy=copy):
                    copy.start()

    def arrived(copies):
        @pl.when(has_next)
        def _():
            copies[0].wait_recv()

        @pl.when(has_prev)
        def _():
            copies[1].wait_recv()

    def sent(copies):
        @pl.when(has_prev)
        def _():
            copies[0].wait_send()

        @pl.when(has_next)
        def _():
            copies[1].wait_send()

    for copy in local[1]:
        copy.wait()

    launch(near_counts)

    columns = pl.ds(pl.multiple_of(x * W, W), W)
    chip = x // C
    sends = []
    for c in range(C):
        for d in range(K):
            j = k ^ d ^ chip if K & (K - 1) == 0 else lax.rem(k + d + K - chip, K)
            at = (c * K + j) * R
            mine = jnp.logical_and(k * C + c == x, j == k)
            low = (j == 0) if c == 0 else None
            high = (j == K - 1) if c == C - 1 else None
            inner = jnp.bool_(True)
            forms = []
            if low is not None:
                inner = jnp.logical_and(inner, jnp.logical_not(low))
                forms.append((low, 0, 1))
            if high is not None:
                inner = jnp.logical_and(inner, jnp.logical_not(high))
                forms.append((high, 1, 0))
            forms.append((inner, 1, 1))
            for want, before, after in forms:
                n = before + R + after
                src = fp.at[:, pl.ds(at - before, n)]
                dst = ub.at[:, pl.ds(1 - before, n), :, columns]
                far = remote(src, dst, s2_send.at[c * K + d], s2_recv.at[x], {"gx": k * C + c, "gy": j})
                near = pltpu.make_async_copy(src, dst, s2_recv.at[x])
                near_when = jnp.logical_and(want, mine)
                far_when = jnp.logical_and(want, jnp.logical_not(mine))

                @pl.when(near_when)
                def _(near=near):
                    near.start()

                @pl.when(far_when)
                def _(far=far):
                    far.start()

                sends.append((far_when, far))

    for n, (want, row, at, gx, gy) in enumerate((
        (k > 0, 0, R + 1, jnp.maximum(k * C - 1, 0), K - 1),
        (k < K - 1, rows - 1, 0, jnp.minimum((k + 1) * C, G - 1), 0),
    )):
        src = fp.at[:, row:row + 1]
        dst = ub.at[:, at:at + 1, :, columns]
        far = remote(src, dst, row_send.at[n], row_recv.at[x], {"gx": gx, "gy": jnp.int32(gy)})
        near = pltpu.make_async_copy(src, dst, row_recv.at[x])
        mine = jnp.logical_and(gx == x, k == gy)
        far_when = jnp.logical_and(want, jnp.logical_not(mine))

        @pl.when(jnp.logical_and(want, mine))
        def _(near=near):
            near.start()

        @pl.when(far_when)
        def _(far=far):
            far.start()

        sends.append((far_when, far))

    launch(far_counts)
    arrived(near_counts)
    for copies in local[2:]:
        for copy in copies:
            copy.wait()

    lane = lax.broadcasted_iota(jnp.int32, (NZ, NY), 1)
    level = lax.broadcasted_iota(jnp.int32, (NZ, NY), 0)

    def above(v):
        return jnp.where(level < NZ - 1, pltpu.roll(v, NZ - 1, 0), 0.0)

    def below(v):
        return jnp.where(level > 0, pltpu.roll(v, 1, 0), 0.0)

    def right(v):
        return jnp.where(lane < NY - 1, pltpu.roll(v, NY - 1, 1), 0.0)

    def left(v):
        return jnp.where(lane > 0, pltpu.roll(v, 1, 1), 0.0)

    def plane_sum(v):
        return above(v) + below(v) + right(v) + left(v)

    def inside(i):
        at = place * R + i
        return jnp.logical_and(at >= 0, at < G * K * R)

    def voids_row(n, carry):
        v = 1.0 - cn[n].astype(jnp.float32) * particle_volume
        vo[n] = jnp.where(inside(n - H), v, 0.0)
        return carry

    lax.fori_loop(H - 1, R + H + 1, voids_row, 0)

    def weight_row(n, carry):
        v = vo[n]
        ws = 0.5 * (6.0 * v + vo[n - 1] + vo[n + 1] + plane_sum(v))
        total_w[n] = ws
        rh[n] = jnp.where(inside(n - H), 1.0 / ws, 0.0)
        wf[n] = 0.5 * (v + vo[n + 1])
        wr[n] = jnp.where(lane < NY - 1, 0.5 * (v + pltpu.roll(v, NY - 1, 1)), 0.0)
        wa[n] = jnp.where(level < NZ - 1, 0.5 * (v + pltpu.roll(v, NZ - 1, 0)), 0.0)
        return carry

    wf[H - 1] = 0.5 * (vo[H - 1] + vo[H])
    lax.fori_loop(H, R + H, weight_row, 0)

    def weighted(n, p, pa, pb):
        r, a = wr[n], wa[n]
        across = r * pltpu.roll(p, NY - 1, 1) + pltpu.roll(r * p, 1, 1)
        upright = a * pltpu.roll(p, NZ - 1, 0) + pltpu.roll(a * p, 1, 0)
        return (wf[n - 1] * pa + wf[n] * pb) + (across + upright)

    for want, copy in sends:
        @pl.when(want)
        def _(copy=copy):
            copy.wait_send()


    here = {"gx": x, "gy": k}
    slab_low = jnp.logical_and(lax.rem(x, C) == 0, k == 0)
    slab_high = jnp.logical_and(lax.rem(x, C) == C - 1, k == K - 1)
    at_side = jnp.logical_or(slab_low, slab_high)
    extra = jnp.logical_or(jnp.logical_and(slab_low, has_prev), jnp.logical_and(slab_high, has_next))

    def landed(n, sem):
        for sender in range(G):
            spot = pl.ds(sender * W, W)
            remote(fp.at[:, 0:n], ub.at[:, 0:n, :, spot], row_send.at[0], sem.at[sender], here).wait_recv()

    @pl.when(at_side)
    def _():
        landed(R + 1, s2_recv)

    @pl.when(jnp.logical_not(at_side))
    def _():
        landed(R + 2, s2_recv)

    @pl.when(extra)
    def _():
        landed(1, row_recv)

    def pass_on(src_up, dst_up, src_down, dst_down, ssem, rsem, at):
        return (
            remote(src_up, dst_up, ssem.at[0, at], rsem.at[0, at], prev_id),
            remote(src_down, dst_down, ssem.at[1, at], rsem.at[1, at], next_id),
        )

    def flux_rows():
        return pass_on(fl.at[1], fr.at[1], fl.at[R], fr.at[0], b_send, b_recv, 0)

    def level_rows(buf, s, ssem, rsem, at):
        return pass_on(buf.at[H + s], buf.at[H + R + s], buf.at[H + R - 1 - s], buf.at[H - 1 - s], ssem, rsem, at)

    def base_rows(s):
        return level_rows(b, s, b_send, b_recv, s + 1)

    def base_last():
        return level_rows(lv.at[1], H - 2, b_send, b_recv, H)

    def edge_rows():
        return pass_on(eb.at[0], b.at[H + R], eb.at[1], b.at[H - 1], b_send, b_recv, 1)

    def mid_rows(s):
        return level_rows(lv.at[first], s, p_send, p_recv, s)

    def mid_last():
        return level_rows(lv.at[first + 1], H - 2, p_send, p_recv, H - 1)

    def momentum(i, which):
        v, ws, drag, u = vo[H + i], total_w[H + i], dr[i], ub[which, i + 1]
        diffusion = weighted(H + i, u, ub[which, i], ub[which, i + 2]) - ws * u
        force = drag * pv[which, i]
        return (v * u + (time_step * viscosity) * diffusion + time_step * force) / (v + time_step * drag)

    def finish(i):
        b[H + i] = -(fl[i + 2] - fl[i] + b[H + i]) * rh[H + i]

    def momentum_step(s, carry):
        pair = (s, R - 1 - s)
        for which in range(3):
            values = [momentum(i, which) for i in pair]
            for i, value in zip(pair, values):
                pred[which, i] = value
            flux = [vo[H + i] * value for i, value in zip(pair, values)]
            if which == 0:
                for i, f in zip(pair, flux):
                    fl[i + 1] = f

                @pl.when(s == 0)
                def _():
                    launch(flux_rows())

            elif which == 1:
                part_source = [right(f) - left(f) for f in flux]
            else:
                for i, f, part in zip(pair, flux, part_source):
                    b[H + i] = part + (above(f) - below(f))

        @pl.when(s > 0)
        def _():
            finish(s - 1)
            finish(R - s)

            @pl.when(s == 1)
            def _():
                eb[0] = b[H]
                eb[1] = b[H + R - 1]
                launch(edge_rows())

            @pl.when(jnp.logical_and(s > 1, s < H))
            def _():
                launch(base_rows(s - 1))

        return carry

    half = R // 2
    lax.fori_loop(0, half, momentum_step, 0)
    finish(half - 1)
    finish(R - half)

    def sweep_pair(l, lo):
        hi = 2 * H + R - 1 - lo
        values = [
            weighted(n, lv[l - 1, n], lv[l - 1, n - 1], lv[l - 1, n + 1]) * rh[n] + b[n] for n in (lo, hi)
        ]
        lv[l, lo] = values[0]
        lv[l, hi] = values[1]

    def diagonal(j, start, stop):
        def level(l, carry):
            sweep_pair(l, l + (H - j))
            return carry

        lax.fori_loop(start, stop, level, 0)

    def rows_of(l, start, stop):
        def row(lo, carry):
            sweep_pair(l, lo)
            return carry

        lax.fori_loop(H + start, H + stop, row, 0, unroll=True)

    for j in range(2 - half, H + 1):
        if j == 0:
            arrived(far_counts)
            lax.fori_loop(1, H - 1, voids_row, 0)
            lax.fori_loop(R + H + 1, R + 2 * H - 1, voids_row, 0)
            wf[1] = 0.5 * (vo[1] + vo[2])
            lax.fori_loop(2, H, weight_row, 0)
            lax.fori_loop(R + H, R + 2 * H - 2, weight_row, 0)
            arrived(flux_rows())
            b[H] = b[H] + fr[0] * rh[H]
            b[H + R - 1] = b[H + R - 1] - fr[1] * rh[H + R - 1]
        elif j == H:
            arrived(base_last())
        elif j > 0:
            arrived(base_rows(j - 1))
            if j == 1:
                b[H - 1] = b[H - 1] - fl[1] * rh[H - 1]
                b[H + R] = b[H + R] + fl[R] * rh[H + R]
        stop = min(last_level, j + half - 1) + 1
        diagonal(j, 2 if j == H else 1, min(stop, first + 1))
        if j == 3 - H:
            launch(base_last())
        if j > 1:
            launch(mid_rows(first - j))
        if stop > first + 1:
            diagonal(j, first + 1, stop)
        if j == first + 3 - H:
            launch(mid_last())

    for s in range(first - 2, 0, -1):
        arrived(mid_rows(s))
    arrived(mid_last())
    arrived(mid_rows(0))
    for l in range(first + 1, last_level + 1):
        low = l - last_level - 1 + (1 if l in (first + 1, last_level) else 0)
        rows_of(l, low, l - H)

    def partner(d, back=False):
        if K & (K - 1) == 0:
            return chip ^ d
        return lax.rem(chip + (K - d if back else d), K)

    outs = []
    for d in range(K):
        for c in range(C):
            target = partner(d) * C + lax.rem(x + c, C)
            src = pf.at[H:H + R, :, pl.ds(pl.multiple_of(target * W, W), W)]
            if d == c == 0:
                pltpu.make_async_copy(src, rl.at[x], out_recv.at[x]).start()
            else:
                outs.append(remote(src, rl.at[x], out_send.at[d * C + c], out_recv.at[x], {"gx": target, "gy": k}))
                outs[-1].start()

    rises = []

    def rise(d):
        to = partner(d, back=True)
        for c in range(C):
            slot = to * C + c
            remote(pf.at[H:H + R, :, 0:W], rl.at[slot], out_send.at[0], out_recv.at[slot], here).wait_recv()
        src = rl.at[pl.ds(to * C, C)]
        far = remote(src, press_out.at[:, k], up_send.at[d], up_recv.at[k], {"gx": x, "gy": to})
        near = pltpu.make_async_copy(src, press_out.at[:, k], up_recv.at[k])

        @pl.when(to != k)
        def _():
            far.start()

        @pl.when(to == k)
        def _():
            near.start()

        rises.append((to, far))

    for d in range(K):
        rise(d)

    rows_of(last_level, -1, 0)

    def slope_row(i, carry):
        n = H + i
        p = pf[n]
        g0 = 0.5 * (pf[n + 1] - pf[n - 1])
        g1 = 0.5 * (right(p) - left(p))
        g2 = 0.5 * (above(p) - below(p))
        for which, g in enumerate((g0, g1, g2)):
            gr[which, i] = g
            pred[which, i] = pred[which, i] - time_step * g
        return carry

    lax.fori_loop(0, R, slope_row, 0)
    written = []
    for z in range(NZ):
        written.append(pltpu.make_async_copy(gr.at[:, :, z], grad_out.at[:, z], loc_sem.at[z]))
        written.append(pltpu.make_async_copy(pred.at[:, :, z], vel_out.at[:, z], loc_sem.at[NZ + z]))
    for copy in written:
        copy.start()

    for copies in [near_counts, far_counts, flux_rows(), edge_rows()] + [base_rows(i) for i in range(1, H - 1)] + [base_last(), mid_last()] + [mid_rows(i) for i in range(first - 1)]:
        sent(copies)

    for copy in outs:
        copy.wait_send()

    for to, far in rises:
        @pl.when(to != k)
        def _(far=far):
            far.wait_send()

    for j in range(K):
        remote(rl.at[0:C], press_out.at[:, j], up_send.at[0], up_recv.at[j], here).wait_recv()
    for copy in written:
        copy.wait()


def settle(press_in, vel_in, grad_in, press_out, vel_out, grad_out, press, vel, grad, in_sem, out_sem):
    C, K, R, NZ, W = press.shape
    steps = []

    def step(src, held, stores):
        at = len(steps)
        steps.append((pltpu.make_async_copy(src, held, in_sem.at[at]), stores))

    step(press_in, press, [pltpu.make_async_copy(press.at[:, :, :, z], press_out.at[z], out_sem.at[2 * vel.shape[0] + z]) for z in range(NZ)])

    for n, (src, held, dst) in enumerate(((vel_in, vel, vel_out), (grad_in, grad, grad_out))):
        for i in range(held.shape[0]):
            stores = [pltpu.make_async_copy(held.at[i], dst.at[i], out_sem.at[n * held.shape[0] + i])]
            step(src.at[i], held.at[i], stores)

    for load, _ in steps:
        load.start()
    for load, stores in steps:
        load.wait()
        for store in stores:
            store.start()
    for _, stores in steps:
        for store in stores:
            store.wait()


def shards(K, G, particle_count, drag_coeff, particle_velocity, fluid_velocity):
    NZ, R, NY = particle_count.shape
    rows, W = fluid_velocity.shape[2:]
    C = G // K
    H = max(ROUNDS)
    f32 = jnp.float32

    dma = pltpu.SemaphoreType.DMA
    pad = (R + 2 * H, NZ, NY)
    scratch = [
        pltpu.VMEM((3, rows, NZ, W), f32),
        pltpu.VMEM((3, R + 2, NZ, NY), f32),
        pltpu.VMEM(pad, jnp.int32),
        pltpu.VMEM((R, NZ, NY), f32),
        pltpu.VMEM((3, R, NZ, NY), f32),
        *[pltpu.VMEM(pad, f32) for _ in range(6)],
        pltpu.VMEM((3, R, NZ, NY), f32),
        pltpu.VMEM((3, R, NZ, NY), f32),
        pltpu.VMEM((R + 2, NZ, NY), f32),
        pltpu.VMEM((2, NZ, NY), f32),
        pltpu.VMEM((2, NZ, NY), f32),
        pltpu.VMEM((SWEEPS,) + pad, f32),
        pltpu.VMEM((G, R, NZ, W), f32),
        dma((4 * NZ,)), dma((2,)), dma((G,)),
        dma((K * C,)), dma((G,)),
        dma((2, 2)), dma((2, 2)), dma((2, H + 1)), dma((2, H + 1)), dma((2, H)), dma((2, H)), dma((G,)), dma((G,)), dma((K,)), dma((K,)),
    ]
    anywhere = pl.BlockSpec(memory_space=pl.ANY)
    pressure, velocity, slopes = pl.pallas_call(
        functools.partial(kernel, K, G, R, NZ, NY, W),
        out_shape=(
            jax.ShapeDtypeStruct((C, K, R, NZ, W), f32),
            jax.ShapeDtypeStruct((3, NZ, R, NY), f32),
            jax.ShapeDtypeStruct((3, NZ, R, NY), f32),
        ),
        in_specs=[anywhere] * 4,
        out_specs=(anywhere, anywhere, anywhere),
        scratch_shapes=scratch,
        compiler_params=pltpu.CompilerParams(collective_id=0, has_side_effects=True, vmem_limit_bytes=67043328),
    )(particle_count, drag_coeff, particle_velocity, fluid_velocity)
    first = [pressure, velocity, slopes]
    pressure, velocity, slopes = pl.pallas_call(
        settle,
        out_shape=[
            jax.ShapeDtypeStruct((NZ, C, K, R, W), f32),
            jax.ShapeDtypeStruct(velocity.shape, f32),
            jax.ShapeDtypeStruct(slopes.shape, f32),
        ],
        in_specs=[anywhere] * 3,
        out_specs=[anywhere] * 3,
        scratch_shapes=[*[pltpu.VMEM(v.shape, f32) for v in first], dma((1 + 2 * 3,)), dma((NZ + 2 * 3,))],
        compiler_params=pltpu.CompilerParams(vmem_limit_bytes=67043328),
    )(*first)
    return pressure.reshape(NZ, rows, W), velocity, slopes


def solution(mesh):
    placed = (
        P(None, ("gx", "gy"), None),
        P(None, ("gx", "gy"), None),
        P(None, None, ("gx", "gy"), None),
        P(None, None, "gy", "gx"),
    )
    return jax.shard_map(
        functools.partial(shards, mesh.shape["gy"], mesh.shape["gx"]),
        mesh=mesh,
        in_specs=placed,
        out_specs=(
            P(None, "gy", "gx"),
            P(None, None, ("gx", "gy"), None),
            P(None, None, ("gx", "gy"), None),
        ),
        check_vma=False,
    )
```

```python
import functools

import jax
import jax.numpy as jnp
from jax import lax
from jax.experimental import pallas as pl
from jax.experimental.pallas import tpu as pltpu
from jax.sharding import PartitionSpec as P

SWEEPS = 8
ROUNDS = (4, 3)

particle_volume = 0.05
time_step = 0.5
viscosity = 0.1


def kernel(
    K, G, R, NZ, NY, W,
    count_in, drag_in, pvel_in, fluid_in,
    press_out, vel_out, grad_out,
    fp, ub, cn, dr, pv, vo, total_w, wf, wr, wa, rh, pred, gr, fl, fr, eb, lv, rl,
    loc_sem, row_send, row_recv, s2_send, s2_recv,
    hal_send, hal_recv, b_send, b_recv, p_send, p_recv, out_send, out_recv, up_send, up_recv,
):
    H = max(ROUNDS)
    first, last_level = ROUNDS[0], SWEEPS - 1
    b, pf = lv.at[0], lv.at[last_level]
    C = G // K
    B = C * K
    x = lax.axis_index("gx")
    k = lax.axis_index("gy")
    place = x * K + k
    has_prev = place > 0
    has_next = place < G * K - 1
    prev_id = {"gx": jnp.where(k > 0, x, jnp.maximum(x - 1, 0)), "gy": lax.rem(k + K - 1, K)}
    next_id = {"gx": jnp.where(k < K - 1, x, jnp.minimum(x + 1, G - 1)), "gy": lax.rem(k + 1, K)}

    def remote(src, dst, ssem, rsem, to):
        return pltpu.make_async_remote_copy(
            src_ref=src, dst_ref=dst, send_sem=ssem, recv_sem=rsem, device_id=to, device_id_type=pl.DeviceIdType.MESH
        )

    rows = R * B

    local = [[] for _ in range(4)]
    for z in range(NZ):
        local[0].append(pltpu.make_async_copy(fluid_in.at[:, z], fp.at[:, :, z], loc_sem.at[z]))
        local[1].append(pltpu.make_async_copy(count_in.at[z], cn.at[H:H + R, z], loc_sem.at[NZ + z]))
        local[2].append(pltpu.make_async_copy(drag_in.at[z], dr.at[:, z], loc_sem.at[2 * NZ + z]))
        local[3].append(pltpu.make_async_copy(pvel_in.at[:, z], pv.at[:, :, z], loc_sem.at[3 * NZ + z]))
    home = x // C
    barrier = pltpu.get_barrier_semaphore()
    for d in range(1, G * K):
        to = {"gx": lax.rem(x + d // K, G), "gy": lax.rem(k + d % K, K)}
        pl.semaphore_signal(barrier, inc=1, device_id=to, device_id_type=pl.DeviceIdType.MESH)

    for copies in local:
        for copy in copies:
            copy.start()

    line = jnp.zeros((NZ, NY), jnp.float32)

    @pl.when(jnp.logical_not(has_prev))
    def _():
        for which in range(3):
            ub[which, 0] = line

    @pl.when(jnp.logical_not(has_next))
    def _():
        for which in range(3):
            ub[which, R + 1] = line

    fl[0] = line
    fl[R + 1] = line
    edge = jnp.zeros((H, NZ, NY), jnp.float32)

    @pl.when(jnp.logical_not(has_prev))
    def _():
        fr[0] = line
        lv[0, 0:H] = edge
        lv[1, 1] = line
        lv[first, 0:H] = edge
        lv[last_level, H - 1] = line

    @pl.when(jnp.logical_not(has_next))
    def _():
        fr[1] = line
        lv[0, H + R:2 * H + R] = edge
        lv[1, 2 * H + R - 2] = line
        lv[first, H + R:2 * H + R] = edge
        lv[last_level, H + R] = line

    for copy in local[0]:
        copy.wait()
    pl.semaphore_wait(barrier, G * K - 1)

    def count_rows(begin, stop, at):
        return (
            remote(cn.at[H + begin:H + stop], cn.at[H + R + begin:H + R + stop], hal_send.at[at, 0], hal_recv.at[at, 0], prev_id),
            remote(cn.at[H + R - stop:H + R - begin], cn.at[H - stop:H - begin], hal_send.at[at, 1], hal_recv.at[at, 1], next_id),
        )

    near_counts, far_counts = count_rows(0, 1, 0), count_rows(1, H - 1, 1)

    turned = k == K - 1
    wraps = (jnp.logical_and(k == 0, has_prev), jnp.logical_and(turned, has_next))
    plain = (jnp.logical_and(k > 0, has_prev), jnp.logical_and(jnp.logical_not(turned), has_next))

    def launch(copies, only=None):
        for group in ((wraps, plain) if only is None else (only,)):
            for when, copy in zip(group, copies):
                @pl.when(when)
                def _(copy=copy):
                    copy.start()

    def arrived(copies):
        @pl.when(has_next)
        def _():
            copies[0].wait_recv()

        @pl.when(has_prev)
        def _():
            copies[1].wait_recv()

    def sent(copies):
        @pl.when(has_prev)
        def _():
            copies[0].wait_send()

        @pl.when(has_next)
        def _():
            copies[1].wait_send()

    for copy in local[1]:
        copy.wait()

    launch(near_counts)

    columns = pl.ds(pl.multiple_of(x * W, W), W)
    chip = x // C
    sends = []
    for c in range(C):
        for d in range(K):
            j = k ^ d ^ chip if K & (K - 1) == 0 else lax.rem(k + d + K - chip, K)
            at = (c * K + j) * R
            mine = jnp.logical_and(k * C + c == x, j == k)
            low = (j == 0) if c == 0 else None
            high = (j == K - 1) if c == C - 1 else None
            inner = jnp.bool_(True)
            forms = []
            if low is not None:
                inner = jnp.logical_and(inner, jnp.logical_not(low))
                forms.append((low, 0, 1))
            if high is not None:
                inner = jnp.logical_and(inner, jnp.logical_not(high))
                forms.append((high, 1, 0))
            forms.append((inner, 1, 1))
            for want, before, after in forms:
                n = before + R + after
                src = fp.at[:, pl.ds(at - before, n)]
                dst = ub.at[:, pl.ds(1 - before, n), :, columns]
                far = remote(src, dst, s2_send.at[c * K + d], s2_recv.at[x], {"gx": k * C + c, "gy": j})
                near = pltpu.make_async_copy(src, dst, s2_recv.at[x])
                near_when = jnp.logical_and(want, mine)
                far_when = jnp.logical_and(want, jnp.logical_not(mine))

                @pl.when(near_when)
                def _(near=near):
                    near.start()

                @pl.when(far_when)
                def _(far=far):
                    far.start()

                sends.append((far_when, far))

    for n, (want, row, at, gx, gy) in enumerate((
        (k > 0, 0, R + 1, jnp.maximum(k * C - 1, 0), K - 1),
        (k < K - 1, rows - 1, 0, jnp.minimum((k + 1) * C, G - 1), 0),
    )):
        src = fp.at[:, row:row + 1]
        dst = ub.at[:, at:at + 1, :, columns]
        far = remote(src, dst, row_send.at[n], row_recv.at[x], {"gx": gx, "gy": jnp.int32(gy)})
        near = pltpu.make_async_copy(src, dst, row_recv.at[x])
        mine = jnp.logical_and(gx == x, k == gy)
        far_when = jnp.logical_and(want, jnp.logical_not(mine))

        @pl.when(jnp.logical_and(want, mine))
        def _(near=near):
            near.start()

        @pl.when(far_when)
        def _(far=far):
            far.start()

        sends.append((far_when, far))

    launch(far_counts)
    arrived(near_counts)
    for copies in local[2:]:
        for copy in copies:
            copy.wait()

    lane = lax.broadcasted_iota(jnp.int32, (NZ, NY), 1)
    level = lax.broadcasted_iota(jnp.int32, (NZ, NY), 0)

    def above(v):
        return jnp.where(level < NZ - 1, pltpu.roll(v, NZ - 1, 0), 0.0)

    def below(v):
        return jnp.where(level > 0, pltpu.roll(v, 1, 0), 0.0)

    def right(v):
        return jnp.where(lane < NY - 1, pltpu.roll(v, NY - 1, 1), 0.0)

    def left(v):
        return jnp.where(lane > 0, pltpu.roll(v, 1, 1), 0.0)

    def plane_sum(v):
        return above(v) + below(v) + right(v) + left(v)

    def inside(i):
        at = place * R + i
        return jnp.logical_and(at >= 0, at < G * K * R)

    def voids_row(n, carry):
        v = 1.0 - cn[n].astype(jnp.float32) * particle_volume
        vo[n] = jnp.where(inside(n - H), v, 0.0)
        return carry

    lax.fori_loop(H - 1, R + H + 1, voids_row, 0)

    def weight_row(n, carry):
        v = vo[n]
        ws = 0.5 * (6.0 * v + vo[n - 1] + vo[n + 1] + plane_sum(v))
        total_w[n] = ws
        rh[n] = jnp.where(inside(n - H), 1.0 / ws, 0.0)
        wf[n] = 0.5 * (v + vo[n + 1])
        wr[n] = jnp.where(lane < NY - 1, 0.5 * (v + pltpu.roll(v, NY - 1, 1)), 0.0)
        wa[n] = jnp.where(level < NZ - 1, 0.5 * (v + pltpu.roll(v, NZ - 1, 0)), 0.0)
        return carry

    wf[H - 1] = 0.5 * (vo[H - 1] + vo[H])
    lax.fori_loop(H, R + H, weight_row, 0)

    def weighted(n, p, pa, pb):
        r, a = wr[n], wa[n]
        across = r * pltpu.roll(p, NY - 1, 1) + pltpu.roll(r * p, 1, 1)
        upright = a * pltpu.roll(p, NZ - 1, 0) + pltpu.roll(a * p, 1, 0)
        return (wf[n - 1] * pa + wf[n] * pb) + (across + upright)

    for want, copy in sends:
        @pl.when(want)
        def _(copy=copy):
            copy.wait_send()


    here = {"gx": x, "gy": k}
    slab_low = jnp.logical_and(lax.rem(x, C) == 0, k == 0)
    slab_high = jnp.logical_and(lax.rem(x, C) == C - 1, k == K - 1)
    at_side = jnp.logical_or(slab_low, slab_high)
    extra = jnp.logical_or(jnp.logical_and(slab_low, has_prev), jnp.logical_and(slab_high, has_next))

    def landed(n, sem):
        for sender in range(G):
            spot = pl.ds(sender * W, W)
            remote(fp.at[:, 0:n], ub.at[:, 0:n, :, spot], row_send.at[0], sem.at[sender], here).wait_recv()

    @pl.when(at_side)
    def _():
        landed(R + 1, s2_recv)

    @pl.when(jnp.logical_not(at_side))
    def _():
        landed(R + 2, s2_recv)

    @pl.when(extra)
    def _():
        landed(1, row_recv)

    def pass_on(src_up, dst_up, src_down, dst_down, ssem, rsem, at):
        return (
            remote(src_up, dst_up, ssem.at[0, at], rsem.at[0, at], prev_id),
            remote(src_down, dst_down, ssem.at[1, at], rsem.at[1, at], next_id),
        )

    def flux_rows():
        return pass_on(fl.at[1], fr.at[1], fl.at[R], fr.at[0], b_send, b_recv, 0)

    def level_rows(buf, s, ssem, rsem, at):
        return pass_on(buf.at[H + s], buf.at[H + R + s], buf.at[H + R - 1 - s], buf.at[H - 1 - s], ssem, rsem, at)

    def base_rows(s):
        return level_rows(b, s, b_send, b_recv, s + 1)

    def base_last():
        return level_rows(lv.at[1], H - 2, b_send, b_recv, H)

    def edge_rows():
        return pass_on(eb.at[0], b.at[H + R], eb.at[1], b.at[H - 1], b_send, b_recv, 1)

    def mid_rows(s):
        return level_rows(lv.at[first], s, p_send, p_recv, s)

    def last_rows():
        return level_rows(pf, 0, p_send, p_recv, H - 1)

    def momentum(i, which):
        v, ws, drag, u = vo[H + i], total_w[H + i], dr[i], ub[which, i + 1]
        diffusion = weighted(H + i, u, ub[which, i], ub[which, i + 2]) - ws * u
        force = drag * pv[which, i]
        return (v * u + (time_step * viscosity) * diffusion + time_step * force) / (v + time_step * drag)

    def finish(i):
        b[H + i] = -(fl[i + 2] - fl[i] + b[H + i]) * rh[H + i]

    def momentum_step(s, carry):
        pair = (s, R - 1 - s)
        for which in range(3):
            values = [momentum(i, which) for i in pair]
            for i, value in zip(pair, values):
                pred[which, i] = value
            flux = [vo[H + i] * value for i, value in zip(pair, values)]
            if which == 0:
                for i, f in zip(pair, flux):
                    fl[i + 1] = f

                @pl.when(s == 0)
                def _():
                    launch(flux_rows())

            elif which == 1:
                part_source = [right(f) - left(f) for f in flux]
            else:
                for i, f, part in zip(pair, flux, part_source):
                    b[H + i] = part + (above(f) - below(f))

        @pl.when(s > 0)
        def _():
            finish(s - 1)
            finish(R - s)

            @pl.when(s == 1)
            def _():
                eb[0] = b[H]
                eb[1] = b[H + R - 1]
                launch(edge_rows())

            @pl.when(jnp.logical_and(s > 1, s < H))
            def _():
                launch(base_rows(s - 1))

        return carry

    half = R // 2
    lax.fori_loop(0, half, momentum_step, 0)
    finish(half - 1)
    finish(R - half)

    def sweep_pair(l, lo):
        hi = 2 * H + R - 1 - lo
        values = [
            weighted(n, lv[l - 1, n], lv[l - 1, n - 1], lv[l - 1, n + 1]) * rh[n] + b[n] for n in (lo, hi)
        ]
        lv[l, lo] = values[0]
        lv[l, hi] = values[1]

    def diagonal(j, start, stop):
        def level(l, carry):
            sweep_pair(l, l + (H - j))
            return carry

        lax.fori_loop(start, stop, level, 0)

    def rows_of(l, start, stop):
        def row(lo, carry):
            sweep_pair(l, lo)
            return carry

        lax.fori_loop(H + start, H + stop, row, 0, unroll=True)

    for j in range(2 - half, H + 1):
        if j == 0:
            arrived(far_counts)
            lax.fori_loop(1, H - 1, voids_row, 0)
            lax.fori_loop(R + H + 1, R + 2 * H - 1, voids_row, 0)
            wf[1] = 0.5 * (vo[1] + vo[2])
            lax.fori_loop(2, H, weight_row, 0)
            lax.fori_loop(R + H, R + 2 * H - 2, weight_row, 0)
            arrived(flux_rows())
            b[H] = b[H] + fr[0] * rh[H]
            b[H + R - 1] = b[H + R - 1] - fr[1] * rh[H + R - 1]
        elif j == H:
            arrived(base_last())
        elif j > 0:
            arrived(base_rows(j - 1))
            if j == 1:
                b[H - 1] = b[H - 1] - fl[1] * rh[H - 1]
                b[H + R] = b[H + R] + fl[R] * rh[H + R]
        stop = min(last_level, j + half - 1) + 1
        diagonal(j, 2 if j == H else 1, min(stop, first + 1))
        if j == 3 - H:
            launch(base_last())
        if first - j < ROUNDS[1]:
            launch(mid_rows(first - j))
        if stop > first + 1:
            diagonal(j, first + 1, stop)

    for s in range(ROUNDS[1] - 1, -1, -1):
        arrived(mid_rows(s))
    for l in range(first + 1, last_level + 1):
        rows_of(l, l - last_level, l - H)

    def partner(d, back=False):
        if K & (K - 1) == 0:
            return chip ^ d
        return lax.rem(chip + (K - d if back else d), K)

    outs = []
    for d in range(K):
        for c in range(C):
            target = partner(d) * C + lax.rem(x + c, C)
            src = pf.at[H:H + R, :, pl.ds(pl.multiple_of(target * W, W), W)]
            if d == c == 0:
                pltpu.make_async_copy(src, rl.at[x], out_recv.at[x]).start()
            else:
                outs.append(remote(src, rl.at[x], out_send.at[d * C + c], out_recv.at[x], {"gx": target, "gy": k}))
                outs[-1].start()

    launch(last_rows())
    rises = []

    def rise(d):
        to = partner(d, back=True)
        for c in range(C):
            slot = to * C + c
            remote(pf.at[H:H + R, :, 0:W], rl.at[slot], out_send.at[0], out_recv.at[slot], here).wait_recv()
        src = rl.at[pl.ds(to * C, C)]
        far = remote(src, press_out.at[:, k], up_send.at[d], up_recv.at[k], {"gx": x, "gy": to})
        near = pltpu.make_async_copy(src, press_out.at[:, k], up_recv.at[k])

        @pl.when(to != k)
        def _():
            far.start()

        @pl.when(to == k)
        def _():
            near.start()

        rises.append((to, far))

    for d in range(K):
        rise(d)

    arrived(last_rows())

    def slope_row(i, carry):
        n = H + i
        p = pf[n]
        g0 = 0.5 * (pf[n + 1] - pf[n - 1])
        g1 = 0.5 * (right(p) - left(p))
        g2 = 0.5 * (above(p) - below(p))
        for which, g in enumerate((g0, g1, g2)):
            gr[which, i] = g
            pred[which, i] = pred[which, i] - time_step * g
        return carry

    lax.fori_loop(0, R, slope_row, 0)
    written = []
    for z in range(NZ):
        written.append(pltpu.make_async_copy(gr.at[:, :, z], grad_out.at[:, z], loc_sem.at[z]))
        written.append(pltpu.make_async_copy(pred.at[:, :, z], vel_out.at[:, z], loc_sem.at[NZ + z]))
    for copy in written:
        copy.start()

    for copies in [near_counts, far_counts, flux_rows(), edge_rows()] + [base_rows(i) for i in range(1, H - 1)] + [base_last(), last_rows()] + [mid_rows(i) for i in range(ROUNDS[1])]:
        sent(copies)

    for copy in outs:
        copy.wait_send()

    for to, far in rises:
        @pl.when(to != k)
        def _(far=far):
            far.wait_send()

    for j in range(K):
        remote(rl.at[0:C], press_out.at[:, j], up_send.at[0], up_recv.at[j], here).wait_recv()
    for copy in written:
        copy.wait()


def settle(press_in, vel_in, grad_in, press_out, vel_out, grad_out, press, vel, grad, in_sem, out_sem):
    C, K, R, NZ, W = press.shape
    steps = []

    def step(src, held, stores):
        at = len(steps)
        steps.append((pltpu.make_async_copy(src, held, in_sem.at[at]), stores))

    step(press_in, press, [pltpu.make_async_copy(press.at[:, :, :, z], press_out.at[z], out_sem.at[2 * vel.shape[0] + z]) for z in range(NZ)])

    for n, (src, held, dst) in enumerate(((vel_in, vel, vel_out), (grad_in, grad, grad_out))):
        for i in range(held.shape[0]):
            stores = [pltpu.make_async_copy(held.at[i], dst.at[i], out_sem.at[n * held.shape[0] + i])]
            step(src.at[i], held.at[i], stores)

    for load, _ in steps:
        load.start()
    for load, stores in steps:
        load.wait()
        for store in stores:
            store.start()
    for _, stores in steps:
        for store in stores:
            store.wait()


def shards(K, G, particle_count, drag_coeff, particle_velocity, fluid_velocity):
    NZ, R, NY = particle_count.shape
    rows, W = fluid_velocity.shape[2:]
    C = G // K
    H = max(ROUNDS)
    f32 = jnp.float32

    dma = pltpu.SemaphoreType.DMA
    pad = (R + 2 * H, NZ, NY)
    scratch = [
        pltpu.VMEM((3, rows, NZ, W), f32),
        pltpu.VMEM((3, R + 2, NZ, NY), f32),
        pltpu.VMEM(pad, jnp.int32),
        pltpu.VMEM((R, NZ, NY), f32),
        pltpu.VMEM((3, R, NZ, NY), f32),
        *[pltpu.VMEM(pad, f32) for _ in range(6)],
        pltpu.VMEM((3, R, NZ, NY), f32),
        pltpu.VMEM((3, R, NZ, NY), f32),
        pltpu.VMEM((R + 2, NZ, NY), f32),
        pltpu.VMEM((2, NZ, NY), f32),
        pltpu.VMEM((2, NZ, NY), f32),
        pltpu.VMEM((SWEEPS,) + pad, f32),
        pltpu.VMEM((G, R, NZ, W), f32),
        dma((4 * NZ,)), dma((2,)), dma((G,)),
        dma((K * C,)), dma((G,)),
        dma((2, 2)), dma((2, 2)), dma((2, H + 1)), dma((2, H + 1)), dma((2, H)), dma((2, H)), dma((G,)), dma((G,)), dma((K,)), dma((K,)),
    ]
    anywhere = pl.BlockSpec(memory_space=pl.ANY)
    pressure, velocity, slopes = pl.pallas_call(
        functools.partial(kernel, K, G, R, NZ, NY, W),
        out_shape=(
            jax.ShapeDtypeStruct((C, K, R, NZ, W), f32),
            jax.ShapeDtypeStruct((3, NZ, R, NY), f32),
            jax.ShapeDtypeStruct((3, NZ, R, NY), f32),
        ),
        in_specs=[anywhere] * 4,
        out_specs=(anywhere, anywhere, anywhere),
        scratch_shapes=scratch,
        compiler_params=pltpu.CompilerParams(collective_id=0, has_side_effects=True, vmem_limit_bytes=67043328),
    )(particle_count, drag_coeff, particle_velocity, fluid_velocity)
    first = [pressure, velocity, slopes]
    pressure, velocity, slopes = pl.pallas_call(
        settle,
        out_shape=[
            jax.ShapeDtypeStruct((NZ, C, K, R, W), f32),
            jax.ShapeDtypeStruct(velocity.shape, f32),
            jax.ShapeDtypeStruct(slopes.shape, f32),
        ],
        in_specs=[anywhere] * 3,
        out_specs=[anywhere] * 3,
        scratch_shapes=[*[pltpu.VMEM(v.shape, f32) for v in first], dma((1 + 2 * 3,)), dma((NZ + 2 * 3,))],
        compiler_params=pltpu.CompilerParams(vmem_limit_bytes=67043328),
    )(*first)
    return pressure.reshape(NZ, rows, W), velocity, slopes


def solution(mesh):
    placed = (
        P(None, ("gx", "gy"), None),
        P(None, ("gx", "gy"), None),
        P(None, None, ("gx", "gy"), None),
        P(None, None, "gy", "gx"),
    )
    return jax.shard_map(
        functools.partial(shards, mesh.shape["gy"], mesh.shape["gx"]),
        mesh=mesh,
        in_specs=placed,
        out_specs=(
            P(None, "gy", "gx"),
            P(None, None, ("gx", "gy"), None),
            P(None, None, ("gx", "gy"), None),
        ),
        check_vma=False,
    )
```

```python
import functools

import jax
import jax.numpy as jnp
from jax import lax
from jax.experimental import pallas as pl
from jax.experimental.pallas import tpu as pltpu
from jax.sharding import PartitionSpec as P

SWEEPS = 8
ROUNDS = (4, 3)

particle_volume = 0.05
time_step = 0.5
viscosity = 0.1


def kernel(
    K, G, R, NZ, NY, W,
    count_in, drag_in, pvel_in, fluid_in,
    press_out, vel_out, grad_out,
    fp, ub, cn, dr, pv, vo, total_w, wf, wr, wa, rh, pred, gr, fl, fr, eb, lv, rl,
    loc_sem, row_send, row_recv, s2_send, s2_recv,
    hal_send, hal_recv, b_send, b_recv, p_send, p_recv, out_send, out_recv, up_send, up_recv,
):
    H = max(ROUNDS)
    first, last_level = ROUNDS[0], SWEEPS - 1
    b, pf = lv.at[0], lv.at[last_level]
    C = G // K
    B = C * K
    x = lax.axis_index("gx")
    k = lax.axis_index("gy")
    place = x * K + k
    has_prev = place > 0
    has_next = place < G * K - 1
    prev_id = {"gx": jnp.where(k > 0, x, jnp.maximum(x - 1, 0)), "gy": lax.rem(k + K - 1, K)}
    next_id = {"gx": jnp.where(k < K - 1, x, jnp.minimum(x + 1, G - 1)), "gy": lax.rem(k + 1, K)}

    def remote(src, dst, ssem, rsem, to):
        return pltpu.make_async_remote_copy(
            src_ref=src, dst_ref=dst, send_sem=ssem, recv_sem=rsem, device_id=to, device_id_type=pl.DeviceIdType.MESH
        )

    rows = R * B

    local = [[] for _ in range(4)]
    for z in range(NZ):
        local[0].append(pltpu.make_async_copy(fluid_in.at[:, z], fp.at[:, :, z], loc_sem.at[z]))
        local[1].append(pltpu.make_async_copy(count_in.at[z], cn.at[H:H + R, z], loc_sem.at[NZ + z]))
        local[2].append(pltpu.make_async_copy(drag_in.at[z], dr.at[:, z], loc_sem.at[2 * NZ + z]))
        local[3].append(pltpu.make_async_copy(pvel_in.at[:, z], pv.at[:, :, z], loc_sem.at[3 * NZ + z]))
    home = x // C
    barrier = pltpu.get_barrier_semaphore()
    for d in range(1, G * K):
        to = {"gx": lax.rem(x + d // K, G), "gy": lax.rem(k + d % K, K)}
        pl.semaphore_signal(barrier, inc=1, device_id=to, device_id_type=pl.DeviceIdType.MESH)

    for copies in local:
        for copy in copies:
            copy.start()

    line = jnp.zeros((NZ, NY), jnp.float32)

    @pl.when(jnp.logical_not(has_prev))
    def _():
        for which in range(3):
            ub[which, 0] = line

    @pl.when(jnp.logical_not(has_next))
    def _():
        for which in range(3):
            ub[which, R + 1] = line

    fl[0] = line
    fl[R + 1] = line
    edge = jnp.zeros((H, NZ, NY), jnp.float32)

    @pl.when(jnp.logical_not(has_prev))
    def _():
        fr[0] = line
        lv[0, 0:H] = edge
        lv[1, 1] = line
        lv[first, 0:H] = edge
        lv[last_level, H - 1] = line

    @pl.when(jnp.logical_not(has_next))
    def _():
        fr[1] = line
        lv[0, H + R:2 * H + R] = edge
        lv[1, 2 * H + R - 2] = line
        lv[first, H + R:2 * H + R] = edge
        lv[last_level, H + R] = line

    for copy in local[0]:
        copy.wait()
    pl.semaphore_wait(barrier, G * K - 1)

    def count_rows(begin, stop, at):
        return (
            remote(cn.at[H + begin:H + stop], cn.at[H + R + begin:H + R + stop], hal_send.at[at, 0], hal_recv.at[at, 0], prev_id),
            remote(cn.at[H + R - stop:H + R - begin], cn.at[H - stop:H - begin], hal_send.at[at, 1], hal_recv.at[at, 1], next_id),
        )

    near_counts, far_counts = count_rows(0, 1, 0), count_rows(1, H - 1, 1)

    turned = k == K - 1
    wraps = (jnp.logical_and(k == 0, has_prev), jnp.logical_and(turned, has_next))
    plain = (jnp.logical_and(k > 0, has_prev), jnp.logical_and(jnp.logical_not(turned), has_next))

    def launch(copies, only=None):
        for group in ((wraps, plain) if only is None else (only,)):
            for when, copy in zip(group, copies):
                @pl.when(when)
                def _(copy=copy):
                    copy.start()

    def arrived(copies):
        @pl.when(has_next)
        def _():
            copies[0].wait_recv()

        @pl.when(has_prev)
        def _():
            copies[1].wait_recv()

    def sent(copies):
        @pl.when(has_prev)
        def _():
            copies[0].wait_send()

        @pl.when(has_next)
        def _():
            copies[1].wait_send()

    for copy in local[1]:
        copy.wait()

    launch(near_counts)

    columns = pl.ds(pl.multiple_of(x * W, W), W)
    chip = x // C
    sends = []
    for c in range(C):
        for d in range(K):
            j = k ^ d ^ chip if K & (K - 1) == 0 else lax.rem(k + d + K - chip, K)
            at = (c * K + j) * R
            mine = jnp.logical_and(k * C + c == x, j == k)
            low = (j == 0) if c == 0 else None
            high = (j == K - 1) if c == C - 1 else None
            inner = jnp.bool_(True)
            forms = []
            if low is not None:
                inner = jnp.logical_and(inner, jnp.logical_not(low))
                forms.append((low, 0, 1))
            if high is not None:
                inner = jnp.logical_and(inner, jnp.logical_not(high))
                forms.append((high, 1, 0))
            forms.append((inner, 1, 1))
            for want, before, after in forms:
                n = before + R + after
                src = fp.at[:, pl.ds(at - before, n)]
                dst = ub.at[:, pl.ds(1 - before, n), :, columns]
                far = remote(src, dst, s2_send.at[c * K + d], s2_recv.at[x], {"gx": k * C + c, "gy": j})
                near = pltpu.make_async_copy(src, dst, s2_recv.at[x])
                near_when = jnp.logical_and(want, mine)
                far_when = jnp.logical_and(want, jnp.logical_not(mine))

                @pl.when(near_when)
                def _(near=near):
                    near.start()

                @pl.when(far_when)
                def _(far=far):
                    far.start()

                sends.append((far_when, far))

    for n, (want, row, at, gx, gy) in enumerate((
        (k > 0, 0, R + 1, jnp.maximum(k * C - 1, 0), K - 1),
        (k < K - 1, rows - 1, 0, jnp.minimum((k + 1) * C, G - 1), 0),
    )):
        src = fp.at[:, row:row + 1]
        dst = ub.at[:, at:at + 1, :, columns]
        far = remote(src, dst, row_send.at[n], row_recv.at[x], {"gx": gx, "gy": jnp.int32(gy)})
        near = pltpu.make_async_copy(src, dst, row_recv.at[x])
        mine = jnp.logical_and(gx == x, k == gy)
        far_when = jnp.logical_and(want, jnp.logical_not(mine))

        @pl.when(jnp.logical_and(want, mine))
        def _(near=near):
            near.start()

        @pl.when(far_when)
        def _(far=far):
            far.start()

        sends.append((far_when, far))

    launch(far_counts)
    arrived(near_counts)
    for copies in local[2:]:
        for copy in copies:
            copy.wait()

    lane = lax.broadcasted_iota(jnp.int32, (NZ, NY), 1)
    level = lax.broadcasted_iota(jnp.int32, (NZ, NY), 0)

    def above(v):
        return jnp.where(level < NZ - 1, pltpu.roll(v, NZ - 1, 0), 0.0)

    def below(v):
        return jnp.where(level > 0, pltpu.roll(v, 1, 0), 0.0)

    def right(v):
        return jnp.where(lane < NY - 1, pltpu.roll(v, NY - 1, 1), 0.0)

    def left(v):
        return jnp.where(lane > 0, pltpu.roll(v, 1, 1), 0.0)

    def plane_sum(v):
        return above(v) + below(v) + right(v) + left(v)

    def inside(i):
        at = place * R + i
        return jnp.logical_and(at >= 0, at < G * K * R)

    def voids_row(n, carry):
        v = 1.0 - cn[n].astype(jnp.float32) * particle_volume
        vo[n] = jnp.where(inside(n - H), v, 0.0)
        return carry

    lax.fori_loop(H - 1, R + H + 1, voids_row, 0)

    def weight_row(n, carry):
        v = vo[n]
        ws = 0.5 * (6.0 * v + vo[n - 1] + vo[n + 1] + plane_sum(v))
        total_w[n] = ws
        rh[n] = jnp.where(inside(n - H), 1.0 / ws, 0.0)
        wf[n] = 0.5 * (v + vo[n + 1])
        wr[n] = jnp.where(lane < NY - 1, 0.5 * (v + pltpu.roll(v, NY - 1, 1)), 0.0)
        wa[n] = jnp.where(level < NZ - 1, 0.5 * (v + pltpu.roll(v, NZ - 1, 0)), 0.0)
        return carry

    wf[H - 1] = 0.5 * (vo[H - 1] + vo[H])
    lax.fori_loop(H, R + H, weight_row, 0)

    def weighted(n, p, pa, pb):
        r, a = wr[n], wa[n]
        across = r * pltpu.roll(p, NY - 1, 1) + pltpu.roll(r * p, 1, 1)
        upright = a * pltpu.roll(p, NZ - 1, 0) + pltpu.roll(a * p, 1, 0)
        return (wf[n - 1] * pa + wf[n] * pb) + (across + upright)

    for want, copy in sends:
        @pl.when(want)
        def _(copy=copy):
            copy.wait_send()


    here = {"gx": x, "gy": k}
    slab_low = jnp.logical_and(lax.rem(x, C) == 0, k == 0)
    slab_high = jnp.logical_and(lax.rem(x, C) == C - 1, k == K - 1)
    at_side = jnp.logical_or(slab_low, slab_high)
    extra = jnp.logical_or(jnp.logical_and(slab_low, has_prev), jnp.logical_and(slab_high, has_next))

    def landed(n, sem):
        for sender in range(G):
            spot = pl.ds(sender * W, W)
            remote(fp.at[:, 0:n], ub.at[:, 0:n, :, spot], row_send.at[0], sem.at[sender], here).wait_recv()

    @pl.when(at_side)
    def _():
        landed(R + 1, s2_recv)

    @pl.when(jnp.logical_not(at_side))
    def _():
        landed(R + 2, s2_recv)

    @pl.when(extra)
    def _():
        landed(1, row_recv)

    def pass_on(src_up, dst_up, src_down, dst_down, ssem, rsem, at):
        return (
            remote(src_up, dst_up, ssem.at[0, at], rsem.at[0, at], prev_id),
            remote(src_down, dst_down, ssem.at[1, at], rsem.at[1, at], next_id),
        )

    def flux_rows():
        return pass_on(fl.at[1], fr.at[1], fl.at[R], fr.at[0], b_send, b_recv, 0)

    def level_rows(buf, s, ssem, rsem, at):
        return pass_on(buf.at[H + s], buf.at[H + R + s], buf.at[H + R - 1 - s], buf.at[H - 1 - s], ssem, rsem, at)

    def base_rows(s):
        return level_rows(b, s, b_send, b_recv, s + 1)

    def base_last():
        return level_rows(lv.at[1], H - 2, b_send, b_recv, H)

    def edge_rows():
        return pass_on(eb.at[0], b.at[H + R], eb.at[1], b.at[H - 1], b_send, b_recv, 1)

    def mid_rows(s):
        return level_rows(lv.at[first], s, p_send, p_recv, s)

    def last_rows():
        return level_rows(pf, 0, p_send, p_recv, H - 1)

    def momentum(i, which):
        v, ws, drag, u = vo[H + i], total_w[H + i], dr[i], ub[which, i + 1]
        diffusion = weighted(H + i, u, ub[which, i], ub[which, i + 2]) - ws * u
        force = drag * pv[which, i]
        return (v * u + (time_step * viscosity) * diffusion + time_step * force) / (v + time_step * drag)

    def finish(i):
        b[H + i] = -(fl[i + 2] - fl[i] + b[H + i]) * rh[H + i]

    def momentum_step(s, carry):
        pair = (s, R - 1 - s)
        for which in range(3):
            values = [momentum(i, which) for i in pair]
            for i, value in zip(pair, values):
                pred[which, i] = value
            flux = [vo[H + i] * value for i, value in zip(pair, values)]
            if which == 0:
                for i, f in zip(pair, flux):
                    fl[i + 1] = f

                @pl.when(s == 0)
                def _():
                    launch(flux_rows())

            elif which == 1:
                part_source = [right(f) - left(f) for f in flux]
            else:
                for i, f, part in zip(pair, flux, part_source):
                    b[H + i] = part + (above(f) - below(f))

        @pl.when(s > 0)
        def _():
            finish(s - 1)
            finish(R - s)

            @pl.when(s == 1)
            def _():
                eb[0] = b[H]
                eb[1] = b[H + R - 1]
                launch(edge_rows())

            @pl.when(jnp.logical_and(s > 1, s < H))
            def _():
                launch(base_rows(s - 1))

        return carry

    half = R // 2
    lax.fori_loop(0, half, momentum_step, 0)
    finish(half - 1)
    finish(R - half)

    def sweep_pair(l, lo):
        hi = 2 * H + R - 1 - lo
        values = [
            weighted(n, lv[l - 1, n], lv[l - 1, n - 1], lv[l - 1, n + 1]) * rh[n] + b[n] for n in (lo, hi)
        ]
        lv[l, lo] = values[0]
        lv[l, hi] = values[1]

    def diagonal(j, start, stop):
        def level(l, carry):
            sweep_pair(l, l + (H - j))
            return carry

        lax.fori_loop(start, stop, level, 0)

    def rows_of(l, start, stop):
        def row(lo, carry):
            sweep_pair(l, lo)
            return carry

        lax.fori_loop(H + start, H + stop, row, 0, unroll=True)

    def partner(d, back=False):
        if K & (K - 1) == 0:
            return chip ^ d
        return lax.rem(chip + (K - d if back else d), K)

    pieces = ((half - 1, half + 1), (0, half - 1), (half + 1, R))
    outs, rises = [], []

    def send_piece(i):
        lo, hi = pieces[i]
        for d in range(K):
            for c in range(C):
                target = partner(d) * C + lax.rem(x + c, C)
                src = pf.at[H + lo:H + hi, :, pl.ds(pl.multiple_of(target * W, W), W)]
                dst = rl.at[x, lo:hi]
                if d == c == 0:
                    pltpu.make_async_copy(src, dst, out_recv.at[i, x]).start()
                else:
                    far = remote(src, dst, out_send.at[i, d * C + c], out_recv.at[i, x], {"gx": target, "gy": k})
                    outs.append(far)
                    far.start()

    def rise(i, d):
        lo, hi = pieces[i]
        to = partner(d, back=True)
        for c in range(C):
            slot = to * C + c
            remote(
                pf.at[H + lo:H + hi, :, 0:W], rl.at[slot, lo:hi], out_send.at[i, 0], out_recv.at[i, slot], here
            ).wait_recv()
        src, dst = rl.at[pl.ds(to * C, C), lo:hi], press_out.at[:, k, lo:hi]
        far = remote(src, dst, up_send.at[i, d], up_recv.at[i, k], {"gx": x, "gy": to})
        near = pltpu.make_async_copy(src, dst, up_recv.at[i, k])

        @pl.when(to != k)
        def _():
            far.start()

        @pl.when(to == k)
        def _():
            near.start()

        rises.append((to, far))

    for j in range(2 - half, H + 1):
        if j == 0:
            arrived(far_counts)
            lax.fori_loop(1, H - 1, voids_row, 0)
            lax.fori_loop(R + H + 1, R + 2 * H - 1, voids_row, 0)
            wf[1] = 0.5 * (vo[1] + vo[2])
            lax.fori_loop(2, H, weight_row, 0)
            lax.fori_loop(R + H, R + 2 * H - 2, weight_row, 0)
            arrived(flux_rows())
            b[H] = b[H] + fr[0] * rh[H]
            b[H + R - 1] = b[H + R - 1] - fr[1] * rh[H + R - 1]
        elif j == H:
            arrived(base_last())
        elif j > 0:
            arrived(base_rows(j - 1))
            if j == 1:
                b[H - 1] = b[H - 1] - fl[1] * rh[H - 1]
                b[H + R] = b[H + R] + fl[R] * rh[H + R]
        stop = min(last_level, j + half - 1) + 1
        diagonal(j, 2 if j == H else 1, min(stop, first + 1))
        if j == 3 - H:
            launch(base_last())
        if first - j < ROUNDS[1]:
            launch(mid_rows(first - j))
        if stop > first + 1:
            diagonal(j, first + 1, stop)

    send_piece(0)
    for s in range(ROUNDS[1] - 1, -1, -1):
        arrived(mid_rows(s))
    for l in range(first + 1, last_level + 1):
        rows_of(l, l - last_level, l - H)

    for i in (1, 2):
        send_piece(i)
    launch(last_rows())
    for d in range(K):
        rise(0, d)
    for d in range(K):
        for i in (1, 2):
            rise(i, d)

    arrived(last_rows())

    def slope_row(i, carry):
        n = H + i
        p = pf[n]
        g0 = 0.5 * (pf[n + 1] - pf[n - 1])
        g1 = 0.5 * (right(p) - left(p))
        g2 = 0.5 * (above(p) - below(p))
        for which, g in enumerate((g0, g1, g2)):
            gr[which, i] = g
            pred[which, i] = pred[which, i] - time_step * g
        return carry

    lax.fori_loop(0, R, slope_row, 0)
    written = []
    for z in range(NZ):
        written.append(pltpu.make_async_copy(gr.at[:, :, z], grad_out.at[:, z], loc_sem.at[z]))
        written.append(pltpu.make_async_copy(pred.at[:, :, z], vel_out.at[:, z], loc_sem.at[NZ + z]))
    for copy in written:
        copy.start()

    for copies in [near_counts, far_counts, flux_rows(), edge_rows()] + [base_rows(i) for i in range(1, H - 1)] + [base_last(), last_rows()] + [mid_rows(i) for i in range(ROUNDS[1])]:
        sent(copies)

    for copy in outs:
        copy.wait_send()

    for to, far in rises:
        @pl.when(to != k)
        def _(far=far):
            far.wait_send()

    for i, (lo, hi) in enumerate(pieces):
        for j in range(K):
            remote(
                rl.at[0:C, lo:hi], press_out.at[:, j, lo:hi], up_send.at[i, 0], up_recv.at[i, j], here
            ).wait_recv()
    for copy in written:
        copy.wait()


def settle(press_in, vel_in, grad_in, press_out, vel_out, grad_out, press, vel, grad, in_sem, out_sem):
    C, K, R, NZ, W = press.shape
    steps = []

    def step(src, held, stores):
        at = len(steps)
        steps.append((pltpu.make_async_copy(src, held, in_sem.at[at]), stores))

    step(press_in, press, [pltpu.make_async_copy(press.at[:, :, :, z], press_out.at[z], out_sem.at[2 * vel.shape[0] + z]) for z in range(NZ)])

    for n, (src, held, dst) in enumerate(((vel_in, vel, vel_out), (grad_in, grad, grad_out))):
        for i in range(held.shape[0]):
            stores = [pltpu.make_async_copy(held.at[i], dst.at[i], out_sem.at[n * held.shape[0] + i])]
            step(src.at[i], held.at[i], stores)

    for load, _ in steps:
        load.start()
    for load, stores in steps:
        load.wait()
        for store in stores:
            store.start()
    for _, stores in steps:
        for store in stores:
            store.wait()


def shards(K, G, particle_count, drag_coeff, particle_velocity, fluid_velocity):
    NZ, R, NY = particle_count.shape
    rows, W = fluid_velocity.shape[2:]
    C = G // K
    H = max(ROUNDS)
    f32 = jnp.float32

    dma = pltpu.SemaphoreType.DMA
    pad = (R + 2 * H, NZ, NY)
    scratch = [
        pltpu.VMEM((3, rows, NZ, W), f32),
        pltpu.VMEM((3, R + 2, NZ, NY), f32),
        pltpu.VMEM(pad, jnp.int32),
        pltpu.VMEM((R, NZ, NY), f32),
        pltpu.VMEM((3, R, NZ, NY), f32),
        *[pltpu.VMEM(pad, f32) for _ in range(6)],
        pltpu.VMEM((3, R, NZ, NY), f32),
        pltpu.VMEM((3, R, NZ, NY), f32),
        pltpu.VMEM((R + 2, NZ, NY), f32),
        pltpu.VMEM((2, NZ, NY), f32),
        pltpu.VMEM((2, NZ, NY), f32),
        pltpu.VMEM((SWEEPS,) + pad, f32),
        pltpu.VMEM((G, R, NZ, W), f32),
        dma((4 * NZ,)), dma((2,)), dma((G,)),
        dma((K * C,)), dma((G,)),
        dma((2, 2)), dma((2, 2)), dma((2, H + 1)), dma((2, H + 1)), dma((2, H)), dma((2, H)), dma((3, G)), dma((3, G)), dma((3, K)), dma((3, K)),
    ]
    anywhere = pl.BlockSpec(memory_space=pl.ANY)
    pressure, velocity, slopes = pl.pallas_call(
        functools.partial(kernel, K, G, R, NZ, NY, W),
        out_shape=(
            jax.ShapeDtypeStruct((C, K, R, NZ, W), f32),
            jax.ShapeDtypeStruct((3, NZ, R, NY), f32),
            jax.ShapeDtypeStruct((3, NZ, R, NY), f32),
        ),
        in_specs=[anywhere] * 4,
        out_specs=(anywhere, anywhere, anywhere),
        scratch_shapes=scratch,
        compiler_params=pltpu.CompilerParams(collective_id=0, has_side_effects=True, vmem_limit_bytes=67043328),
    )(particle_count, drag_coeff, particle_velocity, fluid_velocity)
    first = [pressure, velocity, slopes]
    pressure, velocity, slopes = pl.pallas_call(
        settle,
        out_shape=[
            jax.ShapeDtypeStruct((NZ, C, K, R, W), f32),
            jax.ShapeDtypeStruct(velocity.shape, f32),
            jax.ShapeDtypeStruct(slopes.shape, f32),
        ],
        in_specs=[anywhere] * 3,
        out_specs=[anywhere] * 3,
        scratch_shapes=[*[pltpu.VMEM(v.shape, f32) for v in first], dma((1 + 2 * 3,)), dma((NZ + 2 * 3,))],
        compiler_params=pltpu.CompilerParams(vmem_limit_bytes=67043328),
    )(*first)
    return pressure.reshape(NZ, rows, W), velocity, slopes


def solution(mesh):
    placed = (
        P(None, ("gx", "gy"), None),
        P(None, ("gx", "gy"), None),
        P(None, None, ("gx", "gy"), None),
        P(None, None, "gy", "gx"),
    )
    return jax.shard_map(
        functools.partial(shards, mesh.shape["gy"], mesh.shape["gx"]),
        mesh=mesh,
        in_specs=placed,
        out_specs=(
            P(None, "gy", "gx"),
            P(None, None, ("gx", "gy"), None),
            P(None, None, ("gx", "gy"), None),
        ),
        check_vma=False,
    )
```

```python
import functools

import jax
import jax.numpy as jnp
from jax import lax
from jax.experimental import pallas as pl
from jax.experimental.pallas import tpu as pltpu
from jax.sharding import PartitionSpec as P

SWEEPS = 8
ROUNDS = (4, 3)

particle_volume = 0.05
time_step = 0.5
viscosity = 0.1


def kernel(
    K, G, R, NZ, NY, W,
    count_in, drag_in, pvel_in, fluid_in,
    press_out, vel_out, grad_out,
    fp, ub, cn, dr, pv, vo, total_w, wf, wr, wa, rh, pred, gr, fl, fr, eb, lv, rl,
    loc_sem, row_send, row_recv, s2_send, s2_recv,
    hal_send, hal_recv, b_send, b_recv, p_send, p_recv, out_send, out_recv, up_send, up_recv,
):
    H = max(ROUNDS)
    first, last_level = ROUNDS[0], SWEEPS - 1
    b, pf = lv.at[0], lv.at[last_level]
    C = G // K
    B = C * K
    x = lax.axis_index("gx")
    k = lax.axis_index("gy")
    place = x * K + k
    has_prev = place > 0
    has_next = place < G * K - 1
    prev_id = {"gx": jnp.where(k > 0, x, jnp.maximum(x - 1, 0)), "gy": lax.rem(k + K - 1, K)}
    next_id = {"gx": jnp.where(k < K - 1, x, jnp.minimum(x + 1, G - 1)), "gy": lax.rem(k + 1, K)}

    def remote(src, dst, ssem, rsem, to):
        return pltpu.make_async_remote_copy(
            src_ref=src, dst_ref=dst, send_sem=ssem, recv_sem=rsem, device_id=to, device_id_type=pl.DeviceIdType.MESH
        )

    rows = R * B

    local = [[] for _ in range(4)]
    for z in range(NZ):
        local[0].append(pltpu.make_async_copy(fluid_in.at[:, z], fp.at[:, :, z], loc_sem.at[z]))
        local[1].append(pltpu.make_async_copy(count_in.at[z], cn.at[H:H + R, z], loc_sem.at[NZ + z]))
        local[2].append(pltpu.make_async_copy(drag_in.at[z], dr.at[:, z], loc_sem.at[2 * NZ + z]))
        local[3].append(pltpu.make_async_copy(pvel_in.at[:, z], pv.at[:, :, z], loc_sem.at[3 * NZ + z]))
    home = x // C
    barrier = pltpu.get_barrier_semaphore()
    for d in range(1, G * K):
        to = {"gx": lax.rem(x + d // K, G), "gy": lax.rem(k + d % K, K)}
        pl.semaphore_signal(barrier, inc=1, device_id=to, device_id_type=pl.DeviceIdType.MESH)

    for copies in local:
        for copy in copies:
            copy.start()

    line = jnp.zeros((NZ, NY), jnp.float32)

    @pl.when(jnp.logical_not(has_prev))
    def _():
        for which in range(3):
            ub[which, 0] = line

    @pl.when(jnp.logical_not(has_next))
    def _():
        for which in range(3):
            ub[which, R + 1] = line

    fl[0] = line
    fl[R + 1] = line
    edge = jnp.zeros((H, NZ, NY), jnp.float32)

    @pl.when(jnp.logical_not(has_prev))
    def _():
        fr[0] = line
        lv[0, 0:H] = edge
        lv[1, 1] = line
        lv[first, 0:H] = edge
        lv[last_level, H - 1] = line

    @pl.when(jnp.logical_not(has_next))
    def _():
        fr[1] = line
        lv[0, H + R:2 * H + R] = edge
        lv[1, 2 * H + R - 2] = line
        lv[first, H + R:2 * H + R] = edge
        lv[last_level, H + R] = line

    for copy in local[0]:
        copy.wait()
    pl.semaphore_wait(barrier, G * K - 1)

    def count_rows(begin, stop, at):
        return (
            remote(cn.at[H + begin:H + stop], cn.at[H + R + begin:H + R + stop], hal_send.at[at, 0], hal_recv.at[at, 0], prev_id),
            remote(cn.at[H + R - stop:H + R - begin], cn.at[H - stop:H - begin], hal_send.at[at, 1], hal_recv.at[at, 1], next_id),
        )

    near_counts, far_counts = count_rows(0, 1, 0), count_rows(1, H - 1, 1)

    turned = k == K - 1
    wraps = (jnp.logical_and(k == 0, has_prev), jnp.logical_and(turned, has_next))
    plain = (jnp.logical_and(k > 0, has_prev), jnp.logical_and(jnp.logical_not(turned), has_next))

    def launch(copies, only=None):
        for group in ((wraps, plain) if only is None else (only,)):
            for when, copy in zip(group, copies):
                @pl.when(when)
                def _(copy=copy):
                    copy.start()

    def arrived(copies):
        @pl.when(has_next)
        def _():
            copies[0].wait_recv()

        @pl.when(has_prev)
        def _():
            copies[1].wait_recv()

    def sent(copies):
        @pl.when(has_prev)
        def _():
            copies[0].wait_send()

        @pl.when(has_next)
        def _():
            copies[1].wait_send()

    for copy in local[1]:
        copy.wait()

    launch(near_counts)

    columns = pl.ds(pl.multiple_of(x * W, W), W)
    chip = x // C
    sends = []
    for c in range(C):
        for d in range(K):
            j = k ^ d ^ chip if K & (K - 1) == 0 else lax.rem(k + d + K - chip, K)
            at = (c * K + j) * R
            mine = jnp.logical_and(k * C + c == x, j == k)
            low = (j == 0) if c == 0 else None
            high = (j == K - 1) if c == C - 1 else None
            inner = jnp.bool_(True)
            forms = []
            if low is not None:
                inner = jnp.logical_and(inner, jnp.logical_not(low))
                forms.append((low, 0, 1))
            if high is not None:
                inner = jnp.logical_and(inner, jnp.logical_not(high))
                forms.append((high, 1, 0))
            forms.append((inner, 1, 1))
            for want, before, after in forms:
                n = before + R + after
                src = fp.at[:, pl.ds(at - before, n)]
                dst = ub.at[:, pl.ds(1 - before, n), :, columns]
                far = remote(src, dst, s2_send.at[c * K + d], s2_recv.at[x], {"gx": k * C + c, "gy": j})
                near = pltpu.make_async_copy(src, dst, s2_recv.at[x])
                near_when = jnp.logical_and(want, mine)
                far_when = jnp.logical_and(want, jnp.logical_not(mine))

                @pl.when(near_when)
                def _(near=near):
                    near.start()

                @pl.when(far_when)
                def _(far=far):
                    far.start()

                sends.append((far_when, far))

    for n, (want, row, at, gx, gy) in enumerate((
        (k > 0, 0, R + 1, jnp.maximum(k * C - 1, 0), K - 1),
        (k < K - 1, rows - 1, 0, jnp.minimum((k + 1) * C, G - 1), 0),
    )):
        src = fp.at[:, row:row + 1]
        dst = ub.at[:, at:at + 1, :, columns]
        far = remote(src, dst, row_send.at[n], row_recv.at[x], {"gx": gx, "gy": jnp.int32(gy)})
        near = pltpu.make_async_copy(src, dst, row_recv.at[x])
        mine = jnp.logical_and(gx == x, k == gy)
        far_when = jnp.logical_and(want, jnp.logical_not(mine))

        @pl.when(jnp.logical_and(want, mine))
        def _(near=near):
            near.start()

        @pl.when(far_when)
        def _(far=far):
            far.start()

        sends.append((far_when, far))

    launch(far_counts)
    arrived(near_counts)
    for copies in local[2:]:
        for copy in copies:
            copy.wait()

    lane = lax.broadcasted_iota(jnp.int32, (NZ, NY), 1)
    level = lax.broadcasted_iota(jnp.int32, (NZ, NY), 0)

    def above(v):
        return jnp.where(level < NZ - 1, pltpu.roll(v, NZ - 1, 0), 0.0)

    def below(v):
        return jnp.where(level > 0, pltpu.roll(v, 1, 0), 0.0)

    def right(v):
        return jnp.where(lane < NY - 1, pltpu.roll(v, NY - 1, 1), 0.0)

    def left(v):
        return jnp.where(lane > 0, pltpu.roll(v, 1, 1), 0.0)

    def plane_sum(v):
        return above(v) + below(v) + right(v) + left(v)

    def inside(i):
        at = place * R + i
        return jnp.logical_and(at >= 0, at < G * K * R)

    def voids_row(n, carry):
        v = 1.0 - cn[n].astype(jnp.float32) * particle_volume
        vo[n] = jnp.where(inside(n - H), v, 0.0)
        return carry

    lax.fori_loop(H - 1, R + H + 1, voids_row, 0)

    def weight_row(n, carry):
        v = vo[n]
        ws = 0.5 * (6.0 * v + vo[n - 1] + vo[n + 1] + plane_sum(v))
        total_w[n] = ws
        rh[n] = jnp.where(inside(n - H), 1.0 / ws, 0.0)
        wf[n] = 0.5 * (v + vo[n + 1])
        wr[n] = jnp.where(lane < NY - 1, 0.5 * (v + pltpu.roll(v, NY - 1, 1)), 0.0)
        wa[n] = jnp.where(level < NZ - 1, 0.5 * (v + pltpu.roll(v, NZ - 1, 0)), 0.0)
        return carry

    wf[H - 1] = 0.5 * (vo[H - 1] + vo[H])
    lax.fori_loop(H, R + H, weight_row, 0)

    def weighted(n, p, pa, pb):
        r, a = wr[n], wa[n]
        across = r * pltpu.roll(p, NY - 1, 1) + pltpu.roll(r * p, 1, 1)
        upright = a * pltpu.roll(p, NZ - 1, 0) + pltpu.roll(a * p, 1, 0)
        return (wf[n - 1] * pa + wf[n] * pb) + (across + upright)

    for want, copy in sends:
        @pl.when(want)
        def _(copy=copy):
            copy.wait_send()


    here = {"gx": x, "gy": k}
    slab_low = jnp.logical_and(lax.rem(x, C) == 0, k == 0)
    slab_high = jnp.logical_and(lax.rem(x, C) == C - 1, k == K - 1)
    at_side = jnp.logical_or(slab_low, slab_high)
    extra = jnp.logical_or(jnp.logical_and(slab_low, has_prev), jnp.logical_and(slab_high, has_next))

    def landed(n, sem):
        for sender in range(G):
            spot = pl.ds(sender * W, W)
            remote(fp.at[:, 0:n], ub.at[:, 0:n, :, spot], row_send.at[0], sem.at[sender], here).wait_recv()

    @pl.when(at_side)
    def _():
        landed(R + 1, s2_recv)

    @pl.when(jnp.logical_not(at_side))
    def _():
        landed(R + 2, s2_recv)

    @pl.when(extra)
    def _():
        landed(1, row_recv)

    def pass_on(src_up, dst_up, src_down, dst_down, ssem, rsem, at):
        return (
            remote(src_up, dst_up, ssem.at[0, at], rsem.at[0, at], prev_id),
            remote(src_down, dst_down, ssem.at[1, at], rsem.at[1, at], next_id),
        )

    def flux_rows():
        return pass_on(fl.at[1], fr.at[1], fl.at[R], fr.at[0], b_send, b_recv, 0)

    def level_rows(buf, s, ssem, rsem, at):
        return pass_on(buf.at[H + s], buf.at[H + R + s], buf.at[H + R - 1 - s], buf.at[H - 1 - s], ssem, rsem, at)

    def base_rows(s):
        return level_rows(b, s, b_send, b_recv, s + 1)

    def base_last():
        return level_rows(lv.at[1], H - 2, b_send, b_recv, H)

    def edge_rows():
        return pass_on(eb.at[0], b.at[H + R], eb.at[1], b.at[H - 1], b_send, b_recv, 1)

    def mid_rows(s):
        return level_rows(lv.at[first], s, p_send, p_recv, s)

    def last_rows():
        return level_rows(pf, 0, p_send, p_recv, H - 1)

    def momentum(i, which):
        v, ws, drag, u = vo[H + i], total_w[H + i], dr[i], ub[which, i + 1]
        diffusion = weighted(H + i, u, ub[which, i], ub[which, i + 2]) - ws * u
        force = drag * pv[which, i]
        return (v * u + (time_step * viscosity) * diffusion + time_step * force) / (v + time_step * drag)

    def finish(i):
        b[H + i] = -(fl[i + 2] - fl[i] + b[H + i]) * rh[H + i]

    def momentum_step(s, carry):
        pair = (s, R - 1 - s)
        for which in range(3):
            values = [momentum(i, which) for i in pair]
            for i, value in zip(pair, values):
                pred[which, i] = value
            flux = [vo[H + i] * value for i, value in zip(pair, values)]
            if which == 0:
                for i, f in zip(pair, flux):
                    fl[i + 1] = f

                @pl.when(s == 0)
                def _():
                    launch(flux_rows())

            elif which == 1:
                part_source = [right(f) - left(f) for f in flux]
            else:
                for i, f, part in zip(pair, flux, part_source):
                    b[H + i] = part + (above(f) - below(f))

        @pl.when(s > 0)
        def _():
            finish(s - 1)
            finish(R - s)

            @pl.when(s == 1)
            def _():
                eb[0] = b[H]
                eb[1] = b[H + R - 1]
                launch(edge_rows())

            @pl.when(jnp.logical_and(s > 1, s < H))
            def _():
                launch(base_rows(s - 1))

        return carry

    half = R // 2
    lax.fori_loop(0, half, momentum_step, 0)
    finish(half - 1)
    finish(R - half)

    def sweep_pair(l, lo):
        hi = 2 * H + R - 1 - lo
        values = [
            weighted(n, lv[l - 1, n], lv[l - 1, n - 1], lv[l - 1, n + 1]) * rh[n] + b[n] for n in (lo, hi)
        ]
        lv[l, lo] = values[0]
        lv[l, hi] = values[1]

    def diagonal(j, start, stop):
        def level(l, carry):
            sweep_pair(l, l + (H - j))
            return carry

        lax.fori_loop(start, stop, level, 0, unroll=True)

    def rows_of(l, start, stop):
        def row(lo, carry):
            sweep_pair(l, lo)
            return carry

        lax.fori_loop(H + start, H + stop, row, 0, unroll=True)

    def partner(d, back=False):
        if K & (K - 1) == 0:
            return chip ^ d
        return lax.rem(chip + (K - d if back else d), K)

    pieces = ((half - 1, half + 1), (0, half - 1), (half + 1, R))
    outs, rises = [], []

    def send_piece(i):
        lo, hi = pieces[i]
        for d in range(K):
            for c in range(C):
                target = partner(d) * C + lax.rem(x + c, C)
                src = pf.at[H + lo:H + hi, :, pl.ds(pl.multiple_of(target * W, W), W)]
                dst = rl.at[x, lo:hi]
                if d == c == 0:
                    pltpu.make_async_copy(src, dst, out_recv.at[i, x]).start()
                else:
                    far = remote(src, dst, out_send.at[i, d * C + c], out_recv.at[i, x], {"gx": target, "gy": k})
                    outs.append(far)
                    far.start()

    def rise(i, d):
        lo, hi = pieces[i]
        to = partner(d, back=True)
        for c in range(C):
            slot = to * C + c
            remote(
                pf.at[H + lo:H + hi, :, 0:W], rl.at[slot, lo:hi], out_send.at[i, 0], out_recv.at[i, slot], here
            ).wait_recv()
        src, dst = rl.at[pl.ds(to * C, C), lo:hi], press_out.at[:, k, lo:hi]
        far = remote(src, dst, up_send.at[i, d], up_recv.at[i, k], {"gx": x, "gy": to})
        near = pltpu.make_async_copy(src, dst, up_recv.at[i, k])

        @pl.when(to != k)
        def _():
            far.start()

        @pl.when(to == k)
        def _():
            near.start()

        rises.append((to, far))

    arrived(far_counts)
    lax.fori_loop(1, H - 1, voids_row, 0)
    lax.fori_loop(R + H + 1, R + 2 * H - 1, voids_row, 0)
    wf[1] = 0.5 * (vo[1] + vo[2])
    lax.fori_loop(2, H, weight_row, 0)
    lax.fori_loop(R + H, R + 2 * H - 2, weight_row, 0)

    for j in range(2 - half, H + 1):
        if j == 0:
            arrived(flux_rows())
            b[H] = b[H] + fr[0] * rh[H]
            b[H + R - 1] = b[H + R - 1] - fr[1] * rh[H + R - 1]
        elif j == H:
            arrived(base_last())
        elif j > 0:
            arrived(base_rows(j - 1))
            if j == 1:
                b[H - 1] = b[H - 1] - fl[1] * rh[H - 1]
                b[H + R] = b[H + R] + fl[R] * rh[H + R]
        stop = min(last_level, j + half - 1) + 1
        diagonal(j, 2 if j == H else 1, min(stop, first + 1))
        if j == 3 - H:
            launch(base_last())
        if first - j < ROUNDS[1]:
            launch(mid_rows(first - j))
        if stop > first + 1:
            diagonal(j, first + 1, stop)

    send_piece(0)
    for s in range(ROUNDS[1] - 1, -1, -1):
        arrived(mid_rows(s))
    for l in range(first + 1, last_level + 1):
        rows_of(l, l - last_level, l - H)

    for i in (1, 2):
        send_piece(i)
    launch(last_rows())
    for d in range(K):
        rise(0, d)
    for d in range(K):
        for i in (1, 2):
            rise(i, d)

    arrived(last_rows())

    def slope_row(i, carry):
        n = H + i
        p = pf[n]
        g0 = 0.5 * (pf[n + 1] - pf[n - 1])
        g1 = 0.5 * (right(p) - left(p))
        g2 = 0.5 * (above(p) - below(p))
        for which, g in enumerate((g0, g1, g2)):
            gr[which, i] = g
            pred[which, i] = pred[which, i] - time_step * g
        return carry

    lax.fori_loop(0, R, slope_row, 0)
    written = []
    for z in range(NZ):
        written.append(pltpu.make_async_copy(gr.at[:, :, z], grad_out.at[:, z], loc_sem.at[z]))
        written.append(pltpu.make_async_copy(pred.at[:, :, z], vel_out.at[:, z], loc_sem.at[NZ + z]))
    for copy in written:
        copy.start()

    for copies in [near_counts, far_counts, flux_rows(), edge_rows()] + [base_rows(i) for i in range(1, H - 1)] + [base_last(), last_rows()] + [mid_rows(i) for i in range(ROUNDS[1])]:
        sent(copies)

    for copy in outs:
        copy.wait_send()

    for to, far in rises:
        @pl.when(to != k)
        def _(far=far):
            far.wait_send()

    for i, (lo, hi) in enumerate(pieces):
        for j in range(K):
            remote(
                rl.at[0:C, lo:hi], press_out.at[:, j, lo:hi], up_send.at[i, 0], up_recv.at[i, j], here
            ).wait_recv()
    for copy in written:
        copy.wait()


def settle(press_in, vel_in, grad_in, press_out, vel_out, grad_out, press, vel, grad, in_sem, out_sem):
    C, K, R, NZ, W = press.shape
    steps = []

    def step(src, held, stores):
        at = len(steps)
        steps.append((pltpu.make_async_copy(src, held, in_sem.at[at]), stores))

    step(press_in, press, [pltpu.make_async_copy(press.at[:, :, :, z], press_out.at[z], out_sem.at[2 * vel.shape[0] + z]) for z in range(NZ)])

    for n, (src, held, dst) in enumerate(((vel_in, vel, vel_out), (grad_in, grad, grad_out))):
        for i in range(held.shape[0]):
            stores = [pltpu.make_async_copy(held.at[i], dst.at[i], out_sem.at[n * held.shape[0] + i])]
            step(src.at[i], held.at[i], stores)

    for load, _ in steps:
        load.start()
    for load, stores in steps:
        load.wait()
        for store in stores:
            store.start()
    for _, stores in steps:
        for store in stores:
            store.wait()


def shards(K, G, particle_count, drag_coeff, particle_velocity, fluid_velocity):
    NZ, R, NY = particle_count.shape
    rows, W = fluid_velocity.shape[2:]
    C = G // K
    H = max(ROUNDS)
    f32 = jnp.float32

    dma = pltpu.SemaphoreType.DMA
    pad = (R + 2 * H, NZ, NY)
    scratch = [
        pltpu.VMEM((3, rows, NZ, W), f32),
        pltpu.VMEM((3, R + 2, NZ, NY), f32),
        pltpu.VMEM(pad, jnp.int32),
        pltpu.VMEM((R, NZ, NY), f32),
        pltpu.VMEM((3, R, NZ, NY), f32),
        *[pltpu.VMEM(pad, f32) for _ in range(6)],
        pltpu.VMEM((3, R, NZ, NY), f32),
        pltpu.VMEM((3, R, NZ, NY), f32),
        pltpu.VMEM((R + 2, NZ, NY), f32),
        pltpu.VMEM((2, NZ, NY), f32),
        pltpu.VMEM((2, NZ, NY), f32),
        pltpu.VMEM((SWEEPS,) + pad, f32),
        pltpu.VMEM((G, R, NZ, W), f32),
        dma((4 * NZ,)), dma((2,)), dma((G,)),
        dma((K * C,)), dma((G,)),
        dma((2, 2)), dma((2, 2)), dma((2, H + 1)), dma((2, H + 1)), dma((2, H)), dma((2, H)), dma((3, G)), dma((3, G)), dma((3, K)), dma((3, K)),
    ]
    anywhere = pl.BlockSpec(memory_space=pl.ANY)
    pressure, velocity, slopes = pl.pallas_call(
        functools.partial(kernel, K, G, R, NZ, NY, W),
        out_shape=(
            jax.ShapeDtypeStruct((C, K, R, NZ, W), f32),
            jax.ShapeDtypeStruct((3, NZ, R, NY), f32),
            jax.ShapeDtypeStruct((3, NZ, R, NY), f32),
        ),
        in_specs=[anywhere] * 4,
        out_specs=(anywhere, anywhere, anywhere),
        scratch_shapes=scratch,
        compiler_params=pltpu.CompilerParams(collective_id=0, has_side_effects=True, vmem_limit_bytes=67043328),
    )(particle_count, drag_coeff, particle_velocity, fluid_velocity)
    first = [pressure, velocity, slopes]
    pressure, velocity, slopes = pl.pallas_call(
        settle,
        out_shape=[
            jax.ShapeDtypeStruct((NZ, C, K, R, W), f32),
            jax.ShapeDtypeStruct(velocity.shape, f32),
            jax.ShapeDtypeStruct(slopes.shape, f32),
        ],
        in_specs=[anywhere] * 3,
        out_specs=[anywhere] * 3,
        scratch_shapes=[*[pltpu.VMEM(v.shape, f32) for v in first], dma((1 + 2 * 3,)), dma((NZ + 2 * 3,))],
        compiler_params=pltpu.CompilerParams(vmem_limit_bytes=67043328),
    )(*first)
    return pressure.reshape(NZ, rows, W), velocity, slopes


def solution(mesh):
    placed = (
        P(None, ("gx", "gy"), None),
        P(None, ("gx", "gy"), None),
        P(None, None, ("gx", "gy"), None),
        P(None, None, "gy", "gx"),
    )
    return jax.shard_map(
        functools.partial(shards, mesh.shape["gy"], mesh.shape["gx"]),
        mesh=mesh,
        in_specs=placed,
        out_specs=(
            P(None, "gy", "gx"),
            P(None, None, ("gx", "gy"), None),
            P(None, None, ("gx", "gy"), None),
        ),
        check_vma=False,
    )
```
